32 devices in a mesh: seq: 2 (over x), dp: 16 (over z, y, core).
Axes of the slice: x: 2, y: 2, z: 4, core: 2. Of those that a mesh axis runs over, the one named last changes fastest.
Arguments:
- tokens: bfloat16 [16, 2048, 768], P('dp', 'seq'), may hold values from -6 to 6
- lengths: int32 [16], P('dp'), may hold values from 1024 to 2048, as said below
- w_qkv: bfloat16 [768, 2304], P('dp'), may hold values from -0.21875 to 0.21875
- bias_qv: bfloat16 [1536], P('dp'), may hold values from -3 to 3
- w_out: bfloat16 [768, 768], P('dp'), may hold values from -4 to 4
- bias_out: bfloat16 [768], P('dp'), may hold values from -3 to 3
- w_up: bfloat16 [768, 3072], P('dp'), may hold values from -0.21875 to 0.21875
- bias_up: bfloat16 [3072], P('dp'), may hold values from -3 to 3
- w_down: bfloat16 [3072, 768], P('dp'), may hold values from -0.109375 to 0.109375
- bias_down: bfloat16 [768], P('dp'), may hold values from -3 to 3
- gain_attn: bfloat16 [768], P('dp'), may hold values from 0.099609375 to 1.8984375
- shift_attn: bfloat16 [768], P('dp'), may hold values from -3 to 3
- gain_ffn: bfloat16 [768], P('dp'), may hold values from 0.099609375 to 1.8984375
- shift_ffn: bfloat16 [768], P('dp'), may hold values from -3 to 3
- cotangent: bfloat16 [16, 2048, 768], P('dp', 'seq'), may hold values from -6 to 6
Outputs:
- result: bfloat16 [16, 2048, 768], P('dp', 'seq')
- grad_tokens: float32 [16, 2048, 768], P('dp', 'seq')
- grad_w_qkv: float32 [768, 2304], P('dp')
- grad_bias_qv: float32 [1536], P('dp')
- grad_w_out: float32 [768, 768], P('dp')
- grad_bias_out: float32 [768], P('dp')
- grad_w_up: float32 [768, 3072], P('dp')
- grad_bias_up: float32 [3072], P('dp')
- grad_w_down: float32 [3072, 768], P('dp')
- grad_bias_down: float32 [768], P('dp')
- grad_gain_attn: float32 [768], P('dp')
- grad_shift_attn: float32 [768], P('dp')
- grad_gain_ffn: float32 [768], P('dp')
- grad_shift_ffn: float32 [768], P('dp')
The draws below stay inside these ranges and needn't reach their ends.
Inputs may be any that keep to these rules, and one draw needn't show every extreme that they name: `lengths`: in every draw some sequence is exactly 2048 long and some other exactly 1024.
All inputs are finite; a program needn't handle non-finite values.
Results may differ from the reference program's by a relative error of at most 0.015.
Values may be sent and summed in bfloat16 or wider, within the bound.
A program may use at most 256 MiB of HBM per device.

```python
import jax
import jax.numpy as jnp
from jax import lax

HEADS = 12
HD = 64
D = 768
FF = 3072
SLOT = 2048
SEQS = 16


def draw_lengths(key, part):
    key_len, key_top, key_low = jax.random.split(key, 3)
    values = jax.random.randint(key_len, (SEQS,), SLOT // 2, SLOT + 1)
    longest = jax.random.randint(key_top, (), 0, SEQS)
    shortest = (longest + 1 + jax.random.randint(key_low, (), 0, SEQS - 1)) % SEQS
    values = values.at[longest].set(SLOT).at[shortest].set(SLOT // 2)
    return values.astype(jnp.int32)


def steps_of(own_key, extent, pieces, least, top_value):
    level = 1.0
    for position, blocks in pieces:
        steps = jax.random.uniform(jax.random.fold_in(jax.random.fold_in(own_key, 6), position), (blocks,), jnp.float32, least / len(pieces), top_value / len(pieces))
        level = level * jnp.repeat(jnp.exp(steps), extent[position] // blocks).reshape((-1,) + (1,) * (len(extent) - 1 - position))
    return level


def scatter_about(stream_key, extent, width, limit, pieces=(), dtype=jnp.bfloat16):
    entries = width * jax.random.normal(stream_key, extent, jnp.float32)
    if pieces:
        entries = entries * steps_of(stream_key, extent, pieces, -0.22, 0.18)
    return jnp.clip(entries, -limit, limit).astype(dtype)


def setup_inputs(seed: int = 0) -> dict:
    splits = jax.random.split(jax.random.key(seed), 16)
    tokens = scatter_about(splits[0], (SEQS, SLOT, D), 1.0, 6.0, ((0, 16), (1, 2)))
    lengths = draw_lengths(jax.random.fold_in(splits[15], 71), 0)
    w_qkv = scatter_about(splits[2], (D, 3 * D), D ** -0.5, 0.21875, ((0, 16),))
    bias_qv = scatter_about(splits[3], (2 * D,), 0.5, 3.0, ((0, 16),))
    w_out = scatter_about(splits[4], (D, D), 2 ** -0.5, 4.0, ((0, 16),))
    bias_out = scatter_about(splits[5], (D,), 0.5, 3.0, ((0, 16),))
    w_up = scatter_about(splits[6], (D, FF), D ** -0.5, 0.21875, ((0, 16),))
    bias_up = scatter_about(splits[7], (FF,), 0.5, 3.0, ((0, 16),))
    w_down = scatter_about(splits[8], (FF, D), FF ** -0.5, 0.109375, ((0, 16),))
    bias_down = scatter_about(splits[9], (D,), 0.5, 3.0, ((0, 16),))
    gain_attn = jnp.clip(1.0 + 0.18 * jax.random.normal(splits[10], (D,), jnp.float32), 0.099609375, 1.8984375).astype(jnp.bfloat16)
    shift_attn = scatter_about(splits[11], (D,), 0.5, 3.0, ((0, 16),))
    gain_ffn = jnp.clip(1.0 + 0.18 * jax.random.normal(splits[12], (D,), jnp.float32), 0.099609375, 1.8984375).astype(jnp.bfloat16)
    shift_ffn = scatter_about(splits[13], (D,), 0.5, 3.0, ((0, 16),))
    cotangent = scatter_about(splits[14], (SEQS, SLOT, D), 1.0, 6.0, ((0, 16), (1, 2)))
    return {"tokens": tokens, "lengths": lengths, "w_qkv": w_qkv, "bias_qv": bias_qv, "w_out": w_out, "bias_out": bias_out, "w_up": w_up, "bias_up": bias_up, "w_down": w_down, "bias_down": bias_down, "gain_attn": gain_attn, "shift_attn": shift_attn, "gain_ffn": gain_ffn, "shift_ffn": shift_ffn, "cotangent": cotangent}


EPS = 1e-05
HIGH = lax.Precision.HIGHEST

@jax.custom_vjp
def low(v):
    return lax.optimization_barrier(v.astype(jnp.bfloat16)).astype(jnp.float32)

@jax.custom_vjp
def low_back(v):
    return v

def low_keep(v):
    return (low(v), None)

def low_pass(kept, grad):
    return (grad,)

def back_keep(v):
    return (v, None)

def back_low(kept, grad):
    return (low(grad),)
low.defvjp(low_keep, low_pass)
low_back.defvjp(back_keep, back_low)

def layer_norm(values, gain, offset):
    center = lax.optimization_barrier(jnp.mean(values, axis=-1, keepdims=True))
    shifted = values - center
    spread = lax.optimization_barrier(jnp.mean(shifted * shifted, axis=-1, keepdims=True))
    return shifted * lax.rsqrt(spread + EPS) * gain + offset

def gelu_exact(values):
    return 0.5 * values * (1.0 + lax.erf(values * 0.7071067811865476))

def matmul(left, right):
    return jnp.dot(left, right, precision=HIGH)

def attend_block(query_block, keys_all, values_all, key_bias):
    scores = jnp.einsum('qhe,khe->hqk', query_block, keys_all, precision=HIGH) * HD ** (-0.5) + key_bias
    scores = low_back(scores)
    largest = lax.optimization_barrier(jnp.max(scores, axis=-1, keepdims=True))
    exponent = jnp.exp(scores - largest)
    weights_soft = exponent / lax.optimization_barrier(jnp.sum(exponent, axis=-1, keepdims=True))
    return jnp.einsum('hqk,khe->qhe', low(weights_soft), values_all, precision=HIGH)

def layer(inputs, w_qkv, bias_qv, w_out, bias_out, w_up, bias_up, w_down, bias_down, gain_attn, shift_attn, gain_ffn, shift_ffn, key_bias):
    projected = matmul(inputs, w_qkv).reshape(SLOT, 3, D)
    zeros_row = jnp.zeros((D,), jnp.float32)
    projected = projected + jnp.stack([bias_qv[:D], zeros_row, bias_qv[D:]])[None]
    qkv_all = low_back(low(projected)).reshape(SLOT, 3, HEADS, HD)
    queries = qkv_all[:, 0]
    keys_all = qkv_all[:, 1]
    values_all = qkv_all[:, 2]
    block_rows = min(512, SLOT)
    query_blocks = queries.reshape(SLOT // block_rows, block_rows, HEADS, HD)
    attend = jax.checkpoint(lambda query_block: attend_block(query_block, keys_all, values_all, key_bias))
    context = lax.map(attend, query_blocks).reshape(SLOT, D)
    context = low_back(low(context))
    attn_branch = low_back(matmul(context, w_out) + bias_out)
    resid_one = inputs + attn_branch
    hidden_one = layer_norm(resid_one, gain_attn, shift_attn)
    pre_act = low_back(matmul(low(hidden_one), w_up) + bias_up)
    activated = low(gelu_exact(pre_act))
    ffn_branch = low_back(matmul(activated, w_down) + bias_down)
    return layer_norm(hidden_one + ffn_branch, gain_ffn, shift_ffn)

def reference(tokens, lengths, w_qkv, bias_qv, w_out, bias_out, w_up, bias_up, w_down, bias_down, gain_attn, shift_attn, gain_ffn, shift_ffn, cotangent):
    params = tuple((item.astype(jnp.float32) for item in (w_qkv, bias_qv, w_out, bias_out, w_up, bias_up, w_down, bias_down, gain_attn, shift_attn, gain_ffn, shift_ffn)))

    def one_sequence(carry, item):
        inputs, length, upstream = item
        key_bias = jnp.where(jnp.arange(SLOT) < length, 0.0, -1000000000.0).astype(jnp.float32)

        def forward(inputs_f, *weights):
            return layer(inputs_f, *weights, key_bias)
        output, pull = jax.vjp(forward, inputs.astype(jnp.float32), *params)
        grads = pull(upstream.astype(jnp.float32))
        summed = tuple((total + gradient for total, gradient in zip(carry, grads[1:])))
        return (summed, (output.astype(jnp.bfloat16), grads[0]))
    start = tuple((jnp.zeros(item.shape, jnp.float32) for item in params))
    totals, (outputs, grad_inputs) = lax.scan(one_sequence, start, (tokens, lengths, cotangent))
    return (outputs, grad_inputs) + tuple(totals)
```

```python
import functools

import jax
import jax.numpy as jnp
from jax import lax
from jax.experimental import pallas as pl
from jax.experimental.pallas import tpu as pltpu
from jax.sharding import PartitionSpec as P

HEADS = 12
HD = 64
EPS = 1e-05
BF = jnp.bfloat16
F32 = jnp.float32
SCALE = HD**-0.5
EXP2_SCALE = SCALE * 1.4426950408889634
MASK = -8e9


def dot_nn(a, b):
    return lax.dot_general(a, b, (((1,), (0,)), ((), ())), preferred_element_type=F32)


def dot_nt(a, b):
    return lax.dot_general(a, b, (((1,), (1,)), ((), ())), preferred_element_type=F32)


def dot_tn(a, b):
    return lax.dot_general(a, b, (((0,), (0,)), ((), ())), preferred_element_type=F32)


def layer_norm(values, gain, offset):
    center = jnp.mean(values, axis=-1, keepdims=True)
    shifted = values - center
    spread = jnp.mean(shifted * shifted, axis=-1, keepdims=True)
    return shifted * lax.rsqrt(spread + EPS) * gain + offset


def gelu_exact(values):
    return 0.5 * values * (1.0 + lax.erf(values * 0.7071067811865476))


def column_sum(values):
    return jnp.sum(values.astype(F32), axis=0)


def attend_kernel(chunk, k_ref, qt_ref, vt_ref, aug_ref, o_ref, lse_ref, *scratch):
    keys = k_ref.shape[0]
    queries = qt_ref.shape[1]
    qt = qt_ref[...]
    row = lax.broadcasted_iota(jnp.int32, (128, queries), 0)
    tail = jnp.where(row == 0, 1.0, 0.0).astype(BF)
    for h in range(2):
        held = scratch[h]
        mine = jnp.where((row >= HD * h) & (row < HD * h + HD), qt, 0).astype(BF)
        query = jnp.concatenate([mine, tail], axis=0)
        largest = jnp.full((1, queries), -jnp.inf, F32)
        for c in range(keys // chunk):
            part = slice(c * chunk, (c + 1) * chunk)
            key = jnp.concatenate([k_ref[part, :], aug_ref[part, :]], axis=1)
            scores = dot_nn(key, query)
            held[part, :] = scores
            largest = jnp.maximum(largest, jnp.max(scores, axis=0, keepdims=True))
        total = jnp.zeros((1, queries), F32)
        context = jnp.zeros((HD, queries), F32)
        base = largest * EXP2_SCALE
        for c in range(keys // chunk):
            part = slice(c * chunk, (c + 1) * chunk)
            weight = jnp.exp2(held[part, :] * EXP2_SCALE - base)
            total = total + jnp.sum(weight, axis=0, keepdims=True)
            context = context + dot_nn(vt_ref[HD * h : HD * h + HD, part], weight.astype(BF))
        o_ref[HD * h : HD * h + HD, :] = (context / total).astype(BF)
        lse_ref[h : h + 1, :] = largest * SCALE + jnp.log(total)


def attend(k, qt, vt, aug):
    keys, width = k.shape
    queries = qt.shape[1]
    pairs = width // 128
    block = min(1024, queries)
    chunk = min(256, keys)
    return pl.pallas_call(
        functools.partial(attend_kernel, chunk),
        grid=(pairs, queries // block),
        in_specs=[
            pl.BlockSpec((keys, 128), lambda g, i: (0, g)),
            pl.BlockSpec((128, block), lambda g, i: (g, i)),
            pl.BlockSpec((128, keys), lambda g, i: (g, 0)),
            pl.BlockSpec((keys, 128), lambda g, i: (0, 0)),
        ],
        out_specs=[
            pl.BlockSpec((128, block), lambda g, i: (g, i)),
            pl.BlockSpec((None, 2, block), lambda g, i: (g, 0, i)),
        ],
        out_shape=[
            jax.ShapeDtypeStruct((width, queries), BF),
            jax.ShapeDtypeStruct((pairs, 2, queries), F32),
        ],
        scratch_shapes=[pltpu.VMEM((keys, block), F32)] * 2,
        compiler_params=pltpu.CompilerParams(vmem_limit_bytes=56 << 20),
        cost_estimate=pl.CostEstimate(
            flops=16 * queries * keys * width, transcendentals=queries * keys * 2 * pairs, bytes_accessed=2 * width * (queries + 2 * keys)
        ),
        name="attend",
    )(k, qt, vt, aug)


def three_terms(row, values):
    high = values.astype(BF).astype(F32)
    middle = (values - high).astype(BF).astype(F32)
    low = values - high - middle
    return jnp.where(row == 1, high, 0.0) + jnp.where(row == 2, middle, 0.0) + jnp.where(row == 3, low, 0.0)


def attend_back_kernel(
    chunk, k_ref, kt_ref, v_ref, qt_ref, q_ref, gt_ref, g_ref, aug_ref, lse_ref, delta_ref, dqt_ref, dk_ref, dv_ref, dk_sum, dv_sum
):
    step = pl.program_id(1)
    keys = k_ref.shape[0]
    queries = qt_ref.shape[1]

    @pl.when(step == 0)
    def _():
        dk_sum[...] = jnp.zeros_like(dk_sum)
        dv_sum[...] = jnp.zeros_like(dv_sum)

    qt = qt_ref[...]
    gt = gt_ref[...]
    q = q_ref[...]
    g = g_ref[...]
    row = lax.broadcasted_iota(jnp.int32, (128, queries), 0)
    lane = lax.broadcasted_iota(jnp.int32, (queries, 128), 1)
    query_cols, grad_cols, query_rows, grad_rows = [], [], [], []
    for h in range(2):
        down = (row >= HD * h) & (row < HD * h + HD)
        across = (lane >= HD * h) & (lane < HD * h + HD)
        tail = three_terms(row, lse_ref[h : h + 1, :] * (1.0 / SCALE)) + jnp.where(row == 0, 1.0, 0.0)
        query_cols.append(jnp.concatenate([jnp.where(down, qt, 0).astype(BF), tail.astype(BF)], axis=0))
        tail = three_terms(row, delta_ref[h : h + 1, :])
        grad_cols.append(jnp.concatenate([jnp.where(down, gt, 0).astype(BF), tail.astype(BF)], axis=0))
        query_rows.append(jnp.where(across, q, 0).astype(BF))
        grad_rows.append(jnp.where(across, g, 0).astype(BF))
    query_rows = jnp.concatenate(query_rows, axis=0)
    grad_rows = jnp.concatenate(grad_rows, axis=0)
    dq = [jnp.zeros((HD, queries), F32)] * 2
    for c in range(keys // chunk):
        part = slice(c * chunk, (c + 1) * chunk)
        aug = aug_ref[part, :]
        key = jnp.concatenate([k_ref[part, :], aug], axis=1)
        value = jnp.concatenate([v_ref[part, :], aug], axis=1)
        weights, grads = [], []
        for h in range(2):
            weight = jnp.exp2(dot_nn(key, query_cols[h]) * EXP2_SCALE)
            grad = (weight * dot_nn(value, grad_cols[h])).astype(BF)
            weights.append(weight.astype(BF))
            grads.append(grad)
            dq[h] = dq[h] + dot_nn(kt_ref[HD * h : HD * h + HD, part], grad)
        dv_sum[part, :] += dot_nn(jnp.concatenate(weights, axis=1), grad_rows)
        dk_sum[part, :] += dot_nn(jnp.concatenate(grads, axis=1), query_rows)
    for h in range(2):
        dqt_ref[HD * h : HD * h + HD, :] = (dq[h] * SCALE).astype(BF)

    @pl.when(step == pl.num_programs(1) - 1)
    def _():
        dk_ref[...] = (dk_sum[...] * SCALE).astype(BF)
        dv_ref[...] = dv_sum[...].astype(BF)


def attend_back(k, kt, v, qt, q, gt, g, aug, lse, delta):
    keys, width = k.shape
    queries = qt.shape[1]
    pairs = width // 128
    block = min(1024, queries)
    chunk = min(256, keys)
    key_rows = pl.BlockSpec((keys, 128), lambda g, i: (0, g))
    query_cols = pl.BlockSpec((128, block), lambda g, i: (g, i))
    query_rows = pl.BlockSpec((block, 128), lambda g, i: (i, g))
    stats = pl.BlockSpec((None, 2, block), lambda g, i: (g, 0, i))
    return pl.pallas_call(
        functools.partial(attend_back_kernel, chunk),
        grid=(pairs, queries // block),
        in_specs=[
            key_rows,
            pl.BlockSpec((128, keys), lambda g, i: (g, 0)),
            key_rows,
            query_cols,
            query_rows,
            query_cols,
            query_rows,
            pl.BlockSpec((keys, 128), lambda g, i: (0, 0)),
            stats,
            stats,
        ],
        out_specs=[query_cols, key_rows, key_rows],
        out_shape=[
            jax.ShapeDtypeStruct((width, queries), BF),
            jax.ShapeDtypeStruct((keys, width), BF),
            jax.ShapeDtypeStruct((keys, width), BF),
        ],
        scratch_shapes=[pltpu.VMEM((keys, 128), F32)] * 2,
        compiler_params=pltpu.CompilerParams(vmem_limit_bytes=56 << 20),
        cost_estimate=pl.CostEstimate(
            flops=40 * queries * keys * width, transcendentals=queries * keys * 2 * pairs, bytes_accessed=2 * width * (5 * queries + 5 * keys)
        ),
        name="attend_back",
    )(k, kt, v, qt, q, gt, g, aug, lse, delta)


def local(
    tokens,
    lengths,
    w_qkv,
    bias_qv,
    w_out,
    bias_out,
    w_up,
    bias_up,
    w_down,
    bias_down,
    gain_attn,
    shift_attn,
    gain_ffn,
    shift_ffn,
    cotangent,
):
    x = tokens[0]
    rows, width = x.shape
    ff = w_up.shape[1]
    me = lax.axis_index("seq")
    other = lax.ppermute(x, "seq", [(0, 1), (1, 0)])

    def gather(value):
        return lax.all_gather(value, "dp", axis=0, tiled=True)

    vectors = (bias_qv, bias_out, bias_up, bias_down, gain_attn, shift_attn, gain_ffn, shift_ffn)
    sizes = [v.shape[0] for v in vectors]
    share = w_qkv.shape[0]
    extra = sum(sizes) // share
    beside = jnp.concatenate(vectors).reshape(share, extra)
    full_qkv = gather(jnp.concatenate([w_qkv, jnp.pad(beside, ((0, 0), (0, 128 - extra)))], axis=1))
    full_vectors = full_qkv[:, 3 * width : 3 * width + extra].reshape(-1, sum(sizes)).astype(F32)
    full_qkv = full_qkv[:, : 3 * width]
    full, start = [], 0
    for size in sizes:
        full.append(full_vectors[:, start : start + size].reshape(-1))
        start += size
    full_bqv, full_bout, full_bup, full_bdown, gain_one, shift_one, gain_two, shift_two = full
    full_wout, full_wup, full_wdown = gather(w_out), gather(w_up), gather(w_down)

    both = jnp.concatenate([x, other], axis=0)
    q = (dot_nn(x, full_qkv[:, :width]) + full_bqv[:width]).astype(BF)
    k = dot_nn(both, full_qkv[:, width : 2 * width]).astype(BF)
    v = (dot_nn(both, full_qkv[:, 2 * width :]) + full_bqv[width:]).astype(BF)
    qt, kt, vt = q.T, k.T, v.T
    slot = jnp.arange(2 * rows)
    slot = jnp.where(slot < rows, me * rows + slot, (1 - me) * rows + slot - rows)
    lane = jnp.arange(128)
    masked = jnp.where(slot < lengths[0], 0.0, MASK)
    aug = jnp.where(lane[None] == 0, masked[:, None], jnp.where(lane[None] < 4, -1.0, 0.0)).astype(BF)
    context_t, lse = attend(k, qt, vt, aug)
    context = context_t.T

    attn_branch = dot_nn(context, full_wout) + full_bout
    resid_one = x.astype(F32) + attn_branch
    hidden_one, first_pull = jax.vjp(layer_norm, resid_one, gain_one, shift_one)
    hidden_low = hidden_one.astype(BF)
    pre_act = dot_nn(hidden_low, full_wup) + full_bup
    activated, gelu_pull = jax.vjp(gelu_exact, pre_act)
    act_low = activated.astype(BF)
    ffn_branch = dot_nn(act_low, full_wdown) + full_bdown
    resid_two = hidden_one + ffn_branch
    output, second_pull = jax.vjp(layer_norm, resid_two, gain_two, shift_two)
    grad_two, grad_gain_two, grad_shift_two = second_pull(cotangent[0].astype(F32))
    grad_branch = grad_two.astype(BF)
    grad_wdown = dot_tn(act_low, grad_branch)
    grad_bdown = column_sum(grad_branch)
    (grad_pre,) = gelu_pull(dot_nt(grad_branch, full_wdown))
    grad_pre_low = grad_pre.astype(BF)
    grad_wup = dot_tn(hidden_low, grad_pre_low)
    grad_bup = column_sum(grad_pre_low)
    grad_hidden = grad_two + dot_nt(grad_pre_low, full_wup)
    grad_one, grad_gain_one, grad_shift_one = first_pull(grad_hidden)
    grad_proj = grad_one.astype(BF)
    grad_wout = dot_tn(context, grad_proj)
    grad_bout = column_sum(grad_proj)
    grad_context = dot_nt(grad_proj, full_wout).astype(BF)
    delta = jnp.sum((grad_context.astype(F32) * context.astype(F32)).reshape(rows, HEADS, HD), axis=-1)
    delta = delta.T.reshape(HEADS // 2, 2, rows)

    def scatter(value):
        part = lax.psum_scatter(value.astype(BF), "dp", scatter_dimension=0, tiled=True)
        return part

    share_wdown = scatter(grad_wdown)
    share_wup = scatter(grad_wup)
    share_wout = scatter(grad_wout)

    dqt, dk, dv = attend_back(k, kt, v, qt, q, grad_context.T, grad_context, aug, lse, delta)
    dq = dqt.T
    partial = dot_nt(jnp.concatenate([dk[rows:], dv[rows:]], axis=1), full_qkv[:, width:])
    partial = lax.ppermute(partial.astype(BF), "seq", [(0, 1), (1, 0)])
    own = jnp.concatenate([dq, dk[:rows], dv[:rows]], axis=1)
    grad_wq = dot_tn(x, dq)
    grad_wk = dot_tn(both, dk)
    grad_wv = dot_tn(both, dv)
    grad_inputs = grad_one + dot_nt(own, full_qkv) + partial.astype(F32)
    grad_bqv = jnp.concatenate([column_sum(dq), column_sum(dv)])

    grads = (grad_bqv, grad_bout, grad_bup, grad_bdown, grad_gain_one, grad_shift_one, grad_gain_two, grad_shift_two)
    packed = jnp.concatenate([v.reshape(-1, size) for v, size in zip(grads, sizes)], axis=1).reshape(width, extra)
    packed = jnp.pad(packed, ((0, 0), (0, 128 - extra)))
    share_qkv = scatter(jnp.concatenate([grad_wq, grad_wk, grad_wv, packed], axis=1))

    def over_seq(value):
        value = value.astype(BF)
        return value.astype(F32) + lax.ppermute(value, "seq", [(0, 1), (1, 0)]).astype(F32)

    share_qkv = over_seq(share_qkv)
    packed = share_qkv[:, 3 * width : 3 * width + extra].reshape(-1)
    out_vectors, start = [], 0
    for size in sizes:
        out_vectors.append(packed[start : start + size])
        start += size
    s_bqv, s_bout, s_bup, s_bdown, s_gain_one, s_shift_one, s_gain_two, s_shift_two = out_vectors
    return (
        output.astype(BF)[None],
        grad_inputs[None],
        share_qkv[:, : 3 * width],
        s_bqv,
        over_seq(share_wout),
        s_bout,
        over_seq(share_wup),
        s_bup,
        over_seq(share_wdown),
        s_bdown,
        s_gain_one,
        s_shift_one,
        s_gain_two,
        s_shift_two,
    )


def solution(mesh):
    act, mat, vec = P("dp", "seq", None), P("dp", None), P("dp")
    in_specs = (act, vec, mat, vec, mat, vec, mat, vec, mat, vec, vec, vec, vec, vec, act)
    out_specs = (act, act, mat, vec, mat, vec, mat, vec, mat, vec, vec, vec, vec, vec)
    return jax.shard_map(local, mesh=mesh, in_specs=in_specs, out_specs=out_specs, check_vma=False)
```

```python
import functools

import jax
import jax.numpy as jnp
from jax import lax
from jax.experimental import pallas as pl
from jax.experimental.pallas import tpu as pltpu
from jax.sharding import PartitionSpec as P

HEADS = 12
HD = 64
EPS = 1e-05
BF = jnp.bfloat16
F32 = jnp.float32
SCALE = HD**-0.5
EXP2_SCALE = SCALE * 1.4426950408889634
MASK = -8e9


def dot_nn(a, b):
    return lax.dot_general(a, b, (((1,), (0,)), ((), ())), preferred_element_type=F32)


def dot_nt(a, b):
    return lax.dot_general(a, b, (((1,), (1,)), ((), ())), preferred_element_type=F32)


def dot_tn(a, b):
    return lax.dot_general(a, b, (((0,), (0,)), ((), ())), preferred_element_type=F32)


def layer_norm(values, gain, offset):
    center = jnp.mean(values, axis=-1, keepdims=True)
    shifted = values - center
    spread = jnp.mean(shifted * shifted, axis=-1, keepdims=True)
    return shifted * lax.rsqrt(spread + EPS) * gain + offset


def gelu_exact(values):
    return 0.5 * values * (1.0 + lax.erf(values * 0.7071067811865476))


def column_sum(values):
    return jnp.sum(values.astype(F32), axis=0)


def attend_kernel(chunk, k_ref, qt_ref, vt_ref, aug_ref, o_ref, lse_ref, *scratch):
    keys = k_ref.shape[0]
    queries = qt_ref.shape[1]
    qt = qt_ref[...]
    row = lax.broadcasted_iota(jnp.int32, (128, queries), 0)
    tail = jnp.where(row == 0, 1.0, 0.0).astype(BF)
    for h in range(2):
        held = scratch[h]
        mine = jnp.where((row >= HD * h) & (row < HD * h + HD), qt, 0).astype(BF)
        query = jnp.concatenate([mine, tail], axis=0)
        largest = jnp.full((1, queries), -jnp.inf, F32)
        for c in range(keys // chunk):
            part = slice(c * chunk, (c + 1) * chunk)
            key = jnp.concatenate([k_ref[part, :], aug_ref[part, :]], axis=1)
            scores = dot_nn(key, query)
            held[part, :] = scores
            largest = jnp.maximum(largest, jnp.max(scores, axis=0, keepdims=True))
        total = jnp.zeros((1, queries), F32)
        context = jnp.zeros((HD, queries), F32)
        base = largest * EXP2_SCALE
        for c in range(keys // chunk):
            part = slice(c * chunk, (c + 1) * chunk)
            weight = jnp.exp2(held[part, :] * EXP2_SCALE - base)
            total = total + jnp.sum(weight, axis=0, keepdims=True)
            context = context + dot_nn(vt_ref[HD * h : HD * h + HD, part], weight.astype(BF))
        o_ref[HD * h : HD * h + HD, :] = (context / total).astype(BF)
        lse_ref[h : h + 1, :] = largest * SCALE + jnp.log(total)


def attend(k, qt, vt, aug):
    keys, width = k.shape
    queries = qt.shape[1]
    pairs = width // 128
    block = min(1024, queries)
    chunk = min(256, keys)
    return pl.pallas_call(
        functools.partial(attend_kernel, chunk),
        grid=(pairs, queries // block),
        in_specs=[
            pl.BlockSpec((keys, 128), lambda g, i: (0, g)),
            pl.BlockSpec((128, block), lambda g, i: (g, i)),
            pl.BlockSpec((128, keys), lambda g, i: (g, 0)),
            pl.BlockSpec((keys, 128), lambda g, i: (0, 0)),
        ],
        out_specs=[
            pl.BlockSpec((128, block), lambda g, i: (g, i)),
            pl.BlockSpec((None, 2, block), lambda g, i: (g, 0, i)),
        ],
        out_shape=[
            jax.ShapeDtypeStruct((width, queries), BF),
            jax.ShapeDtypeStruct((pairs, 2, queries), F32),
        ],
        scratch_shapes=[pltpu.VMEM((keys, block), F32)] * 2,
        compiler_params=pltpu.CompilerParams(vmem_limit_bytes=56 << 20),
        cost_estimate=pl.CostEstimate(
            flops=16 * queries * keys * width, transcendentals=queries * keys * 2 * pairs, bytes_accessed=2 * width * (queries + 2 * keys)
        ),
        name="attend",
    )(k, qt, vt, aug)


def three_terms(row, values):
    high = values.astype(BF).astype(F32)
    middle = (values - high).astype(BF).astype(F32)
    low = values - high - middle
    return jnp.where(row == 1, high, 0.0) + jnp.where(row == 2, middle, 0.0) + jnp.where(row == 3, low, 0.0)


def attend_back_kernel(
    chunk, k_ref, kt_ref, v_ref, qt_ref, q_ref, gt_ref, g_ref, aug_ref, lse_ref, delta_ref, dqt_ref, dk_ref, dv_ref, dk_sum, dv_sum
):
    step = pl.program_id(1)
    keys = k_ref.shape[0]
    queries = qt_ref.shape[1]

    @pl.when(step == 0)
    def _():
        dk_sum[...] = jnp.zeros_like(dk_sum)
        dv_sum[...] = jnp.zeros_like(dv_sum)

    qt = qt_ref[...]
    gt = gt_ref[...]
    q = q_ref[...]
    g = g_ref[...]
    row = lax.broadcasted_iota(jnp.int32, (128, queries), 0)
    lane = lax.broadcasted_iota(jnp.int32, (queries, 128), 1)
    query_cols, grad_cols, query_rows, grad_rows = [], [], [], []
    for h in range(2):
        down = (row >= HD * h) & (row < HD * h + HD)
        across = (lane >= HD * h) & (lane < HD * h + HD)
        tail = three_terms(row, lse_ref[h : h + 1, :] * (1.0 / SCALE)) + jnp.where(row == 0, 1.0, 0.0)
        query_cols.append(jnp.concatenate([jnp.where(down, qt, 0).astype(BF), tail.astype(BF)], axis=0))
        tail = three_terms(row, delta_ref[h : h + 1, :])
        grad_cols.append(jnp.concatenate([jnp.where(down, gt, 0).astype(BF), tail.astype(BF)], axis=0))
        query_rows.append(jnp.where(across, q, 0).astype(BF))
        grad_rows.append(jnp.where(across, g, 0).astype(BF))
    query_rows = jnp.concatenate(query_rows, axis=0)
    grad_rows = jnp.concatenate(grad_rows, axis=0)
    dq = [jnp.zeros((HD, queries), F32)] * 2
    for c in range(keys // chunk):
        part = slice(c * chunk, (c + 1) * chunk)
        aug = aug_ref[part, :]
        key = jnp.concatenate([k_ref[part, :], aug], axis=1)
        value = jnp.concatenate([v_ref[part, :], aug], axis=1)
        weights, grads = [], []
        for h in range(2):
            weight = jnp.exp2(dot_nn(key, query_cols[h]) * EXP2_SCALE)
            grad = (weight * dot_nn(value, grad_cols[h])).astype(BF)
            weights.append(weight.astype(BF))
            grads.append(grad)
            dq[h] = dq[h] + dot_nn(kt_ref[HD * h : HD * h + HD, part], grad)
        dv_sum[part, :] += dot_nn(jnp.concatenate(weights, axis=1), grad_rows)
        dk_sum[part, :] += dot_nn(jnp.concatenate(grads, axis=1), query_rows)
    for h in range(2):
        dqt_ref[HD * h : HD * h + HD, :] = (dq[h] * SCALE).astype(BF)

    @pl.when(step == pl.num_programs(1) - 1)
    def _():
        dk_ref[...] = (dk_sum[...] * SCALE).astype(BF)
        dv_ref[...] = dv_sum[...].astype(BF)


def attend_back(k, kt, v, qt, q, gt, g, aug, lse, delta):
    keys, width = k.shape
    queries = qt.shape[1]
    pairs = width // 128
    block = min(1024, queries)
    chunk = min(256, keys)
    key_rows = pl.BlockSpec((keys, 128), lambda g, i: (0, g))
    query_cols = pl.BlockSpec((128, block), lambda g, i: (g, i))
    query_rows = pl.BlockSpec((block, 128), lambda g, i: (i, g))
    stats = pl.BlockSpec((None, 2, block), lambda g, i: (g, 0, i))
    return pl.pallas_call(
        functools.partial(attend_back_kernel, chunk),
        grid=(pairs, queries // block),
        in_specs=[
            key_rows,
            pl.BlockSpec((128, keys), lambda g, i: (g, 0)),
            key_rows,
            query_cols,
            query_rows,
            query_cols,
            query_rows,
            pl.BlockSpec((keys, 128), lambda g, i: (0, 0)),
            stats,
            stats,
        ],
        out_specs=[query_cols, key_rows, key_rows],
        out_shape=[
            jax.ShapeDtypeStruct((width, queries), BF),
            jax.ShapeDtypeStruct((keys, width), BF),
            jax.ShapeDtypeStruct((keys, width), BF),
        ],
        scratch_shapes=[pltpu.VMEM((keys, 128), F32)] * 2,
        compiler_params=pltpu.CompilerParams(vmem_limit_bytes=56 << 20),
        cost_estimate=pl.CostEstimate(
            flops=40 * queries * keys * width, transcendentals=queries * keys * 2 * pairs, bytes_accessed=2 * width * (5 * queries + 5 * keys)
        ),
        name="attend_back",
    )(k, kt, v, qt, q, gt, g, aug, lse, delta)


MESH = pl.DeviceIdType.MESH


class Links:
    def __init__(self, depth, send_sem, recv_sem):
        index = lax.axis_index("dp")
        self.depth = depth
        self.core = index % 2
        self.near = (index // 2) % 2
        self.far = index // 4
        self.seq = lax.axis_index("seq")
        self.send_sem, self.recv_sem = send_sem, recv_sem

    def peer(self, core=None, near=None, far=None):
        core = self.core if core is None else core
        near = self.near if near is None else near
        far = self.far if far is None else far
        return {"dp": (far * 2 + near) * 2 + core}

    def to_core(self):
        return self.peer(core=1 - self.core)

    def to_near(self):
        return self.peer(near=1 - self.near)

    def to_far(self, k):
        return self.peer(far=(self.far + k) % self.depth)

    def to_seq(self):
        return {"seq": 1 - self.seq}

    def all_peers(self):
        return [self.to_core(), self.to_near(), self.to_seq()] + [self.to_far(k) for k in range(1, self.depth)]

    def barrier(self):
        semaphore = pltpu.get_barrier_semaphore()
        peers = self.all_peers()
        for peer in peers:
            pl.semaphore_signal(semaphore, inc=1, device_id=peer, device_id_type=MESH)
        pl.semaphore_wait(semaphore, len(peers))

    def copy(self, src, dst, index, peer):
        return pltpu.make_async_remote_copy(
            src_ref=src, dst_ref=dst, send_sem=self.send_sem.at[index], recv_sem=self.recv_sem.at[index], device_id=peer, device_id_type=MESH
        )


class Piece:
    def __init__(self, links, base, own, from_core, from_near, from_far, from_seq):
        self.links, self.base = links, base
        self.own, self.from_core, self.from_near, self.from_far, self.from_seq = own, from_core, from_near, from_far, from_seq

    def near_copy(self):
        k = self.links
        return k.copy(self.own.at[:, 1 - k.near], self.from_near, self.base + 1, k.to_near())

    def far_copy(self, distance):
        k = self.links
        target = (k.far + distance) % k.depth
        return k.copy(self.own.at[target, k.near], self.from_far.at[distance - 1], self.base + 2 + distance, k.to_far(distance))

    def seq_copy(self):
        k = self.links
        return k.copy(self.own.at[k.far, k.near], self.from_seq, self.base + 2, k.to_seq())

    def send_near(self):
        k = self.links
        for z in range(k.depth):
            total = self.own[z, 1 - k.near].astype(F32) + self.from_core[z, 1 - k.near].astype(F32)
            self.own[z, 1 - k.near] = total.astype(BF)
        self.near_copy().start()

    def send_far(self):
        k = self.links
        self.near_copy().wait_recv()
        for z in range(k.depth):
            total = self.own[z, k.near].astype(F32) + self.from_core[z, k.near].astype(F32) + self.from_near[z].astype(F32)
            self.own[z, k.near] = total.astype(BF)
        for distance in range(1, k.depth):
            self.far_copy(distance).start()

    def send_seq(self):
        k = self.links
        total = self.own[k.far, k.near].astype(F32)
        for distance in range(1, k.depth):
            self.far_copy(distance).wait_recv()
            total = total + self.from_far[distance - 1].astype(F32)
        self.own[k.far, k.near] = total.astype(BF)
        self.seq_copy().start()

    def result(self):
        k = self.links
        self.seq_copy().wait_recv()
        return self.own[k.far, k.near].astype(F32) + self.from_seq[...].astype(F32)

    def finish(self):
        self.near_copy().wait_send()
        for distance in range(1, self.links.depth):
            self.far_copy(distance).wait_send()
        self.seq_copy().wait_send()


def back_kernel(depth, pairs, early, chunk, *refs):
    (
        k_ref,
        kt_ref,
        v_ref,
        qt_ref,
        q_ref,
        gt_ref,
        g_ref,
        aug_ref,
        lse_ref,
        delta_ref,
        wq_ref,
        wk_ref,
        wv_ref,
        xt_ref,
        one_ref,
        sums_ref,
    ) = refs[:16]
    n_src = 1 + max(source for source, _, _ in early)
    sources = refs[16 : 16 + n_src]
    refs = refs[16 + n_src :]
    share_qkv = refs[0]
    shares = refs[1 : 1 + n_src]
    sums_out, tokens_out = refs[1 + n_src : 3 + n_src]
    refs = refs[3 + n_src :]
    stage = [refs[5 * e : 5 * e + 5] for e in range(len(early))]
    refs = refs[5 * len(early) :]
    p_full, p_core, p_near, p_far, p_seq, acc, dq_sum, tok_send, tok_recv, dqkv = refs[:10]
    s_own, s_core, s_near, s_far, s_seq, send_sem, recv_sem, local_sem = refs[10:]

    step = pl.program_id(0)
    last = 2 * pairs - 1
    g = step % pairs
    rows = k_ref.shape[0]
    queries = qt_ref.shape[1]
    links = Links(depth, send_sem, recv_sem)
    span = depth + 2
    pieces = [Piece(links, e * span, *stage[e]) for e in range(len(early))]
    pair_base = len(early) * span
    sums_base = pair_base + pairs * span

    def pair_piece(index):
        own = p_full.at[index, :, :, links.core]
        return Piece(links, pair_base + index * span, own, p_core.at[index], p_near.at[index], p_far.at[index], p_seq.at[index])

    def pair_core_copy(index):
        return links.copy(p_full.at[index, :, :, 1 - links.core], p_core.at[index], pair_base + index * span, links.to_core())

    def early_core_copy(e):
        source, start, width = early[e]
        part = sources[source].at[:, :, 1 - links.core, :, pl.ds(start, width)]
        return links.copy(part, stage[e][1], e * span, links.to_core())

    def early_load(e):
        source, start, width = early[e]
        part = sources[source].at[:, :, links.core, :, pl.ds(start, width)]
        return pltpu.make_async_copy(part, stage[e][0], local_sem.at[e])

    one_copy = pltpu.make_async_copy(one_ref, acc, local_sem.at[len(early)])
    tokens_copy = links.copy(tok_send, tok_recv, sums_base + span, links.to_seq())

    def early_near(e):
        early_load(e).wait()
        early_core_copy(e).wait_recv()
        pieces[e].send_near()

    def early_done(e):
        source, start, width = early[e]
        shares[source][:, start : start + width] = pieces[e].result()

    def pair_near(index):
        pair_core_copy(index).wait_recv()
        pair_piece(index).send_near()

    def pair_done(index):
        value = pair_piece(index).result()
        for third in range(3):
            at = pl.multiple_of((third * pairs + index) * 128, 128)
            share_qkv[:, pl.ds(at, 128)] = value[:, third * 128 : third * 128 + 128]

    @pl.when(step == 0)
    def _():
        links.barrier()
        for e in range(len(early)):
            early_core_copy(e).start()
            early_load(e).start()
        s_own[0] = sums_ref[...]

    def at(moment, when, action, e):
        @pl.when(moment == when)
        def _():
            action(e)

    qt = qt_ref[...]
    gt = gt_ref[...]
    q = q_ref[...]
    grad = g_ref[...]
    row = lax.broadcasted_iota(jnp.int32, (128, queries), 0)
    lane = lax.broadcasted_iota(jnp.int32, (queries, 128), 1)
    query_cols, grad_cols, query_rows, grad_rows = [], [], [], []
    for h in range(2):
        down = (row >= HD * h) & (row < HD * h + HD)
        across = (lane >= HD * h) & (lane < HD * h + HD)
        tail = three_terms(row, lse_ref[h : h + 1, :] * (1.0 / SCALE)) + jnp.where(row == 0, 1.0, 0.0)
        query_cols.append(jnp.concatenate([jnp.where(down, qt, 0).astype(BF), tail.astype(BF)], axis=0))
        tail = three_terms(row, delta_ref[h : h + 1, :])
        grad_cols.append(jnp.concatenate([jnp.where(down, gt, 0).astype(BF), tail.astype(BF)], axis=0))
        query_rows.append(jnp.where(across, q, 0).astype(BF))
        grad_rows.append(jnp.where(across, grad, 0).astype(BF))
    query_rows = jnp.concatenate(query_rows, axis=0)
    grad_rows = jnp.concatenate(grad_rows, axis=0)
    dq = [jnp.zeros((HD, queries), F32)] * 2
    dv_total = jnp.zeros((1, 128), F32)
    chunks = rows // chunk
    for c in range(chunks):
        part = slice(c * chunk, (c + 1) * chunk)
        aug = aug_ref[part, :]
        key = jnp.concatenate([k_ref[part, :], aug], axis=1)
        value = jnp.concatenate([v_ref[part, :], aug], axis=1)
        weights, grads = [], []
        for h in range(2):
            weight = jnp.exp2(dot_nn(key, query_cols[h]) * EXP2_SCALE)
            dscore = (weight * dot_nn(value, grad_cols[h])).astype(BF)
            weights.append(weight.astype(BF))
            grads.append(dscore)
            dq[h] = dq[h] + dot_nn(kt_ref[HD * h : HD * h + HD, part], dscore)
        dv = dot_nn(jnp.concatenate(weights, axis=1), grad_rows)
        dk = dot_nn(jnp.concatenate(grads, axis=1), query_rows)
        dqkv[part, 128:256] = (dk * SCALE).astype(BF)
        dqkv[part, 256:384] = dv.astype(BF)
        dv_total = dv_total + jnp.sum(dv, axis=0, keepdims=True)
        if c == chunks // 2 - 1:
            for e, when in ((0, 0), (2, 2), (4, 5)):
                at(step, when, early_near, e)
            for e, when in ((0, 2), (2, 5), (3, 7), (4, 8)):
                at(step, when, lambda e: pieces[e].send_far(), e)
            at(step, 4, lambda e: pieces[e].send_seq(), 0)
            at(step, 8, early_done, 1)

            @pl.when(step >= pairs + 1)
            def _():
                pair_near(step - pairs - 1)

            @pl.when(step >= pairs + 2)
            def _():
                pair_piece(step - pairs - 2).send_far()

            @pl.when(step >= pairs + 3)
            def _():
                pair_piece(step - pairs - 3).send_seq()

            @pl.when(step >= pairs + 4)
            def _():
                pair_done(step - pairs - 4)

    dq = jnp.concatenate(dq, axis=0)
    column = pl.ds(pl.multiple_of(g * 128, 128), 128)

    @pl.when(step < pairs)
    def _():
        dq_sum[g] = dq
        both = jnp.concatenate([wk_ref[...], wv_ref[...]], axis=1)
        total = dot_nt(dqkv[:, 128:384], both)

        @pl.when(step == 0)
        def _():
            acc[...] = total

        @pl.when(step > 0)
        def _():
            acc[...] += total

        half = dot_nn(xt_ref[...], dqkv[:, 128:384])
        p_full[g, :, :, :, :, 128:384] = half.astype(BF).reshape(p_full.shape[1:5] + (256,))
        s_own[0, 1:2, column] = dv_total

    @pl.when(step == pairs - 1)
    def _():
        tok_send[...] = acc[...].astype(BF)
        tokens_copy.start()
        one_copy.start()

    @pl.when(step >= pairs)
    def _():
        turned = ((dq_sum[g] + dq) * SCALE).T
        dqkv[:, 0:128] = turned.astype(BF)
        s_own[0, 0:1, column] = jnp.sum(turned, axis=0, keepdims=True)
        s_own[0, 1:2, column] += dv_total

        @pl.when(step == pairs)
        def _():
            one_copy.wait()

        every = jnp.concatenate([wq_ref[...], wk_ref[...], wv_ref[...]], axis=1)
        acc[...] += dot_nt(dqkv[...], every)
        product = dot_nn(xt_ref[...], dqkv[...])
        shape = p_full.shape[1:5]
        before = p_full[g, :, :, :, :, 128:384].astype(F32)
        p_full[g, :, :, :, :, 0:128] = product[:, 0:128].astype(BF).reshape(shape + (128,))
        p_full[g, :, :, :, :, 128:384] = (product[:, 128:384].reshape(shape + (256,)) + before).astype(BF)
        pair_core_copy(g).start()

    for e, when in ((1, 0), (3, 3)):
        at(step, when, early_near, e)
    at(step, 3, lambda e: pieces[e].send_far(), 1)
    for e, when in ((1, 5), (2, 7), (3, 9), (4, 9)):
        at(step, when, lambda e: pieces[e].send_seq(), e)
    for e, when in ((0, 5), (2, 9)):
        at(step, when, early_done, e)

    @pl.when(step == last)
    def _():
        final = pairs - 1
        hops = [(s_core, 0, links.to_core()), (s_near, 1, links.to_near())]
        hops += [(s_far.at[k - 1], 2 + k, links.to_far(k)) for k in range(1, depth)]
        hops += [(s_seq, 2, links.to_seq())]
        level = [0, 1] + [2] * (depth - 1) + [3]
        sums = [links.copy(s_own.at[n], dst, sums_base + index, peer) for n, (dst, index, peer) in zip(level, hops)]
        sums[0].start()
        pair_piece(final - 1).send_far()
        pair_piece(final - 2).send_seq()
        pair_done(final - 3)
        pair_near(final)
        sums[0].wait_recv()
        s_own[1] = s_own[0] + s_core[...]
        sums[1].start()
        tokens_copy.wait_recv()
        out_copies = []
        for n in range(4):
            part = pl.ds(n * (rows // 4), rows // 4)
            acc[part, :] += tok_recv[part, :].astype(F32)
            out_copies.append(pltpu.make_async_copy(acc.at[part], tokens_out.at[part], local_sem.at[len(early) + 1 + n]))
            out_copies[-1].start()
        pair_piece(final).send_far()
        sums[1].wait_recv()
        s_own[2] = s_own[1] + s_near[...]
        for n in range(2, depth + 1):
            sums[n].start()
        pair_piece(final - 1).send_seq()
        pair_done(final - 2)
        early_done(3)
        early_done(4)
        pair_piece(final).send_seq()
        total = s_own[2]
        for n in range(2, depth + 1):
            sums[n].wait_recv()
            total = total + s_far[n - 2]
        s_own[3] = total
        sums[depth + 1].start()
        pair_done(final - 1)
        pair_done(final)
        sums[depth + 1].wait_recv()
        sums_out[...] = s_own[3] + s_seq[...]
        for n in range(4):
            out_copies[n].wait()
        for item in sums:
            item.wait_send()
        tokens_copy.wait_send()
        for e in range(len(early)):
            early_core_copy(e).wait_send()
            pieces[e].finish()
        for index in range(pairs):
            pair_core_copy(index).wait_send()
            pair_piece(index).finish()


EARLY = ((0, 0, 2), (0, 1, 2), (1, 0, 2), (1, 1, 2), (2, 0, 1))


def back_reduce(k, kt, v, qt, q, gt, g, aug, lse, delta, full_qkv, xt, grad_one, sums, sources, depth):
    keys, width = k.shape
    rows = keys // 2
    pairs = width // 128
    chunk = min(256, rows)
    share = width // (4 * depth)
    views = [s.reshape(depth, 2, 2, s.shape[0] // (4 * depth), s.shape[1]) for s in sources]
    early = [(n, part * (views[n].shape[-1] // of), views[n].shape[-1] // of) for n, part, of in EARLY]
    key_rows = pl.BlockSpec((rows, 128), lambda i: (1 - i // pairs, i % pairs))
    query_cols = pl.BlockSpec((128, rows), lambda i: (i % pairs, 0))
    query_rows = pl.BlockSpec((rows, 128), lambda i: (0, i % pairs))
    stats = pl.BlockSpec((None, 2, rows), lambda i: (i % pairs, 0, 0))
    whole = pl.BlockSpec(memory_space=pltpu.VMEM)
    there = pl.BlockSpec(memory_space=pl.ANY)
    stages = []
    for n, _, wide in early:
        high = views[n].shape[3]
        stages += [
            pltpu.VMEM((depth, 2, high, wide), BF),
            pltpu.VMEM((depth, 2, high, wide), BF),
            pltpu.VMEM((depth, high, wide), BF),
            pltpu.VMEM((depth - 1, high, wide), BF),
            pltpu.VMEM((high, wide), BF),
        ]
    copies = (len(early) + pairs + 1) * (depth + 2) + 1
    return pl.pallas_call(
        functools.partial(back_kernel, depth, pairs, early, chunk),
        grid=(2 * pairs,),
        in_specs=[
            key_rows,
            pl.BlockSpec((128, rows), lambda i: (i % pairs, 1 - i // pairs)),
            key_rows,
            query_cols,
            query_rows,
            query_cols,
            query_rows,
            pl.BlockSpec((rows, 128), lambda i: (1 - i // pairs, 0)),
            stats,
            stats,
            pl.BlockSpec((width, 128), lambda i: (0, i % pairs)),
            pl.BlockSpec((width, 128), lambda i: (0, pairs + i % pairs)),
            pl.BlockSpec((width, 128), lambda i: (0, 2 * pairs + i % pairs)),
            pl.BlockSpec((width, rows), lambda i: (0, 1 - i // pairs)),
            there,
            whole,
        ]
        + [there] * len(views),
        out_specs=[whole] * (2 + len(views)) + [there],
        out_shape=[jax.ShapeDtypeStruct((share, 3 * width), F32)]
        + [jax.ShapeDtypeStruct(s.shape[3:], F32) for s in views]
        + [jax.ShapeDtypeStruct(sums.shape, F32), jax.ShapeDtypeStruct((rows, width), F32)],
        scratch_shapes=stages
        + [
            pltpu.VMEM((pairs, depth, 2, 2, share, 384), BF),
            pltpu.VMEM((pairs, depth, 2, share, 384), BF),
            pltpu.VMEM((pairs, depth, share, 384), BF),
            pltpu.VMEM((pairs, depth - 1, share, 384), BF),
            pltpu.VMEM((pairs, share, 384), BF),
            pltpu.VMEM((rows, width), F32),
            pltpu.VMEM((pairs, 128, rows), F32),
            pltpu.VMEM((rows, width), BF),
            pltpu.VMEM((rows, width), BF),
            pltpu.VMEM((rows, 384), BF),
            pltpu.VMEM((4,) + sums.shape, F32),
            pltpu.VMEM(sums.shape, F32),
            pltpu.VMEM(sums.shape, F32),
            pltpu.VMEM((depth - 1,) + sums.shape, F32),
            pltpu.VMEM(sums.shape, F32),
            pltpu.SemaphoreType.DMA((copies,)),
            pltpu.SemaphoreType.DMA((copies,)),
            pltpu.SemaphoreType.DMA((len(early) + 5,)),
        ],
        compiler_params=pltpu.CompilerParams(vmem_limit_bytes=58 << 20, collective_id=1, has_side_effects=True),
        cost_estimate=pl.CostEstimate(
            flops=40 * rows * keys * width, transcendentals=rows * keys * 2 * pairs, bytes_accessed=2 * width * 20 * rows
        ),
        name="back_reduce",
    )(k, kt, v, qt, q, gt, g, aug, lse, delta, full_qkv, full_qkv, full_qkv, xt, grad_one, sums, *views)


def back_plain(k, kt, v, qt, q, grad_context, aug, lse, delta, full_qkv, both, grad_one, grads, sources, sizes):
    width = k.shape[1]
    rows = q.shape[0]

    def scatter(value):
        return lax.psum_scatter(value.astype(BF), "dp", scatter_dimension=0, tiled=True)

    def over_seq(value):
        value = value.astype(BF)
        return value.astype(F32) + lax.ppermute(value, "seq", [(0, 1), (1, 0)]).astype(F32)

    share_wout, share_wup, share_wdown = [scatter(s) for s in sources]
    dqt, dk, dv = attend_back(k, kt, v, qt, q, grad_context.T, grad_context, aug, lse, delta)
    dq = dqt.T
    partial = dot_nt(jnp.concatenate([dk[rows:], dv[rows:]], axis=1), full_qkv[:, width:])
    partial = lax.ppermute(partial.astype(BF), "seq", [(0, 1), (1, 0)])
    own = jnp.concatenate([dq, dk[:rows], dv[:rows]], axis=1)
    grad_wq, grad_wk, grad_wv = dot_tn(both[:rows], dq), dot_tn(both, dk), dot_tn(both, dv)
    grad_inputs = grad_one + dot_nt(own, full_qkv) + partial.astype(F32)
    grads = (jnp.concatenate([column_sum(dq), column_sum(dv)]),) + tuple(grads)
    extra = sum(g.shape[0] for g in grads) // width
    packed = jnp.concatenate([g.reshape(-1, size) for g, size in zip(grads, sizes)], axis=1).reshape(width, extra)
    packed = jnp.pad(packed, ((0, 0), (0, 128 - extra)))
    share_qkv = over_seq(scatter(jnp.concatenate([grad_wq, grad_wk, grad_wv, packed], axis=1)))
    packed = share_qkv[:, 3 * width : 3 * width + extra].reshape(-1)
    out_vectors, start = [], 0
    for size in sizes:
        out_vectors.append(packed[start : start + size])
        start += size
    return share_qkv[:, : 3 * width], over_seq(share_wout), over_seq(share_wup), over_seq(share_wdown), out_vectors, grad_inputs


def local(
    tokens,
    lengths,
    w_qkv,
    bias_qv,
    w_out,
    bias_out,
    w_up,
    bias_up,
    w_down,
    bias_down,
    gain_attn,
    shift_attn,
    gain_ffn,
    shift_ffn,
    cotangent,
):
    x = tokens[0]
    rows, width = x.shape
    ff = w_up.shape[1]
    me = lax.axis_index("seq")
    other = lax.ppermute(x, "seq", [(0, 1), (1, 0)])

    def gather(value):
        return lax.all_gather(value, "dp", axis=0, tiled=True)

    vectors = (bias_qv, bias_out, bias_up, bias_down, gain_attn, shift_attn, gain_ffn, shift_ffn)
    sizes = [v.shape[0] for v in vectors]
    share = w_qkv.shape[0]
    extra = sum(sizes) // share
    beside = jnp.concatenate(vectors).reshape(share, extra)
    full_qkv = gather(jnp.concatenate([w_qkv, jnp.pad(beside, ((0, 0), (0, 128 - extra)))], axis=1))
    full_vectors = full_qkv[:, 3 * width : 3 * width + extra].reshape(-1, sum(sizes)).astype(F32)
    full_qkv = full_qkv[:, : 3 * width]
    full, start = [], 0
    for size in sizes:
        full.append(full_vectors[:, start : start + size].reshape(-1))
        start += size
    full_bqv, full_bout, full_bup, full_bdown, gain_one, shift_one, gain_two, shift_two = full
    full_wout, full_wup, full_wdown = gather(w_out), gather(w_up), gather(w_down)

    both = jnp.concatenate([x, other], axis=0)
    q = (dot_nn(x, full_qkv[:, :width]) + full_bqv[:width]).astype(BF)
    k = dot_nn(both, full_qkv[:, width : 2 * width]).astype(BF)
    v = (dot_nn(both, full_qkv[:, 2 * width :]) + full_bqv[width:]).astype(BF)
    qt, kt, vt = q.T, k.T, v.T
    slot = jnp.arange(2 * rows)
    slot = jnp.where(slot < rows, me * rows + slot, (1 - me) * rows + slot - rows)
    lane = jnp.arange(128)
    masked = jnp.where(slot < lengths[0], 0.0, MASK)
    aug = jnp.where(lane[None] == 0, masked[:, None], jnp.where(lane[None] < 4, -1.0, 0.0)).astype(BF)
    context_t, lse = attend(k, qt, vt, aug)
    context = context_t.T

    attn_branch = dot_nn(context, full_wout) + full_bout
    resid_one = x.astype(F32) + attn_branch
    hidden_one, first_pull = jax.vjp(layer_norm, resid_one, gain_one, shift_one)
    hidden_low = hidden_one.astype(BF)
    pre_act = dot_nn(hidden_low, full_wup) + full_bup
    activated, gelu_pull = jax.vjp(gelu_exact, pre_act)
    act_low = activated.astype(BF)
    ffn_branch = dot_nn(act_low, full_wdown) + full_bdown
    resid_two = hidden_one + ffn_branch
    output, second_pull = jax.vjp(layer_norm, resid_two, gain_two, shift_two)
    grad_two, grad_gain_two, grad_shift_two = second_pull(cotangent[0].astype(F32))
    grad_branch = grad_two.astype(BF)
    grad_wdown = dot_tn(act_low, grad_branch)
    grad_bdown = column_sum(grad_branch)
    (grad_pre,) = gelu_pull(dot_nt(grad_branch, full_wdown))
    grad_pre_low = grad_pre.astype(BF)
    grad_wup = dot_tn(hidden_low, grad_pre_low)
    grad_bup = column_sum(grad_pre_low)
    grad_hidden = grad_two + dot_nt(grad_pre_low, full_wup)
    grad_one, grad_gain_one, grad_shift_one = first_pull(grad_hidden)
    grad_proj = grad_one.astype(BF)
    grad_wout = dot_tn(context, grad_proj)
    grad_bout = column_sum(grad_proj)
    grad_context = dot_nt(grad_proj, full_wout).astype(BF)
    delta = jnp.sum((grad_context.astype(F32) * context.astype(F32)).reshape(rows, HEADS, HD), axis=-1)
    delta = delta.T.reshape(HEADS // 2, 2, rows)

    parts = lax.axis_size("dp")
    aligned = parts % 4 == 0 and width % (16 * parts) == 0 and 2 * rows == k.shape[0]
    grads = (grad_bout, grad_bup, grad_bdown, grad_gain_one, grad_shift_one, grad_gain_two, grad_shift_two)
    if aligned:
        sums = jnp.concatenate([g.reshape(-1, width) for g in grads], axis=0)
        sums = jnp.pad(sums, ((2, 16 - 2 - sums.shape[0]), (0, 0)))
        sources = (grad_wdown.astype(BF), grad_wup.astype(BF), grad_wout.astype(BF))
        share_qkv, share_down, share_up, share_out, sums, grad_inputs = back_reduce(
            k, kt, v, qt, q, grad_context.T, grad_context, aug, lse, delta, full_qkv, jnp.concatenate([x.T, other.T], axis=1), grad_one, sums, sources, parts // 4
        )
        out_vectors, start = [], 0
        sums = sums.reshape(-1)
        for size in sizes:
            out_vectors.append(lax.dynamic_slice(sums, (start * parts + lax.axis_index("dp") * size,), (size,)))
            start += size
    else:
        share_qkv, share_out, share_up, share_down, out_vectors, grad_inputs = back_plain(
            k, kt, v, qt, q, grad_context, aug, lse, delta, full_qkv, both, grad_one, grads, (grad_wout, grad_wup, grad_wdown), sizes
        )
    s_bqv, s_bout, s_bup, s_bdown, s_gain_one, s_shift_one, s_gain_two, s_shift_two = out_vectors
    return (
        output.astype(BF)[None],
        grad_inputs[None],
        share_qkv,
        s_bqv,
        share_out,
        s_bout,
        share_up,
        s_bup,
        share_down,
        s_bdown,
        s_gain_one,
        s_shift_one,
        s_gain_two,
        s_shift_two,
    )


def solution(mesh):
    act, mat, vec = P("dp", "seq", None), P("dp", None), P("dp")
    in_specs = (act, vec, mat, vec, mat, vec, mat, vec, mat, vec, vec, vec, vec, vec, act)
    out_specs = (act, act, mat, vec, mat, vec, mat, vec, mat, vec, vec, vec, vec, vec)
    return jax.shard_map(local, mesh=mesh, in_specs=in_specs, out_specs=out_specs, check_vma=False)
```

```python
import functools

import jax
import jax.numpy as jnp
from jax import lax
from jax.experimental import pallas as pl
from jax.experimental.pallas import tpu as pltpu
from jax.sharding import PartitionSpec as P

HEADS = 12
HD = 64
EPS = 1e-05
BF = jnp.bfloat16
F32 = jnp.float32
SCALE = HD**-0.5
EXP2_SCALE = SCALE * 1.4426950408889634
MASK = -8e9


def dot_nn(a, b):
    return lax.dot_general(a, b, (((1,), (0,)), ((), ())), preferred_element_type=F32)


def dot_nt(a, b):
    return lax.dot_general(a, b, (((1,), (1,)), ((), ())), preferred_element_type=F32)


def dot_tn(a, b):
    return lax.dot_general(a, b, (((0,), (0,)), ((), ())), preferred_element_type=F32)


def layer_norm(values, gain, offset):
    center = jnp.mean(values, axis=-1, keepdims=True)
    shifted = values - center
    spread = jnp.mean(shifted * shifted, axis=-1, keepdims=True)
    return shifted * lax.rsqrt(spread + EPS) * gain + offset


def gelu_exact(values):
    return 0.5 * values * (1.0 + lax.erf(values * 0.7071067811865476))


def column_sum(values):
    return jnp.sum(values.astype(F32), axis=0)


def attend_kernel(chunk, k_ref, qt_ref, vt_ref, aug_ref, o_ref, lse_ref, *scratch):
    keys = k_ref.shape[0]
    queries = qt_ref.shape[1]
    qt = qt_ref[...]
    row = lax.broadcasted_iota(jnp.int32, (128, queries), 0)
    tail = jnp.where(row == 0, 1.0, 0.0).astype(BF)
    for h in range(2):
        held = scratch[h]
        mine = jnp.where((row >= HD * h) & (row < HD * h + HD), qt, 0).astype(BF)
        query = jnp.concatenate([mine, tail], axis=0)
        largest = jnp.full((1, queries), -jnp.inf, F32)
        for c in range(keys // chunk):
            part = slice(c * chunk, (c + 1) * chunk)
            key = jnp.concatenate([k_ref[part, :], aug_ref[part, :]], axis=1)
            scores = dot_nn(key, query)
            held[part, :] = scores
            largest = jnp.maximum(largest, jnp.max(scores, axis=0, keepdims=True))
        total = jnp.zeros((1, queries), F32)
        context = jnp.zeros((HD, queries), F32)
        base = largest * EXP2_SCALE
        for c in range(keys // chunk):
            part = slice(c * chunk, (c + 1) * chunk)
            weight = jnp.exp2(held[part, :] * EXP2_SCALE - base)
            total = total + jnp.sum(weight, axis=0, keepdims=True)
            context = context + dot_nn(vt_ref[HD * h : HD * h + HD, part], weight.astype(BF))
        o_ref[HD * h : HD * h + HD, :] = (context / total).astype(BF)
        lse_ref[h : h + 1, :] = largest * SCALE + jnp.log(total)


def attend(k, qt, vt, aug):
    keys, width = k.shape
    queries = qt.shape[1]
    pairs = width // 128
    block = min(1024, queries)
    chunk = min(256, keys)
    return pl.pallas_call(
        functools.partial(attend_kernel, chunk),
        grid=(pairs, queries // block),
        in_specs=[
            pl.BlockSpec((keys, 128), lambda g, i: (0, g)),
            pl.BlockSpec((128, block), lambda g, i: (g, i)),
            pl.BlockSpec((128, keys), lambda g, i: (g, 0)),
            pl.BlockSpec((keys, 128), lambda g, i: (0, 0)),
        ],
        out_specs=[
            pl.BlockSpec((128, block), lambda g, i: (g, i)),
            pl.BlockSpec((None, 2, block), lambda g, i: (g, 0, i)),
        ],
        out_shape=[
            jax.ShapeDtypeStruct((width, queries), BF),
            jax.ShapeDtypeStruct((pairs, 2, queries), F32),
        ],
        scratch_shapes=[pltpu.VMEM((keys, block), F32)] * 2,
        compiler_params=pltpu.CompilerParams(vmem_limit_bytes=56 << 20),
        cost_estimate=pl.CostEstimate(
            flops=16 * queries * keys * width, transcendentals=queries * keys * 2 * pairs, bytes_accessed=2 * width * (queries + 2 * keys)
        ),
        name="attend",
    )(k, qt, vt, aug)


def three_terms(row, values):
    high = values.astype(BF).astype(F32)
    middle = (values - high).astype(BF).astype(F32)
    low = values - high - middle
    return jnp.where(row == 1, high, 0.0) + jnp.where(row == 2, middle, 0.0) + jnp.where(row == 3, low, 0.0)


def attend_back_kernel(
    chunk, k_ref, kt_ref, v_ref, qt_ref, q_ref, gt_ref, g_ref, aug_ref, lse_ref, delta_ref, dqt_ref, dk_ref, dv_ref, dk_sum, dv_sum
):
    step = pl.program_id(1)
    keys = k_ref.shape[0]
    queries = qt_ref.shape[1]

    @pl.when(step == 0)
    def _():
        dk_sum[...] = jnp.zeros_like(dk_sum)
        dv_sum[...] = jnp.zeros_like(dv_sum)

    qt = qt_ref[...]
    gt = gt_ref[...]
    q = q_ref[...]
    g = g_ref[...]
    row = lax.broadcasted_iota(jnp.int32, (128, queries), 0)
    lane = lax.broadcasted_iota(jnp.int32, (queries, 128), 1)
    query_cols, grad_cols, query_rows, grad_rows = [], [], [], []
    for h in range(2):
        down = (row >= HD * h) & (row < HD * h + HD)
        across = (lane >= HD * h) & (lane < HD * h + HD)
        tail = three_terms(row, lse_ref[h : h + 1, :] * (1.0 / SCALE)) + jnp.where(row == 0, 1.0, 0.0)
        query_cols.append(jnp.concatenate([jnp.where(down, qt, 0).astype(BF), tail.astype(BF)], axis=0))
        tail = three_terms(row, delta_ref[h : h + 1, :])
        grad_cols.append(jnp.concatenate([jnp.where(down, gt, 0).astype(BF), tail.astype(BF)], axis=0))
        query_rows.append(jnp.where(across, q, 0).astype(BF))
        grad_rows.append(jnp.where(across, g, 0).astype(BF))
    query_rows = jnp.concatenate(query_rows, axis=0)
    grad_rows = jnp.concatenate(grad_rows, axis=0)
    dq = [jnp.zeros((HD, queries), F32)] * 2
    for c in range(keys // chunk):
        part = slice(c * chunk, (c + 1) * chunk)
        aug = aug_ref[part, :]
        key = jnp.concatenate([k_ref[part, :], aug], axis=1)
        value = jnp.concatenate([v_ref[part, :], aug], axis=1)
        weights, grads = [], []
        for h in range(2):
            weight = jnp.exp2(dot_nn(key, query_cols[h]) * EXP2_SCALE)
            grad = (weight * dot_nn(value, grad_cols[h])).astype(BF)
            weights.append(weight.astype(BF))
            grads.append(grad)
            dq[h] = dq[h] + dot_nn(kt_ref[HD * h : HD * h + HD, part], grad)
        dv_sum[part, :] += dot_nn(jnp.concatenate(weights, axis=1), grad_rows)
        dk_sum[part, :] += dot_nn(jnp.concatenate(grads, axis=1), query_rows)
    for h in range(2):
        dqt_ref[HD * h : HD * h + HD, :] = (dq[h] * SCALE).astype(BF)

    @pl.when(step == pl.num_programs(1) - 1)
    def _():
        dk_ref[...] = (dk_sum[...] * SCALE).astype(BF)
        dv_ref[...] = dv_sum[...].astype(BF)


def attend_back(k, kt, v, qt, q, gt, g, aug, lse, delta):
    keys, width = k.shape
    queries = qt.shape[1]
    pairs = width // 128
    block = min(1024, queries)
    chunk = min(256, keys)
    key_rows = pl.BlockSpec((keys, 128), lambda g, i: (0, g))
    query_cols = pl.BlockSpec((128, block), lambda g, i: (g, i))
    query_rows = pl.BlockSpec((block, 128), lambda g, i: (i, g))
    stats = pl.BlockSpec((None, 2, block), lambda g, i: (g, 0, i))
    return pl.pallas_call(
        functools.partial(attend_back_kernel, chunk),
        grid=(pairs, queries // block),
        in_specs=[
            key_rows,
            pl.BlockSpec((128, keys), lambda g, i: (g, 0)),
            key_rows,
            query_cols,
            query_rows,
            query_cols,
            query_rows,
            pl.BlockSpec((keys, 128), lambda g, i: (0, 0)),
            stats,
            stats,
        ],
        out_specs=[query_cols, key_rows, key_rows],
        out_shape=[
            jax.ShapeDtypeStruct((width, queries), BF),
            jax.ShapeDtypeStruct((keys, width), BF),
            jax.ShapeDtypeStruct((keys, width), BF),
        ],
        scratch_shapes=[pltpu.VMEM((keys, 128), F32)] * 2,
        compiler_params=pltpu.CompilerParams(vmem_limit_bytes=56 << 20),
        cost_estimate=pl.CostEstimate(
            flops=40 * queries * keys * width, transcendentals=queries * keys * 2 * pairs, bytes_accessed=2 * width * (5 * queries + 5 * keys)
        ),
        name="attend_back",
    )(k, kt, v, qt, q, gt, g, aug, lse, delta)


MESH = pl.DeviceIdType.MESH


class Links:
    def __init__(self, depth, send_sem, recv_sem):
        index = lax.axis_index("dp")
        self.depth = depth
        self.core = index % 2
        self.near = (index // 2) % 2
        self.far = index // 4
        self.seq = lax.axis_index("seq")
        self.send_sem, self.recv_sem = send_sem, recv_sem

    def peer(self, core=None, near=None, far=None):
        core = self.core if core is None else core
        near = self.near if near is None else near
        far = self.far if far is None else far
        return {"dp": (far * 2 + near) * 2 + core}

    def to_core(self):
        return self.peer(core=1 - self.core)

    def to_near(self):
        return self.peer(near=1 - self.near)

    def to_far(self, k):
        return self.peer(far=(self.far + k) % self.depth)

    def to_seq(self):
        return {"seq": 1 - self.seq}

    def all_peers(self):
        return [self.to_core(), self.to_near(), self.to_seq()] + [self.to_far(k) for k in range(1, self.depth)]

    def barrier(self):
        semaphore = pltpu.get_barrier_semaphore()
        peers = self.all_peers()
        for peer in peers:
            pl.semaphore_signal(semaphore, inc=1, device_id=peer, device_id_type=MESH)
        pl.semaphore_wait(semaphore, len(peers))

    def copy(self, src, dst, index, peer):
        return self.copy_two(src, dst, index, index, peer)

    def copy_two(self, src, dst, send, recv, peer):
        return pltpu.make_async_remote_copy(
            src_ref=src, dst_ref=dst, send_sem=self.send_sem.at[send], recv_sem=self.recv_sem.at[recv], device_id=peer, device_id_type=MESH
        )


class Piece:
    def __init__(self, links, base, own, from_core, from_near, from_far, from_seq):
        self.links, self.base = links, base
        self.own, self.from_core, self.from_near, self.from_far, self.from_seq = own, from_core, from_near, from_far, from_seq

    def near_copy(self):
        k = self.links
        return k.copy(self.own.at[:, 1 - k.near], self.from_near, self.base + 1, k.to_near())

    def far_copy(self, distance):
        k = self.links
        target = (k.far + distance) % k.depth
        return k.copy(self.own.at[target, k.near], self.from_far.at[distance - 1], self.base + 2 + distance, k.to_far(distance))

    def seq_copy(self):
        k = self.links
        return k.copy(self.own.at[k.far, k.near], self.from_seq, self.base + 2, k.to_seq())

    def send_near(self):
        k = self.links
        for z in range(k.depth):
            total = self.own[z, 1 - k.near].astype(F32) + self.from_core[z, 1 - k.near].astype(F32)
            self.own[z, 1 - k.near] = total.astype(BF)
        self.near_copy().start()

    def send_far(self):
        k = self.links
        self.near_copy().wait_recv()
        for z in range(k.depth):
            total = self.own[z, k.near].astype(F32) + self.from_core[z, k.near].astype(F32) + self.from_near[z].astype(F32)
            self.own[z, k.near] = total.astype(BF)
        for distance in range(1, k.depth):
            self.far_copy(distance).start()

    def send_seq(self):
        k = self.links
        total = self.own[k.far, k.near].astype(F32)
        for distance in range(1, k.depth):
            self.far_copy(distance).wait_recv()
            total = total + self.from_far[distance - 1].astype(F32)
        self.own[k.far, k.near] = total.astype(BF)
        self.seq_copy().start()

    def result(self):
        k = self.links
        self.seq_copy().wait_recv()
        return self.own[k.far, k.near].astype(F32) + self.from_seq[...].astype(F32)

    def finish(self):
        self.near_copy().wait_send()
        for distance in range(1, self.links.depth):
            self.far_copy(distance).wait_send()
        self.seq_copy().wait_send()


def back_kernel(depth, pairs, early, chunk, *refs):
    (
        k_ref,
        kt_ref,
        v_ref,
        qt_ref,
        q_ref,
        gt_ref,
        g_ref,
        aug_ref,
        lse_ref,
        delta_ref,
        wq_ref,
        wk_ref,
        wv_ref,
        xt_ref,
        one_ref,
        sums_ref,
    ) = refs[:16]
    n_src = 1 + max(source for source, _, _ in early)
    sources = refs[16 : 16 + n_src]
    refs = refs[16 + n_src :]
    share_qkv = refs[0]
    shares = refs[1 : 1 + n_src]
    sums_out, tokens_out = refs[1 + n_src : 3 + n_src]
    refs = refs[3 + n_src :]
    stage = [refs[5 * e : 5 * e + 5] for e in range(len(early))]
    refs = refs[5 * len(early) :]
    p_full, p_core, p_near, p_far, p_seq, acc, dq_sum, tok_send, tok_recv, dqkv = refs[:10]
    s_own, s_core, s_near, s_far, s_seq, send_sem, recv_sem, local_sem = refs[10:]

    step = pl.program_id(0)
    last = 2 * pairs - 1
    g = step % pairs
    rows = k_ref.shape[0]
    queries = qt_ref.shape[1]
    links = Links(depth, send_sem, recv_sem)
    span = depth + 2
    pieces = [Piece(links, e * span, *stage[e]) for e in range(len(early))]
    pair_base = len(early) * span
    sums_base = pair_base + pairs * span

    def pair_piece(index):
        own = p_full.at[index, :, :, links.core]
        return Piece(links, pair_base + index * span, own, p_core.at[index], p_near.at[index], p_far.at[index], p_seq.at[index])

    def pair_core_copy(index):
        return links.copy(p_full.at[index, :, :, 1 - links.core], p_core.at[index], pair_base + index * span, links.to_core())

    def early_core_copy(e):
        source, start, width = early[e]
        part = sources[source].at[:, :, 1 - links.core, :, pl.ds(start, width)]
        return links.copy(part, stage[e][1], e * span, links.to_core())

    def early_load(e):
        source, start, width = early[e]
        part = sources[source].at[:, :, links.core, :, pl.ds(start, width)]
        return pltpu.make_async_copy(part, stage[e][0], local_sem.at[e])

    one_copy = pltpu.make_async_copy(one_ref, acc, local_sem.at[len(early)])
    tokens_copy = links.copy(tok_send, tok_recv, sums_base + span, links.to_seq())

    def early_near(e):
        early_load(e).wait()
        early_core_copy(e).wait_recv()
        pieces[e].send_near()

    def early_done(e):
        source, start, width = early[e]
        shares[source][:, start : start + width] = pieces[e].result()

    def pair_near(index):
        pair_core_copy(index).wait_recv()
        pair_piece(index).send_near()

    def pair_done(index):
        value = pair_piece(index).result()
        for third in range(3):
            at = pl.multiple_of((third * pairs + index) * 128, 128)
            share_qkv[:, pl.ds(at, 128)] = value[:, third * 128 : third * 128 + 128]

    @pl.when(step == 0)
    def _():
        links.barrier()
        for e in range(len(early)):
            early_core_copy(e).start()
            early_load(e).start()
        s_own[0] = sums_ref[...]

    def at(moment, when, action, e):
        @pl.when(moment == when)
        def _():
            action(e)

    qt = qt_ref[...]
    gt = gt_ref[...]
    q = q_ref[...]
    grad = g_ref[...]
    row = lax.broadcasted_iota(jnp.int32, (128, queries), 0)
    lane = lax.broadcasted_iota(jnp.int32, (queries, 128), 1)
    query_cols, grad_cols, query_rows, grad_rows = [], [], [], []
    for h in range(2):
        down = (row >= HD * h) & (row < HD * h + HD)
        across = (lane >= HD * h) & (lane < HD * h + HD)
        tail = three_terms(row, lse_ref[h : h + 1, :] * (1.0 / SCALE)) + jnp.where(row == 0, 1.0, 0.0)
        query_cols.append(jnp.concatenate([jnp.where(down, qt, 0).astype(BF), tail.astype(BF)], axis=0))
        tail = three_terms(row, delta_ref[h : h + 1, :])
        grad_cols.append(jnp.concatenate([jnp.where(down, gt, 0).astype(BF), tail.astype(BF)], axis=0))
        query_rows.append(jnp.where(across, q, 0).astype(BF))
        grad_rows.append(jnp.where(across, grad, 0).astype(BF))
    query_rows = jnp.concatenate(query_rows, axis=0)
    grad_rows = jnp.concatenate(grad_rows, axis=0)
    dq = [jnp.zeros((HD, queries), F32)] * 2
    dv_total = jnp.zeros((1, 128), F32)
    chunks = rows // chunk
    for c in range(chunks):
        part = slice(c * chunk, (c + 1) * chunk)
        aug = aug_ref[part, :]
        key = jnp.concatenate([k_ref[part, :], aug], axis=1)
        value = jnp.concatenate([v_ref[part, :], aug], axis=1)
        weights, grads = [], []
        for h in range(2):
            weight = jnp.exp2(dot_nn(key, query_cols[h]) * EXP2_SCALE)
            dscore = (weight * dot_nn(value, grad_cols[h])).astype(BF)
            weights.append(weight.astype(BF))
            grads.append(dscore)
            dq[h] = dq[h] + dot_nn(kt_ref[HD * h : HD * h + HD, part], dscore)
        dv = dot_nn(jnp.concatenate(weights, axis=1), grad_rows)
        dk = dot_nn(jnp.concatenate(grads, axis=1), query_rows)
        dqkv[part, 128:256] = (dk * SCALE).astype(BF)
        dqkv[part, 256:384] = dv.astype(BF)
        dv_total = dv_total + jnp.sum(dv, axis=0, keepdims=True)
        if c == chunks // 2 - 1:
            for e, when in ((0, 0), (2, 2), (4, 5)):
                at(step, when, early_near, e)
            for e, when in ((0, 2), (2, 5), (3, 7), (4, 8)):
                at(step, when, lambda e: pieces[e].send_far(), e)
            at(step, 4, lambda e: pieces[e].send_seq(), 0)
            at(step, 8, early_done, 1)

            @pl.when(step >= pairs + 1)
            def _():
                pair_near(step - pairs - 1)

            @pl.when(step >= pairs + 2)
            def _():
                pair_piece(step - pairs - 2).send_far()

            @pl.when(step >= pairs + 3)
            def _():
                pair_piece(step - pairs - 3).send_seq()

            @pl.when(step >= pairs + 4)
            def _():
                pair_done(step - pairs - 4)

    dq = jnp.concatenate(dq, axis=0)
    column = pl.ds(pl.multiple_of(g * 128, 128), 128)

    @pl.when(step < pairs)
    def _():
        dq_sum[g] = dq
        both = jnp.concatenate([wk_ref[...], wv_ref[...]], axis=1)
        total = dot_nt(dqkv[:, 128:384], both)

        @pl.when(step == 0)
        def _():
            acc[...] = total

        @pl.when(step > 0)
        def _():
            acc[...] += total

        half = dot_nn(xt_ref[...], dqkv[:, 128:384])
        p_full[g, :, :, :, :, 128:384] = half.astype(BF).reshape(p_full.shape[1:5] + (256,))
        s_own[0, 1:2, column] = dv_total

    @pl.when(step == pairs - 1)
    def _():
        tok_send[...] = acc[...].astype(BF)
        tokens_copy.start()
        one_copy.start()

    @pl.when(step >= pairs)
    def _():
        turned = ((dq_sum[g] + dq) * SCALE).T
        dqkv[:, 0:128] = turned.astype(BF)
        s_own[0, 0:1, column] = jnp.sum(turned, axis=0, keepdims=True)
        s_own[0, 1:2, column] += dv_total

        @pl.when(step == pairs)
        def _():
            one_copy.wait()

        every = jnp.concatenate([wq_ref[...], wk_ref[...], wv_ref[...]], axis=1)
        acc[...] += dot_nt(dqkv[...], every)
        product = dot_nn(xt_ref[...], dqkv[...])
        shape = p_full.shape[1:5]
        before = p_full[g, :, :, :, :, 128:384].astype(F32)
        p_full[g, :, :, :, :, 0:128] = product[:, 0:128].astype(BF).reshape(shape + (128,))
        p_full[g, :, :, :, :, 128:384] = (product[:, 128:384].reshape(shape + (256,)) + before).astype(BF)
        pair_core_copy(g).start()

    for e, when in ((1, 0), (3, 3)):
        at(step, when, early_near, e)
    at(step, 3, lambda e: pieces[e].send_far(), 1)
    for e, when in ((1, 5), (2, 7), (3, 9), (4, 9)):
        at(step, when, lambda e: pieces[e].send_seq(), e)
    for e, when in ((0, 5), (2, 9)):
        at(step, when, early_done, e)

    @pl.when(step == last)
    def _():
        final = pairs - 1
        hops = [(s_core, 0, links.to_core()), (s_near, 1, links.to_near())]
        hops += [(s_far.at[k - 1], 2 + k, links.to_far(k)) for k in range(1, depth)]
        hops += [(s_seq, 2, links.to_seq())]
        level = [0, 1] + [2] * (depth - 1) + [3]
        sums = [links.copy(s_own.at[n], dst, sums_base + index, peer) for n, (dst, index, peer) in zip(level, hops)]
        sums[0].start()
        pair_piece(final - 1).send_far()
        pair_piece(final - 2).send_seq()
        pair_done(final - 3)
        pair_near(final)
        sums[0].wait_recv()
        s_own[1] = s_own[0] + s_core[...]
        sums[1].start()
        tokens_copy.wait_recv()
        out_copies = []
        for n in range(4):
            part = pl.ds(n * (rows // 4), rows // 4)
            acc[part, :] += tok_recv[part, :].astype(F32)
            out_copies.append(pltpu.make_async_copy(acc.at[part], tokens_out.at[part], local_sem.at[len(early) + 1 + n]))
            out_copies[-1].start()
        pair_piece(final).send_far()
        sums[1].wait_recv()
        s_own[2] = s_own[1] + s_near[...]
        for n in range(2, depth + 1):
            sums[n].start()
        pair_piece(final - 1).send_seq()
        pair_done(final - 2)
        early_done(3)
        early_done(4)
        pair_piece(final).send_seq()
        total = s_own[2]
        for n in range(2, depth + 1):
            sums[n].wait_recv()
            total = total + s_far[n - 2]
        s_own[3] = total
        sums[depth + 1].start()
        pair_done(final - 1)
        pair_done(final)
        sums[depth + 1].wait_recv()
        sums_out[...] = s_own[3] + s_seq[...]
        for n in range(4):
            out_copies[n].wait()
        for item in sums:
            item.wait_send()
        tokens_copy.wait_send()
        for e in range(len(early)):
            early_core_copy(e).wait_send()
            pieces[e].finish()
        for index in range(pairs):
            pair_core_copy(index).wait_send()
            pair_piece(index).finish()


EARLY = ((0, 0, 2), (0, 1, 2), (1, 0, 2), (1, 1, 2), (2, 0, 1))


def back_reduce(k, kt, v, qt, q, gt, g, aug, lse, delta, full_qkv, xt, grad_one, sums, sources, depth):
    keys, width = k.shape
    rows = keys // 2
    pairs = width // 128
    chunk = min(256, rows)
    share = width // (4 * depth)
    views = [s.reshape(depth, 2, 2, s.shape[0] // (4 * depth), s.shape[1]) for s in sources]
    early = [(n, part * (views[n].shape[-1] // of), views[n].shape[-1] // of) for n, part, of in EARLY]
    key_rows = pl.BlockSpec((rows, 128), lambda i: (1 - i // pairs, i % pairs))
    query_cols = pl.BlockSpec((128, rows), lambda i: (i % pairs, 0))
    query_rows = pl.BlockSpec((rows, 128), lambda i: (0, i % pairs))
    stats = pl.BlockSpec((None, 2, rows), lambda i: (i % pairs, 0, 0))
    whole = pl.BlockSpec(memory_space=pltpu.VMEM)
    there = pl.BlockSpec(memory_space=pl.ANY)
    stages = []
    for n, _, wide in early:
        high = views[n].shape[3]
        stages += [
            pltpu.VMEM((depth, 2, high, wide), BF),
            pltpu.VMEM((depth, 2, high, wide), BF),
            pltpu.VMEM((depth, high, wide), BF),
            pltpu.VMEM((depth - 1, high, wide), BF),
            pltpu.VMEM((high, wide), BF),
        ]
    copies = (len(early) + pairs + 1) * (depth + 2) + 1
    return pl.pallas_call(
        functools.partial(back_kernel, depth, pairs, early, chunk),
        grid=(2 * pairs,),
        in_specs=[
            key_rows,
            pl.BlockSpec((128, rows), lambda i: (i % pairs, 1 - i // pairs)),
            key_rows,
            query_cols,
            query_rows,
            query_cols,
            query_rows,
            pl.BlockSpec((rows, 128), lambda i: (1 - i // pairs, 0)),
            stats,
            stats,
            pl.BlockSpec((width, 128), lambda i: (0, i % pairs)),
            pl.BlockSpec((width, 128), lambda i: (0, pairs + i % pairs)),
            pl.BlockSpec((width, 128), lambda i: (0, 2 * pairs + i % pairs)),
            pl.BlockSpec((width, rows), lambda i: (0, 1 - i // pairs)),
            there,
            whole,
        ]
        + [there] * len(views),
        out_specs=[whole] * (2 + len(views)) + [there],
        out_shape=[jax.ShapeDtypeStruct((share, 3 * width), F32)]
        + [jax.ShapeDtypeStruct(s.shape[3:], F32) for s in views]
        + [jax.ShapeDtypeStruct(sums.shape, F32), jax.ShapeDtypeStruct((rows, width), F32)],
        scratch_shapes=stages
        + [
            pltpu.VMEM((pairs, depth, 2, 2, share, 384), BF),
            pltpu.VMEM((pairs, depth, 2, share, 384), BF),
            pltpu.VMEM((pairs, depth, share, 384), BF),
            pltpu.VMEM((pairs, depth - 1, share, 384), BF),
            pltpu.VMEM((pairs, share, 384), BF),
            pltpu.VMEM((rows, width), F32),
            pltpu.VMEM((pairs, 128, rows), F32),
            pltpu.VMEM((rows, width), BF),
            pltpu.VMEM((rows, width), BF),
            pltpu.VMEM((rows, 384), BF),
            pltpu.VMEM((4,) + sums.shape, F32),
            pltpu.VMEM(sums.shape, F32),
            pltpu.VMEM(sums.shape, F32),
            pltpu.VMEM((depth - 1,) + sums.shape, F32),
            pltpu.VMEM(sums.shape, F32),
            pltpu.SemaphoreType.DMA((copies,)),
            pltpu.SemaphoreType.DMA((copies,)),
            pltpu.SemaphoreType.DMA((len(early) + 5,)),
        ],
        compiler_params=pltpu.CompilerParams(vmem_limit_bytes=58 << 20, collective_id=1, has_side_effects=True),
        cost_estimate=pl.CostEstimate(
            flops=40 * rows * keys * width, transcendentals=rows * keys * 2 * pairs, bytes_accessed=2 * width * 20 * rows
        ),
        name="back_reduce",
    )(k, kt, v, qt, q, gt, g, aug, lse, delta, full_qkv, full_qkv, full_qkv, xt, grad_one, sums, *views)


class Spread:
    def __init__(self, links, base, share, full, local):
        self.links, self.share, self.full = links, share, full
        self.send_base = base * (4 * links.depth - 1)
        self.recv_base = base * 4 * links.depth
        k = links
        self.local = pltpu.make_async_copy(share, full.at[k.far, k.near, k.core], local)

    def index(self, far, near, core):
        return self.recv_base + (far * 2 + near) * 2 + core

    def copy(self, src, slot, send, peer):
        return self.links.copy_two(src, self.full.at[slot], self.send_base + send, self.index(*slot), peer)

    def source(self, k):
        return (self.links.far - k) % self.links.depth

    def far_copy(self, k):
        links = self.links
        return self.copy(self.share, (links.far, links.near, links.core), k - 1, links.to_far(k))

    def near_copy(self, k):
        links = self.links
        slot = (self.source(k), links.near, links.core)
        return self.copy(self.share if k == 0 else self.full.at[slot], slot, links.depth - 1 + k, links.to_near())

    def core_copy(self, k, across):
        links = self.links
        slot = (self.source(k), 1 - links.near if across else links.near, links.core)
        src = self.share if k == 0 and not across else self.full.at[slot]
        return self.copy(src, slot, 2 * links.depth - 1 + 2 * k + across, links.to_core())

    def arrive(self, far, near, core):
        self.copy(self.share, (far, near, core), 0, self.links.to_core()).wait_recv()

    def begin(self):
        self.local.start()
        for k in range(1, self.links.depth):
            self.far_copy(k).start()
        self.near_copy(0).start()
        self.core_copy(0, 0).start()

    def pass_far(self):
        links = self.links
        for k in range(1, links.depth):
            self.arrive(self.source(k), links.near, links.core)
            self.near_copy(k).start()
            self.core_copy(k, 0).start()

    def pass_near(self):
        links = self.links
        for k in range(links.depth):
            self.arrive(self.source(k), 1 - links.near, links.core)
            self.core_copy(k, 1).start()

    def complete(self):
        links = self.links
        for k in range(links.depth):
            for near in range(2):
                self.arrive(self.source(k), near, 1 - links.core)
        self.local.wait()

    def finish(self):
        for k in range(self.links.depth):
            if k:
                self.far_copy(k).wait_send()
            self.near_copy(k).wait_send()
            self.core_copy(k, 0).wait_send()
            self.core_copy(k, 1).wait_send()


ROWS = (0, 2, 3, 7, 8, 9, 10, 11)


def forward_kernel(depth, pairs, later, chunk, *refs):
    x_ref, aug_ref, vec_ref, qkv_share = refs[:4]
    n_src = 1 + max(source for source, _, _ in later)
    shares = refs[4 : 4 + n_src]
    refs = refs[4 + n_src :]
    q_ref, qt_ref, k_ref, kt_ref, v_ref, o_ref, lse_ref, xt_ref, sums_ref, qkv_out = refs[:10]
    fulls = refs[10 : 10 + n_src]
    w_all, v_all, v_own, other, vt, bias, held_0, held_1, send_sem, recv_sem, local_sem = refs[10 + n_src :]
    g = pl.program_id(0)
    rows, width = x_ref.shape
    links = Links(depth, send_sem, recv_sem)
    first = Spread(links, 0, qkv_share, w_all, local_sem.at[0])
    vectors = Spread(links, 1, v_own, v_all, local_sem.at[1])
    pieces = []
    for n, (source, start, wide) in enumerate(later):
        part = pl.ds(start, wide)
        pieces.append(Spread(links, 2 + n, shares[source].at[:, part], fulls[source].at[:, :, :, :, part], local_sem.at[2 + n]))
    spare = (2 + len(later)) * (4 * depth)
    tokens_copy = links.copy_two(x_ref, other, spare, spare, links.to_seq())
    qkv_copy = pltpu.make_async_copy(w_all, qkv_out, local_sem.at[2 + len(later)])

    @pl.when(g == 0)
    def _():
        links.barrier()
        first.begin()
        tokens_copy.start()
        place = lax.axis_index("dp")
        values = vec_ref[...]
        fitted = {}
        for size in VECTOR_UNITS:
            fitted[size] = pltpu.roll(values, (place % (16 // size)) * (width * size // 16), 1)
        target = lax.broadcasted_iota(jnp.int32, (16, width), 0)
        total = jnp.zeros((16, width), F32)
        for n, (base, size) in enumerate(zip(ROWS, VECTOR_SIZES)):
            total = total + jnp.where(target == base + place // (16 // size), fitted[size][n : n + 1, :], 0.0)
        v_own[...] = total.astype(BF)
        vectors.begin()
        xt_ref[:, 0:rows] = x_ref[...].T
        first.pass_far()
        vectors.pass_far()
        pieces[0].begin()
        pieces[1].begin()
        first.pass_near()
        vectors.pass_near()
        first.complete()
        qkv_copy.start()
        vectors.complete()
        total = jnp.zeros((16, width), F32)
        for z in range(depth):
            for y in range(2):
                for c in range(2):
                    total = total + v_all[z, y, c].astype(F32)
        sums_ref[...] = total
        for n in range(pairs):
            bias[n, 0:2, :] = total[0:2, n * 128 : n * 128 + 128]
        tokens_copy.wait_recv()
        xt_ref[:, rows : 2 * rows] = other[...].T

    def at(when, action):
        @pl.when(g == when)
        def _():
            action()

    def weight(third):
        column = pl.ds(pl.multiple_of((third * pairs + g) * 128, 128), 128)
        return w_all[:, :, :, :, column].reshape(width, 128)

    w_kv = jnp.concatenate([weight(1), weight(2)], axis=1)
    w_q = weight(0)
    bias_q = bias[g, 0:1, :]
    bias_v = bias[g, 1:2, :]
    q = dot_nn(x_ref[...], w_q) + bias_q
    q_ref[...] = q.astype(BF)
    qt_ref[...] = q.T.astype(BF)
    for n, tokens in enumerate((x_ref, other)):
        part = slice(n * rows, n * rows + rows)
        kv = dot_nn(tokens[...], w_kv)
        k = kv[:, 0:128]
        v = kv[:, 128:256] + bias_v
        k_ref[part, :] = k.astype(BF)
        kt_ref[:, part] = k.T.astype(BF)
        v_ref[part, :] = v.astype(BF)
        vt[:, part] = v.T.astype(BF)
    at(0, pieces[0].pass_far)
    at(0, pieces[2].begin)
    at(3, pieces[3].pass_far)

    keys = 2 * rows
    qt = qt_ref[...]
    row = lax.broadcasted_iota(jnp.int32, (128, rows), 0)
    tail = jnp.where(row == 0, 1.0, 0.0).astype(BF)
    for h, held in enumerate((held_0, held_1)):
        mine = jnp.where((row >= HD * h) & (row < HD * h + HD), qt, 0).astype(BF)
        query = jnp.concatenate([mine, tail], axis=0)
        largest = jnp.full((1, rows), -jnp.inf, F32)
        for c in range(keys // chunk):
            part = slice(c * chunk, (c + 1) * chunk)
            key = jnp.concatenate([k_ref[part, :], aug_ref[part, :]], axis=1)
            scores = dot_nn(key, query)
            held[part, :] = scores
            largest = jnp.maximum(largest, jnp.max(scores, axis=0, keepdims=True))
        total = jnp.zeros((1, rows), F32)
        context = jnp.zeros((HD, rows), F32)
        base = largest * EXP2_SCALE
        for c in range(keys // chunk):
            part = slice(c * chunk, (c + 1) * chunk)
            weights = jnp.exp2(held[part, :] * EXP2_SCALE - base)
            total = total + jnp.sum(weights, axis=0, keepdims=True)
            context = context + dot_nn(vt[HD * h : HD * h + HD, part], weights.astype(BF))
        o_ref[HD * h : HD * h + HD, :] = (context / total).astype(BF)
        lse_ref[h : h + 1, :] = largest * SCALE + jnp.log(total)
        if h == 0:
            at(0, pieces[1].pass_far)
            at(1, pieces[3].begin)
            at(2, pieces[4].begin)
            at(3, pieces[2].pass_near)
            at(4, pieces[4].pass_far)
    at(0, pieces[0].pass_near)
    at(1, pieces[2].pass_far)
    at(1, pieces[1].pass_near)
    at(4, pieces[3].pass_near)

    @pl.when(g == pairs - 1)
    def _():
        pieces[4].pass_near()
        for piece in pieces:
            piece.complete()
        qkv_copy.wait()
        for piece in [first, vectors] + pieces:
            piece.finish()
        tokens_copy.wait_send()


VECTOR_SIZES = (2, 1, 4, 1, 1, 1, 1, 1)
VECTOR_UNITS = (1, 2, 4)
LATER = ((0, 0, 1), (1, 0, 2), (1, 1, 2), (2, 0, 2), (2, 1, 2))


def forward(x, aug, vectors, w_qkv, w_out, w_up, w_down, depth):
    rows, width = x.shape
    pairs = width // 128
    keys = 2 * rows
    chunk = min(256, keys)
    shares = (w_out, w_up, w_down)
    later = [(n, part * (shares[n].shape[1] // of), shares[n].shape[1] // of) for n, part, of in LATER]
    whole = pl.BlockSpec(memory_space=pltpu.VMEM)
    there = pl.BlockSpec(memory_space=pl.ANY)
    down = lambda high: pl.BlockSpec((high, 128), lambda i: (0, i))
    across = lambda wide: pl.BlockSpec((128, wide), lambda i: (i, 0))
    fulls = [(depth, 2, 2) + s.shape for s in (w_qkv,) + shares]
    low = lambda *shape: jax.ShapeDtypeStruct(shape, BF)
    copies = (2 + len(later)) * 4 * depth + 1
    return pl.pallas_call(
        functools.partial(forward_kernel, depth, pairs, later, chunk),
        grid=(pairs,),
        in_specs=[whole, whole, whole, there, there, there, there],
        out_specs=[
            down(rows),
            across(rows),
            down(keys),
            across(keys),
            down(keys),
            across(rows),
            pl.BlockSpec((None, 2, rows), lambda i: (i, 0, 0)),
            whole,
            whole,
            there,
            there,
            there,
            there,
        ],
        out_shape=[
            low(rows, width),
            low(width, rows),
            low(keys, width),
            low(width, keys),
            low(keys, width),
            low(width, rows),
            jax.ShapeDtypeStruct((pairs, 2, rows), F32),
            low(width, keys),
            jax.ShapeDtypeStruct((16, width), F32),
        ]
        + [low(*f) for f in fulls],
        scratch_shapes=[
            pltpu.VMEM(fulls[0], BF),
            pltpu.VMEM((depth, 2, 2, 16, width), BF),
            pltpu.VMEM((16, width), BF),
            pltpu.VMEM((rows, width), BF),
            pltpu.VMEM((128, keys), BF),
            pltpu.VMEM((pairs, 8, 128), F32),
            pltpu.VMEM((keys, rows), F32),
            pltpu.VMEM((keys, rows), F32),
            pltpu.SemaphoreType.DMA((copies,)),
            pltpu.SemaphoreType.DMA((copies,)),
            pltpu.SemaphoreType.DMA((3 + len(later),)),
        ],
        compiler_params=pltpu.CompilerParams(vmem_limit_bytes=58 << 20, collective_id=2, has_side_effects=True),
        cost_estimate=pl.CostEstimate(
            flops=16 * rows * keys * width, transcendentals=rows * keys * 2 * pairs, bytes_accessed=2 * width * 10 * keys
        ),
        name="forward",
    )(x, aug, vectors, w_qkv, *shares)


def back_plain(k, kt, v, qt, q, grad_context, aug, lse, delta, full_qkv, both, grad_one, grads, sources, sizes):
    width = k.shape[1]
    rows = q.shape[0]

    def scatter(value):
        return lax.psum_scatter(value.astype(BF), "dp", scatter_dimension=0, tiled=True)

    def over_seq(value):
        value = value.astype(BF)
        return value.astype(F32) + lax.ppermute(value, "seq", [(0, 1), (1, 0)]).astype(F32)

    share_wout, share_wup, share_wdown = [scatter(s) for s in sources]
    dqt, dk, dv = attend_back(k, kt, v, qt, q, grad_context.T, grad_context, aug, lse, delta)
    dq = dqt.T
    partial = dot_nt(jnp.concatenate([dk[rows:], dv[rows:]], axis=1), full_qkv[:, width:])
    partial = lax.ppermute(partial.astype(BF), "seq", [(0, 1), (1, 0)])
    own = jnp.concatenate([dq, dk[:rows], dv[:rows]], axis=1)
    grad_wq, grad_wk, grad_wv = dot_tn(both[:rows], dq), dot_tn(both, dk), dot_tn(both, dv)
    grad_inputs = grad_one + dot_nt(own, full_qkv) + partial.astype(F32)
    grads = (jnp.concatenate([column_sum(dq), column_sum(dv)]),) + tuple(grads)
    extra = sum(g.shape[0] for g in grads) // width
    packed = jnp.concatenate([g.reshape(-1, size) for g, size in zip(grads, sizes)], axis=1).reshape(width, extra)
    packed = jnp.pad(packed, ((0, 0), (0, 128 - extra)))
    share_qkv = over_seq(scatter(jnp.concatenate([grad_wq, grad_wk, grad_wv, packed], axis=1)))
    packed = share_qkv[:, 3 * width : 3 * width + extra].reshape(-1)
    out_vectors, start = [], 0
    for size in sizes:
        out_vectors.append(packed[start : start + size])
        start += size
    return share_qkv[:, : 3 * width], over_seq(share_wout), over_seq(share_wup), over_seq(share_wdown), out_vectors, grad_inputs


def forward_plain(x, aug, vectors, w_qkv):
    width = x.shape[1]
    other = lax.ppermute(x, "seq", [(0, 1), (1, 0)])
    sizes = [v.shape[0] for v in vectors]
    share = w_qkv.shape[0]
    extra = sum(sizes) // share
    beside = jnp.concatenate(vectors).reshape(share, extra)
    beside = jnp.concatenate([w_qkv, jnp.pad(beside, ((0, 0), (0, 128 - extra)))], axis=1)
    full_qkv = lax.all_gather(beside, "dp", axis=0, tiled=True)
    full_vectors = full_qkv[:, 3 * width : 3 * width + extra].reshape(-1, sum(sizes)).astype(F32)
    full_qkv = full_qkv[:, : 3 * width]
    full, start = [], 0
    for size in sizes:
        full.append(full_vectors[:, start : start + size].reshape(-1))
        start += size
    both = jnp.concatenate([x, other], axis=0)
    q = (dot_nn(x, full_qkv[:, :width]) + full[0][:width]).astype(BF)
    k = dot_nn(both, full_qkv[:, width : 2 * width]).astype(BF)
    v = (dot_nn(both, full_qkv[:, 2 * width :]) + full[0][width:]).astype(BF)
    qt, kt, vt = q.T, k.T, v.T
    context_t, lse = attend(k, qt, vt, aug)
    return q, qt, k, kt, v, both, context_t, lse, full_qkv, full[1:]


def local(
    tokens,
    lengths,
    w_qkv,
    bias_qv,
    w_out,
    bias_out,
    w_up,
    bias_up,
    w_down,
    bias_down,
    gain_attn,
    shift_attn,
    gain_ffn,
    shift_ffn,
    cotangent,
):
    x = tokens[0]
    rows, width = x.shape
    ff = w_up.shape[1]
    me = lax.axis_index("seq")
    parts = lax.axis_size("dp")
    aligned = parts % 4 == 0 and width % (16 * parts) == 0 and ff % (16 * parts) == 0
    vectors = (bias_qv, bias_out, bias_up, bias_down, gain_attn, shift_attn, gain_ffn, shift_ffn)
    sizes = [v.shape[0] for v in vectors]
    aligned = aligned and tuple(s * parts for s in sizes) == tuple(n * width for n in VECTOR_SIZES) and parts == 16

    slot = jnp.arange(2 * rows)
    slot = jnp.where(slot < rows, me * rows + slot, (1 - me) * rows + slot - rows)
    lane = jnp.arange(128)
    masked = jnp.where(slot < lengths[0], 0.0, MASK)
    aug = jnp.where(lane[None] == 0, masked[:, None], jnp.where(lane[None] < 4, -1.0, 0.0)).astype(BF)

    if aligned:
        padded = jnp.stack([jnp.pad(v.astype(F32), (0, width - v.shape[0])) for v in vectors])
        q, qt, k, kt, v, context_t, lse, xt, summed, full_qkv, full_wout, full_wup, full_wdown = forward(
            x, aug, padded, w_qkv, w_out, w_up, w_down, parts // 4
        )
        full_qkv = full_qkv.reshape(width, 3 * width)
        full_wout = full_wout.reshape(width, width)
        full_wup = full_wup.reshape(width, ff)
        full_wdown = full_wdown.reshape(ff, width)
        full_bqv, full_bout, full_bup, full_bdown, gain_one, shift_one, gain_two, shift_two = [
            summed[n : n + size].reshape(-1) for n, size in zip(ROWS, VECTOR_SIZES)
        ]
    else:
        q, qt, k, kt, v, both, context_t, lse, full_qkv, full = forward_plain(x, aug, vectors, w_qkv)
        full_bout, full_bup, full_bdown, gain_one, shift_one, gain_two, shift_two = full
        full_wout, full_wup, full_wdown = [lax.all_gather(w, "dp", axis=0, tiled=True) for w in (w_out, w_up, w_down)]
    context = context_t.T

    attn_branch = dot_nn(context, full_wout) + full_bout
    resid_one = x.astype(F32) + attn_branch
    hidden_one, first_pull = jax.vjp(layer_norm, resid_one, gain_one, shift_one)
    hidden_low = hidden_one.astype(BF)
    pre_act = dot_nn(hidden_low, full_wup) + full_bup
    activated, gelu_pull = jax.vjp(gelu_exact, pre_act)
    act_low = activated.astype(BF)
    ffn_branch = dot_nn(act_low, full_wdown) + full_bdown
    resid_two = hidden_one + ffn_branch
    output, second_pull = jax.vjp(layer_norm, resid_two, gain_two, shift_two)
    grad_two, grad_gain_two, grad_shift_two = second_pull(cotangent[0].astype(F32))
    grad_branch = grad_two.astype(BF)
    grad_wdown = dot_tn(act_low, grad_branch)
    grad_bdown = column_sum(grad_branch)
    (grad_pre,) = gelu_pull(dot_nt(grad_branch, full_wdown))
    grad_pre_low = grad_pre.astype(BF)
    grad_wup = dot_tn(hidden_low, grad_pre_low)
    grad_bup = column_sum(grad_pre_low)
    grad_hidden = grad_two + dot_nt(grad_pre_low, full_wup)
    grad_one, grad_gain_one, grad_shift_one = first_pull(grad_hidden)
    grad_proj = grad_one.astype(BF)
    grad_wout = dot_tn(context, grad_proj)
    grad_bout = column_sum(grad_proj)
    grad_context = dot_nt(grad_proj, full_wout).astype(BF)
    delta = jnp.sum((grad_context.astype(F32) * context.astype(F32)).reshape(rows, HEADS, HD), axis=-1)
    delta = delta.T.reshape(HEADS // 2, 2, rows)

    grads = (grad_bout, grad_bup, grad_bdown, grad_gain_one, grad_shift_one, grad_gain_two, grad_shift_two)
    if aligned:
        sums = jnp.concatenate([g.reshape(-1, width) for g in grads], axis=0)
        sums = jnp.pad(sums, ((2, 16 - 2 - sums.shape[0]), (0, 0)))
        sources = (grad_wdown.astype(BF), grad_wup.astype(BF), grad_wout.astype(BF))
        share_qkv, share_down, share_up, share_out, sums, grad_inputs = back_reduce(
            k, kt, v, qt, q, grad_context.T, grad_context, aug, lse, delta, full_qkv, xt, grad_one, sums, sources, parts // 4
        )
        out_vectors, start = [], 0
        sums = sums.reshape(-1)
        for size in sizes:
            out_vectors.append(lax.dynamic_slice(sums, (start * parts + lax.axis_index("dp") * size,), (size,)))
            start += size
    else:
        share_qkv, share_out, share_up, share_down, out_vectors, grad_inputs = back_plain(
            k, kt, v, qt, q, grad_context, aug, lse, delta, full_qkv, both, grad_one, grads, (grad_wout, grad_wup, grad_wdown), sizes
        )
    s_bqv, s_bout, s_bup, s_bdown, s_gain_one, s_shift_one, s_gain_two, s_shift_two = out_vectors
    return (
        output.astype(BF)[None],
        grad_inputs[None],
        share_qkv,
        s_bqv,
        share_out,
        s_bout,
        share_up,
        s_bup,
        share_down,
        s_bdown,
        s_gain_one,
        s_shift_one,
        s_gain_two,
        s_shift_two,
    )


def solution(mesh):
    act, mat, vec = P("dp", "seq", None), P("dp", None), P("dp")
    in_specs = (act, vec, mat, vec, mat, vec, mat, vec, mat, vec, vec, vec, vec, vec, act)
    out_specs = (act, act, mat, vec, mat, vec, mat, vec, mat, vec, vec, vec, vec, vec)
    return jax.shard_map(local, mesh=mesh, in_specs=in_specs, out_specs=out_specs, check_vma=False)
```

```python
import functools

import jax
import jax.numpy as jnp
from jax import lax
from jax.experimental import pallas as pl
from jax.experimental.pallas import tpu as pltpu
from jax.sharding import PartitionSpec as P

HEADS = 12
HD = 64
EPS = 1e-05
BF = jnp.bfloat16
F32 = jnp.float32
SCALE = HD**-0.5
EXP2_SCALE = SCALE * 1.4426950408889634
MASK = -8e9


def dot_nn(a, b):
    return lax.dot_general(a, b, (((1,), (0,)), ((), ())), preferred_element_type=F32)


def dot_nt(a, b):
    return lax.dot_general(a, b, (((1,), (1,)), ((), ())), preferred_element_type=F32)


def dot_tn(a, b):
    return lax.dot_general(a, b, (((0,), (0,)), ((), ())), preferred_element_type=F32)


def layer_norm(values, gain, offset):
    center = jnp.mean(values, axis=-1, keepdims=True)
    shifted = values - center
    spread = jnp.mean(shifted * shifted, axis=-1, keepdims=True)
    return shifted * lax.rsqrt(spread + EPS) * gain + offset


def gelu_exact(values):
    return 0.5 * values * (1.0 + lax.erf(values * 0.7071067811865476))


def column_sum(values):
    return jnp.sum(values.astype(F32), axis=0)


def total_rows(values):
    return jnp.sum(values, axis=0, keepdims=True)


def attend_kernel(chunk, k_ref, qt_ref, vt_ref, aug_ref, o_ref, lse_ref, *scratch):
    keys = k_ref.shape[0]
    queries = qt_ref.shape[1]
    qt = qt_ref[...]
    row = lax.broadcasted_iota(jnp.int32, (128, queries), 0)
    tail = jnp.where(row == 0, 1.0, 0.0).astype(BF)
    for h in range(2):
        held = scratch[h]
        mine = jnp.where((row >= HD * h) & (row < HD * h + HD), qt, 0).astype(BF)
        query = jnp.concatenate([mine, tail], axis=0)
        largest = jnp.full((1, queries), -jnp.inf, F32)
        for c in range(keys // chunk):
            part = slice(c * chunk, (c + 1) * chunk)
            key = jnp.concatenate([k_ref[part, :], aug_ref[part, :]], axis=1)
            scores = dot_nn(key, query)
            held[part, :] = scores
            largest = jnp.maximum(largest, jnp.max(scores, axis=0, keepdims=True))
        total = jnp.zeros((1, queries), F32)
        context = jnp.zeros((HD, queries), F32)
        base = largest * EXP2_SCALE
        for c in range(keys // chunk):
            part = slice(c * chunk, (c + 1) * chunk)
            weight = jnp.exp2(held[part, :] * EXP2_SCALE - base)
            total = total + jnp.sum(weight, axis=0, keepdims=True)
            context = context + dot_nn(vt_ref[HD * h : HD * h + HD, part], weight.astype(BF))
        o_ref[HD * h : HD * h + HD, :] = (context / total).astype(BF)
        lse_ref[h : h + 1, :] = largest * SCALE + jnp.log(total)


def attend(k, qt, vt, aug):
    keys, width = k.shape
    queries = qt.shape[1]
    pairs = width // 128
    block = min(1024, queries)
    chunk = min(256, keys)
    return pl.pallas_call(
        functools.partial(attend_kernel, chunk),
        grid=(pairs, queries // block),
        in_specs=[
            pl.BlockSpec((keys, 128), lambda g, i: (0, g)),
            pl.BlockSpec((128, block), lambda g, i: (g, i)),
            pl.BlockSpec((128, keys), lambda g, i: (g, 0)),
            pl.BlockSpec((keys, 128), lambda g, i: (0, 0)),
        ],
        out_specs=[
            pl.BlockSpec((128, block), lambda g, i: (g, i)),
            pl.BlockSpec((None, 2, block), lambda g, i: (g, 0, i)),
        ],
        out_shape=[
            jax.ShapeDtypeStruct((width, queries), BF),
            jax.ShapeDtypeStruct((pairs, 2, queries), F32),
        ],
        scratch_shapes=[pltpu.VMEM((keys, block), F32)] * 2,
        compiler_params=pltpu.CompilerParams(vmem_limit_bytes=56 << 20),
        cost_estimate=pl.CostEstimate(
            flops=16 * queries * keys * width, transcendentals=queries * keys * 2 * pairs, bytes_accessed=2 * width * (queries + 2 * keys)
        ),
        name="attend",
    )(k, qt, vt, aug)


def three_terms(row, values):
    high = values.astype(BF).astype(F32)
    middle = (values - high).astype(BF).astype(F32)
    low = values - high - middle
    return jnp.where(row == 1, high, 0.0) + jnp.where(row == 2, middle, 0.0) + jnp.where(row == 3, low, 0.0)


def attend_back_kernel(
    chunk, k_ref, kt_ref, v_ref, qt_ref, q_ref, gt_ref, g_ref, aug_ref, lse_ref, delta_ref, dqt_ref, dk_ref, dv_ref, dk_sum, dv_sum
):
    step = pl.program_id(1)
    keys = k_ref.shape[0]
    queries = qt_ref.shape[1]

    @pl.when(step == 0)
    def _():
        dk_sum[...] = jnp.zeros_like(dk_sum)
        dv_sum[...] = jnp.zeros_like(dv_sum)

    qt = qt_ref[...]
    gt = gt_ref[...]
    q = q_ref[...]
    g = g_ref[...]
    row = lax.broadcasted_iota(jnp.int32, (128, queries), 0)
    lane = lax.broadcasted_iota(jnp.int32, (queries, 128), 1)
    query_cols, grad_cols, query_rows, grad_rows = [], [], [], []
    for h in range(2):
        down = (row >= HD * h) & (row < HD * h + HD)
        across = (lane >= HD * h) & (lane < HD * h + HD)
        tail = three_terms(row, lse_ref[h : h + 1, :] * (1.0 / SCALE)) + jnp.where(row == 0, 1.0, 0.0)
        query_cols.append(jnp.concatenate([jnp.where(down, qt, 0).astype(BF), tail.astype(BF)], axis=0))
        tail = three_terms(row, delta_ref[h : h + 1, :])
        grad_cols.append(jnp.concatenate([jnp.where(down, gt, 0).astype(BF), tail.astype(BF)], axis=0))
        query_rows.append(jnp.where(across, q, 0).astype(BF))
        grad_rows.append(jnp.where(across, g, 0).astype(BF))
    query_rows = jnp.concatenate(query_rows, axis=0)
    grad_rows = jnp.concatenate(grad_rows, axis=0)
    dq = [jnp.zeros((HD, queries), F32)] * 2
    for c in range(keys // chunk):
        part = slice(c * chunk, (c + 1) * chunk)
        aug = aug_ref[part, :]
        key = jnp.concatenate([k_ref[part, :], aug], axis=1)
        value = jnp.concatenate([v_ref[part, :], aug], axis=1)
        weights, grads = [], []
        for h in range(2):
            weight = jnp.exp2(dot_nn(key, query_cols[h]) * EXP2_SCALE)
            grad = (weight * dot_nn(value, grad_cols[h])).astype(BF)
            weights.append(weight.astype(BF))
            grads.append(grad)
            dq[h] = dq[h] + dot_nn(kt_ref[HD * h : HD * h + HD, part], grad)
        dv_sum[part, :] += dot_nn(jnp.concatenate(weights, axis=1), grad_rows)
        dk_sum[part, :] += dot_nn(jnp.concatenate(grads, axis=1), query_rows)
    for h in range(2):
        dqt_ref[HD * h : HD * h + HD, :] = (dq[h] * SCALE).astype(BF)

    @pl.when(step == pl.num_programs(1) - 1)
    def _():
        dk_ref[...] = (dk_sum[...] * SCALE).astype(BF)
        dv_ref[...] = dv_sum[...].astype(BF)


def attend_back(k, kt, v, qt, q, gt, g, aug, lse, delta):
    keys, width = k.shape
    queries = qt.shape[1]
    pairs = width // 128
    block = min(1024, queries)
    chunk = min(256, keys)
    key_rows = pl.BlockSpec((keys, 128), lambda g, i: (0, g))
    query_cols = pl.BlockSpec((128, block), lambda g, i: (g, i))
    query_rows = pl.BlockSpec((block, 128), lambda g, i: (i, g))
    stats = pl.BlockSpec((None, 2, block), lambda g, i: (g, 0, i))
    return pl.pallas_call(
        functools.partial(attend_back_kernel, chunk),
        grid=(pairs, queries // block),
        in_specs=[
            key_rows,
            pl.BlockSpec((128, keys), lambda g, i: (g, 0)),
            key_rows,
            query_cols,
            query_rows,
            query_cols,
            query_rows,
            pl.BlockSpec((keys, 128), lambda g, i: (0, 0)),
            stats,
            stats,
        ],
        out_specs=[query_cols, key_rows, key_rows],
        out_shape=[
            jax.ShapeDtypeStruct((width, queries), BF),
            jax.ShapeDtypeStruct((keys, width), BF),
            jax.ShapeDtypeStruct((keys, width), BF),
        ],
        scratch_shapes=[pltpu.VMEM((keys, 128), F32)] * 2,
        compiler_params=pltpu.CompilerParams(vmem_limit_bytes=56 << 20),
        cost_estimate=pl.CostEstimate(
            flops=40 * queries * keys * width, transcendentals=queries * keys * 2 * pairs, bytes_accessed=2 * width * (5 * queries + 5 * keys)
        ),
        name="attend_back",
    )(k, kt, v, qt, q, gt, g, aug, lse, delta)


MESH = pl.DeviceIdType.MESH


class Links:
    def __init__(self, depth, send_sem, recv_sem):
        index = lax.axis_index("dp")
        self.depth = depth
        self.core = index % 2
        self.near = (index // 2) % 2
        self.far = index // 4
        self.seq = lax.axis_index("seq")
        self.send_sem, self.recv_sem = send_sem, recv_sem

    def peer(self, core=None, near=None, far=None):
        core = self.core if core is None else core
        near = self.near if near is None else near
        far = self.far if far is None else far
        return {"dp": (far * 2 + near) * 2 + core}

    def to_core(self):
        return self.peer(core=1 - self.core)

    def to_near(self):
        return self.peer(near=1 - self.near)

    def to_far(self, k):
        return self.peer(far=(self.far + k) % self.depth)

    def to_seq(self):
        return {"seq": 1 - self.seq}

    def all_peers(self):
        return [self.to_core(), self.to_near(), self.to_seq()] + [self.to_far(k) for k in range(1, self.depth)]

    def barrier(self):
        semaphore = pltpu.get_barrier_semaphore()
        peers = self.all_peers()
        for peer in peers:
            pl.semaphore_signal(semaphore, inc=1, device_id=peer, device_id_type=MESH)
        pl.semaphore_wait(semaphore, len(peers))

    def copy(self, src, dst, index, peer):
        return self.copy_two(src, dst, index, index, peer)

    def copy_two(self, src, dst, send, recv, peer):
        return pltpu.make_async_remote_copy(
            src_ref=src, dst_ref=dst, send_sem=self.send_sem.at[send], recv_sem=self.recv_sem.at[recv], device_id=peer, device_id_type=MESH
        )


class Piece:
    def __init__(self, links, base, own, from_core, from_near, from_far, from_seq):
        self.links, self.base = links, base
        self.own, self.from_core, self.from_near, self.from_far, self.from_seq = own, from_core, from_near, from_far, from_seq

    def near_copy(self):
        k = self.links
        return k.copy(self.own.at[:, 1 - k.near], self.from_near, self.base + 1, k.to_near())

    def far_copy(self, distance):
        k = self.links
        target = (k.far + distance) % k.depth
        return k.copy(self.own.at[target, k.near], self.from_far.at[distance - 1], self.base + 2 + distance, k.to_far(distance))

    def seq_copy(self):
        k = self.links
        return k.copy(self.own.at[k.far, k.near], self.from_seq, self.base + 2, k.to_seq())

    def send_near(self):
        k = self.links
        for z in range(k.depth):
            total = self.own[z, 1 - k.near].astype(F32) + self.from_core[z, 1 - k.near].astype(F32)
            self.own[z, 1 - k.near] = total.astype(BF)
        self.near_copy().start()

    def send_far(self):
        k = self.links
        self.near_copy().wait_recv()
        for z in range(k.depth):
            total = self.own[z, k.near].astype(F32) + self.from_core[z, k.near].astype(F32) + self.from_near[z].astype(F32)
            self.own[z, k.near] = total.astype(BF)
        for distance in range(1, k.depth):
            self.far_copy(distance).start()

    def send_seq(self):
        k = self.links
        total = self.own[k.far, k.near].astype(F32)
        for distance in range(1, k.depth):
            self.far_copy(distance).wait_recv()
            total = total + self.from_far[distance - 1].astype(F32)
        self.own[k.far, k.near] = total.astype(BF)
        self.seq_copy().start()

    def result(self):
        k = self.links
        self.seq_copy().wait_recv()
        return self.own[k.far, k.near].astype(F32) + self.from_seq[...].astype(F32)

    def finish(self):
        self.near_copy().wait_send()
        for distance in range(1, self.links.depth):
            self.far_copy(distance).wait_send()
        self.seq_copy().wait_send()


def back_kernel(depth, pairs, early, chunk, *refs):
    k_ref, kt_ref, v_ref, qt_ref, q_ref, gt_ref, g_ref, aug_ref, lse_ref, delta_ref, w_ref, xt_ref, one_ref, sums_ref = refs[:14]
    n_src = 1 + max(source for source, _, _ in early)
    sources = refs[14 : 14 + n_src]
    refs = refs[14 + n_src :]
    share_qkv = refs[0]
    shares = refs[1 : 1 + n_src]
    sums_out, tokens_out = refs[1 + n_src : 3 + n_src]
    refs = refs[3 + n_src :]
    stage = [refs[5 * e : 5 * e + 5] for e in range(len(early))]
    refs = refs[5 * len(early) :]
    p_full, p_core, p_near, p_far, p_seq, acc, dq_sum, tok_send, tok_recv, dqkv = refs[:10]
    s_own, s_core, s_near, s_far, s_seq, send_sem, recv_sem, local_sem = refs[10:]

    step = pl.program_id(0)
    last = 2 * pairs - 1
    g = step % pairs
    rows = k_ref.shape[0]
    queries = qt_ref.shape[1]
    width = pairs * 128
    links = Links(depth, send_sem, recv_sem)
    span = depth + 2
    pieces = [Piece(links, e * span, *stage[e]) for e in range(len(early))]
    pair_base = len(early) * span
    sums_base = pair_base + pairs * span

    def pair_piece(index):
        own = p_full.at[index, :, :, links.core]
        return Piece(links, pair_base + index * span, own, p_core.at[index], p_near.at[index], p_far.at[index], p_seq.at[index])

    def pair_core_copy(index):
        return links.copy(p_full.at[index, :, :, 1 - links.core], p_core.at[index], pair_base + index * span, links.to_core())

    def early_core_copy(e):
        source, start, wide = early[e]
        part = sources[source].at[:, :, 1 - links.core, :, pl.ds(start, wide)]
        return links.copy(part, stage[e][1], e * span, links.to_core())

    def early_load(e):
        source, start, wide = early[e]
        part = sources[source].at[:, :, links.core, :, pl.ds(start, wide)]
        return pltpu.make_async_copy(part, stage[e][0], local_sem.at[e])

    one_copy = pltpu.make_async_copy(one_ref, acc, local_sem.at[len(early)])
    tokens_copy = links.copy(tok_send, tok_recv, sums_base + span, links.to_seq())

    def early_begin(e):
        early_core_copy(e).start()
        early_load(e).start()

    def early_near(e):
        early_load(e).wait()
        early_core_copy(e).wait_recv()
        pieces[e].send_near()

    def early_far(e):
        pieces[e].send_far()

    def early_seq(e):
        pieces[e].send_seq()

    def early_done(e):
        source, start, wide = early[e]
        shares[source][:, start : start + wide] = pieces[e].result()

    def pair_near(index):
        pair_core_copy(index).wait_recv()
        pair_piece(index).send_near()

    def pair_done(index):
        value = pair_piece(index).result()
        for third in range(3):
            at = pl.multiple_of((third * pairs + index) * 128, 128)
            share_qkv[:, pl.ds(at, 128)] = value[:, third * 128 : third * 128 + 128]

    @pl.when(step == 0)
    def _():
        links.barrier()
        early_begin(0)
        early_begin(1)
        one_copy.start()
        s_own[0] = sums_ref[...]

    def at(when, *actions):
        @pl.when(step == when)
        def _():
            for action, e in actions:
                action(e)

    lane = lax.broadcasted_iota(jnp.int32, (1, 128), 1)
    row = lax.broadcasted_iota(jnp.int32, (16, queries), 0)
    none = jnp.zeros((HD, queries), BF)
    rest = jnp.zeros((112, queries), BF)
    query_cols, grad_cols, query_rows, grad_rows = [], [], [], []
    for h in range(2):

        def placed(ref):
            half = ref[HD * h : HD * h + HD, :]
            return [half, none] if h == 0 else [none, half]

        tail = three_terms(row, lse_ref[h : h + 1, :] * (1.0 / SCALE)) + jnp.where(row == 0, 1.0, 0.0)
        query_cols.append(jnp.concatenate(placed(qt_ref) + [tail.astype(BF), rest], axis=0))
        tail = three_terms(row, delta_ref[h : h + 1, :])
        grad_cols.append(jnp.concatenate(placed(gt_ref) + [tail.astype(BF), rest], axis=0))
        mine = jnp.where((lane >= HD * h) & (lane < HD * h + HD), 1.0, 0.0).astype(BF)
        query_rows.append(q_ref[...] * mine)
        grad_rows.append(g_ref[...] * mine)
    query_rows = jnp.concatenate(query_rows, axis=0)
    grad_rows = jnp.concatenate(grad_rows, axis=0)
    nothing = jnp.zeros((HD, chunk), BF)
    dq = jnp.zeros((128, queries), F32)
    dv_total = jnp.zeros((1, 128), F32)

    def column(third):
        return pl.ds(pl.multiple_of((third * pairs + g) * 128, 128), 128)

    chunks = rows // chunk
    for c in range(chunks):
        part = slice(c * chunk, (c + 1) * chunk)
        aug = aug_ref[part, :]
        key = jnp.concatenate([k_ref[part, :], aug], axis=1)
        value = jnp.concatenate([v_ref[part, :], aug], axis=1)
        weights, grads = [], []
        for h in range(2):
            weight = jnp.exp2(dot_nn(key, query_cols[h]) * EXP2_SCALE)
            grads.append((weight * dot_nn(value, grad_cols[h])).astype(BF))
            weights.append(weight.astype(BF))
        upper = jnp.concatenate([kt_ref[0:HD, part], nothing], axis=1)
        lower = jnp.concatenate([nothing, kt_ref[HD : 2 * HD, part]], axis=1)
        dq = dq + dot_nn(jnp.concatenate([upper, lower], axis=0), jnp.concatenate(grads, axis=0))
        dv = dot_nn(jnp.concatenate(weights, axis=1), grad_rows)
        dk = dot_nn(jnp.concatenate(grads, axis=1), query_rows)
        dqkv[part, column(1)] = (dk * SCALE).astype(BF)
        dqkv[part, column(2)] = dv.astype(BF)
        dv_total = dv_total + total_rows(dv)
        if c == chunks // 2 - 1:
            at(0, (early_near, 0))
            at(3, (early_near, 2))
            at(5, (early_near, 3))
            at(7, (early_near, 4), (early_far, 2), (early_seq, 1))
            at(9, (early_far, 3), (early_seq, 2))
            at(10, (early_far, 4))

            @pl.when(step >= pairs + 1)
            def _():
                pair_near(step - pairs - 1)

            @pl.when(step == pairs + 5)
            def _():
                pair_piece(1).send_far()

    @pl.when(step < pairs)
    def _():
        dq_sum[g] = dq
        pair = jnp.concatenate([dqkv[:, column(1)], dqkv[:, column(2)]], axis=1)
        half = dot_nn(xt_ref[...], pair)
        p_full[g, :, :, :, :, 128:384] = half.astype(BF).reshape(p_full.shape[1:5] + (256,))
        s_own[0, 1:2, column(0)] = dv_total

    @pl.when(step == pairs - 1)
    def _():
        tok_send[...] = dot_nt(dqkv[:, width:], w_ref[:, width:]).astype(BF)
        tokens_copy.start()

    @pl.when(step >= pairs)
    def _():
        turned = ((dq_sum[g] + dq) * SCALE).T
        low = turned.astype(BF)
        dqkv[:, column(0)] = low
        s_own[0, 0:1, column(0)] = total_rows(turned)
        s_own[0, 1:2, column(0)] += dv_total
        product = dot_nn(xt_ref[...], jnp.concatenate([low, dqkv[:, column(1)], dqkv[:, column(2)]], axis=1))
        shape = p_full.shape[1:5]
        before = p_full[g, :, :, :, :, 128:384].astype(F32)
        p_full[g, :, :, :, :, 0:128] = product[:, 0:128].astype(BF).reshape(shape + (128,))
        p_full[g, :, :, :, :, 128:384] = (product[:, 128:384].reshape(shape + (256,)) + before).astype(BF)
        pair_core_copy(g).start()

    at(0, (early_near, 1), (early_begin, 2), (early_begin, 3), (early_begin, 4))
    at(2, (early_far, 0))
    at(4, (early_far, 1), (early_seq, 0))

    @pl.when(step == pairs + 4)
    def _():
        pair_piece(0).send_far()

    @pl.when(step == last)
    def _():
        final = pairs - 1
        hops = [(s_core, 0, links.to_core()), (s_near, 1, links.to_near())]
        hops += [(s_far.at[k - 1], 2 + k, links.to_far(k)) for k in range(1, depth)]
        hops += [(s_seq, 2, links.to_seq())]
        level = [0, 1] + [2] * (depth - 1) + [3]
        sums = [links.copy(s_own.at[n], dst, sums_base + index, peer) for n, (dst, index, peer) in zip(level, hops)]
        sums[0].start()
        out_copies = []

        def tokens(n):
            part = pl.ds(n * (rows // 4), rows // 4)
            acc[part, :] += dot_nt(dqkv[part, :], w_ref[...]) + tok_recv[part, :].astype(F32)
            out_copies.append(pltpu.make_async_copy(acc.at[part], tokens_out.at[part], local_sem.at[len(early) + 1 + n]))
            out_copies[-1].start()

        tokens_copy.wait_recv()
        one_copy.wait()
        pair_piece(2).send_far()
        tokens(0)
        pair_near(final)
        sums[0].wait_recv()
        s_own[1] = s_own[0] + s_core[...]
        sums[1].start()
        pair_piece(3).send_far()
        tokens(1)
        early_seq(3)
        early_seq(4)
        tokens(2)
        pair_piece(final - 1).send_far()
        pair_piece(0).send_seq()
        pair_piece(1).send_seq()
        tokens(3)
        sums[1].wait_recv()
        s_own[2] = s_own[1] + s_near[...]
        for n in range(2, depth + 1):
            sums[n].start()
        pair_piece(final).send_far()
        for e in range(3):
            early_done(e)
        pair_piece(2).send_seq()
        pair_piece(3).send_seq()
        total = s_own[2]
        for n in range(2, depth + 1):
            sums[n].wait_recv()
            total = total + s_far[n - 2]
        s_own[3] = total
        sums[depth + 1].start()
        pair_piece(final - 1).send_seq()
        pair_piece(final).send_seq()
        early_done(3)
        early_done(4)
        for index in range(final):
            pair_done(index)
        sums[depth + 1].wait_recv()
        sums_out[...] = s_own[3] + s_seq[...]
        pair_done(final)
        for n in range(4):
            out_copies[n].wait()
        for item in sums:
            item.wait_send()
        tokens_copy.wait_send()
        for e in range(len(early)):
            early_core_copy(e).wait_send()
            pieces[e].finish()
        for index in range(pairs):
            pair_core_copy(index).wait_send()
            pair_piece(index).finish()


EARLY = ((0, 0, 2), (0, 1, 2), (1, 0, 2), (1, 1, 2), (2, 0, 1))


def back_reduce(k, kt, v, qt, q, gt, g, aug, lse, delta, full_qkv, xt, grad_one, sums, sources, depth):
    keys, width = k.shape
    rows = keys // 2
    pairs = width // 128
    chunk = min(512, rows // 2)
    share = width // (4 * depth)
    views = [s.reshape(depth, 2, 2, s.shape[0] // (4 * depth), s.shape[1]) for s in sources]
    early = [(n, part * (views[n].shape[-1] // of), views[n].shape[-1] // of) for n, part, of in EARLY]
    key_rows = pl.BlockSpec((rows, 128), lambda i: (1 - i // pairs, i % pairs))
    query_cols = pl.BlockSpec((128, rows), lambda i: (i % pairs, 0))
    query_rows = pl.BlockSpec((rows, 128), lambda i: (0, i % pairs))
    stats = pl.BlockSpec((None, 2, rows), lambda i: (i % pairs, 0, 0))
    whole = pl.BlockSpec(memory_space=pltpu.VMEM)
    there = pl.BlockSpec(memory_space=pl.ANY)
    stages = []
    for n, _, wide in early:
        high = views[n].shape[3]
        stages += [
            pltpu.VMEM((depth, 2, high, wide), BF),
            pltpu.VMEM((depth, 2, high, wide), BF),
            pltpu.VMEM((depth, high, wide), BF),
            pltpu.VMEM((depth - 1, high, wide), BF),
            pltpu.VMEM((high, wide), BF),
        ]
    copies = (len(early) + pairs + 1) * (depth + 2) + 1
    return pl.pallas_call(
        functools.partial(back_kernel, depth, pairs, early, chunk),
        grid=(2 * pairs,),
        in_specs=[
            key_rows,
            pl.BlockSpec((128, rows), lambda i: (i % pairs, 1 - i // pairs)),
            key_rows,
            query_cols,
            query_rows,
            query_cols,
            query_rows,
            pl.BlockSpec((rows, 128), lambda i: (1 - i // pairs, 0)),
            stats,
            stats,
            whole,
            pl.BlockSpec((width, rows), lambda i: (0, 1 - i // pairs)),
            there,
            whole,
        ]
        + [there] * len(views),
        out_specs=[whole] * (2 + len(views)) + [there],
        out_shape=[jax.ShapeDtypeStruct((share, 3 * width), F32)]
        + [jax.ShapeDtypeStruct(s.shape[3:], F32) for s in views]
        + [jax.ShapeDtypeStruct(sums.shape, F32), jax.ShapeDtypeStruct((rows, width), F32)],
        scratch_shapes=stages
        + [
            pltpu.VMEM((pairs, depth, 2, 2, share, 384), BF),
            pltpu.VMEM((pairs, depth, 2, share, 384), BF),
            pltpu.VMEM((pairs, depth, share, 384), BF),
            pltpu.VMEM((pairs, depth - 1, share, 384), BF),
            pltpu.VMEM((pairs, share, 384), BF),
            pltpu.VMEM((rows, width), F32),
            pltpu.VMEM((pairs, 128, rows), F32),
            pltpu.VMEM((rows, width), BF),
            pltpu.VMEM((rows, width), BF),
            pltpu.VMEM((rows, 3 * width), BF),
            pltpu.VMEM((4,) + sums.shape, F32),
            pltpu.VMEM(sums.shape, F32),
            pltpu.VMEM(sums.shape, F32),
            pltpu.VMEM((depth - 1,) + sums.shape, F32),
            pltpu.VMEM(sums.shape, F32),
            pltpu.SemaphoreType.DMA((copies,)),
            pltpu.SemaphoreType.DMA((copies,)),
            pltpu.SemaphoreType.DMA((len(early) + 5,)),
        ],
        compiler_params=pltpu.CompilerParams(vmem_limit_bytes=61 << 20, collective_id=1, has_side_effects=True),
        cost_estimate=pl.CostEstimate(
            flops=40 * rows * keys * width, transcendentals=rows * keys * 2 * pairs, bytes_accessed=2 * width * 20 * rows
        ),
        name="back_reduce",
    )(k, kt, v, qt, q, gt, g, aug, lse, delta, full_qkv, xt, grad_one, sums, *views)


class Spread:
    def __init__(self, links, base, share, full, local):
        self.links, self.share, self.full = links, share, full
        self.send_base = base * (4 * links.depth - 1)
        self.recv_base = base * 4 * links.depth
        k = links
        self.local = pltpu.make_async_copy(share, full.at[k.far, k.near, k.core], local)

    def index(self, far, near, core):
        return self.recv_base + (far * 2 + near) * 2 + core

    def copy(self, src, slot, send, peer):
        return self.links.copy_two(src, self.full.at[slot], self.send_base + send, self.index(*slot), peer)

    def source(self, k):
        return (self.links.far - k) % self.links.depth

    def far_copy(self, k):
        links = self.links
        return self.copy(self.share, (links.far, links.near, links.core), k - 1, links.to_far(k))

    def near_copy(self, k):
        links = self.links
        slot = (self.source(k), links.near, links.core)
        return self.copy(self.share if k == 0 else self.full.at[slot], slot, links.depth - 1 + k, links.to_near())

    def core_copy(self, k, across):
        links = self.links
        slot = (self.source(k), 1 - links.near if across else links.near, links.core)
        src = self.share if k == 0 and not across else self.full.at[slot]
        return self.copy(src, slot, 2 * links.depth - 1 + 2 * k + across, links.to_core())

    def arrive(self, far, near, core):
        self.copy(self.share, (far, near, core), 0, self.links.to_core()).wait_recv()

    def begin(self):
        self.local.start()
        for k in range(1, self.links.depth):
            self.far_copy(k).start()
        self.near_copy(0).start()
        self.core_copy(0, 0).start()

    def pass_far(self):
        links = self.links
        for k in range(1, links.depth):
            self.arrive(self.source(k), links.near, links.core)
            self.near_copy(k).start()
            self.core_copy(k, 0).start()

    def pass_near(self):
        links = self.links
        for k in range(links.depth):
            self.arrive(self.source(k), 1 - links.near, links.core)
            self.core_copy(k, 1).start()

    def complete(self):
        links = self.links
        for k in range(links.depth):
            for near in range(2):
                self.arrive(self.source(k), near, 1 - links.core)
        self.local.wait()

    def finish(self):
        for k in range(self.links.depth):
            if k:
                self.far_copy(k).wait_send()
            self.near_copy(k).wait_send()
            self.core_copy(k, 0).wait_send()
            self.core_copy(k, 1).wait_send()


ROWS = (0, 2, 3, 7, 8, 9, 10, 11)


def forward_kernel(depth, pairs, later, chunk, *refs):
    x_ref, aug_ref, qkv_share = refs[:3]
    vec_refs = refs[3 : 3 + len(ROWS)]
    refs = refs[3 + len(ROWS) :]
    n_src = 1 + max(source for source, _, _ in later)
    shares = refs[:n_src]
    refs = refs[n_src:]
    q_ref, qt_ref, k_ref, kt_ref, v_ref, o_ref, lse_ref, xt_ref, sums_ref, qkv_out = refs[:10]
    fulls = refs[10 : 10 + n_src]
    w_all, v_all, v_own, other, vt, bias, fitting, send_sem, recv_sem, local_sem = refs[10 + n_src :]
    g = pl.program_id(0)
    rows, width = x_ref.shape
    links = Links(depth, send_sem, recv_sem)
    first = Spread(links, 0, qkv_share, w_all, local_sem.at[0])
    vectors = Spread(links, 1, v_own, v_all, local_sem.at[1])
    pieces = []
    for n, (source, start, wide) in enumerate(later):
        part = pl.ds(start, wide)
        pieces.append(Spread(links, 2 + n, shares[source].at[:, part], fulls[source].at[:, :, :, :, part], local_sem.at[2 + n]))
    spare = (2 + len(later)) * (4 * depth)
    tokens_copy = links.copy_two(x_ref, other, spare, spare, links.to_seq())
    qkv_copy = pltpu.make_async_copy(w_all, qkv_out, local_sem.at[2 + len(later)])

    @pl.when(g == 0)
    def _():
        links.barrier()
        first.begin()
        tokens_copy.start()
        place = lax.axis_index("dp")
        fitting[...] = jnp.zeros_like(fitting)
        for n, ref in enumerate(vec_refs):
            fitting[n : n + 1, 0 : ref.shape[1]] = ref[...].astype(F32)
        values = fitting[...]
        fitted = {}
        for size in VECTOR_UNITS:
            fitted[size] = pltpu.roll(values, (place % (16 // size)) * (width * size // 16), 1)
        target = lax.broadcasted_iota(jnp.int32, (16, width), 0)
        total = jnp.zeros((16, width), F32)
        for n, (base, size) in enumerate(zip(ROWS, VECTOR_SIZES)):
            total = total + jnp.where(target == base + place // (16 // size), fitted[size][n : n + 1, :], 0.0)
        v_own[...] = total.astype(BF)
        vectors.begin()
        xt_ref[:, 0:rows] = x_ref[...].T
        first.pass_far()
        vectors.pass_far()
        pieces[0].begin()
        pieces[1].begin()
        first.pass_near()
        vectors.pass_near()
        first.complete()
        qkv_copy.start()
        vectors.complete()
        total = jnp.zeros((16, width), F32)
        for z in range(depth):
            for y in range(2):
                for c in range(2):
                    total = total + v_all[z, y, c].astype(F32)
        sums_ref[...] = total
        for n in range(pairs):
            bias[n, 0:2, :] = total[0:2, n * 128 : n * 128 + 128]

    def at(when, *actions):
        @pl.when(g == when)
        def _():
            for action in actions:
                action()

    def turn_other():
        xt_ref[:, rows : 2 * rows] = other[...].T

    def weight(third):
        column = pl.ds(pl.multiple_of((third * pairs + g) * 128, 128), 128)
        return w_all[:, :, :, :, column].reshape(width, 128)

    w_kv = jnp.concatenate([weight(1), weight(2)], axis=1)
    w_q = weight(0)
    bias_q = bias[g, 0:1, :]
    bias_v = bias[g, 1:2, :]
    q = dot_nn(x_ref[...], w_q) + bias_q
    q_ref[...] = q.astype(BF)
    qt_ref[...] = q.T.astype(BF)
    def project(n, tokens):
        part = slice(n * rows, n * rows + rows)
        kv = dot_nn(tokens[...], w_kv)
        k = kv[:, 0:128]
        v = kv[:, 128:256] + bias_v
        k_ref[part, :] = k.astype(BF)
        kt_ref[:, part] = k.T.astype(BF)
        v_ref[part, :] = v.astype(BF)
        vt[:, part] = v.T.astype(BF)

    row = lax.broadcasted_iota(jnp.int32, (16, rows), 0)
    tail = jnp.where(row == 0, 1.0, 0.0).astype(BF)
    none = jnp.zeros((HD, rows), BF)
    rest = jnp.zeros((112, rows), BF)
    queries = [
        jnp.concatenate([qt_ref[0:HD, :], none, tail, rest], axis=0),
        jnp.concatenate([none, qt_ref[HD : 2 * HD, :], tail, rest], axis=0),
    ]
    largest = [jnp.full((1, rows), -jnp.inf, F32)] * 2
    total = [jnp.zeros((1, rows), F32)] * 2
    context = [jnp.zeros((HD, rows), F32)] * 2

    def score(c, h):
        part = slice(c * chunk, (c + 1) * chunk)
        return dot_nn(jnp.concatenate([k_ref[part, :], aug_ref[part, :]], axis=1), queries[h])

    def attend_to(first, last):
        ahead = [score(first, h) for h in range(2)]
        for c in range(first, last):
            part = slice(c * chunk, (c + 1) * chunk)
            for h in range(2):
                scores = ahead[h]
                if c + 1 < last:
                    ahead[h] = score(c + 1, h)
                top = jnp.maximum(largest[h], jnp.max(scores, axis=0, keepdims=True))
                fade = jnp.exp2((largest[h] - top) * EXP2_SCALE)
                weights = jnp.exp2((scores - top) * EXP2_SCALE)
                largest[h] = top
                total[h] = total[h] * fade + total_rows(weights)
                context[h] = context[h] * fade + dot_nn(vt[HD * h : HD * h + HD, part], weights.astype(BF))

    project(0, x_ref)
    attend_to(0, rows // chunk)
    at(0, pieces[0].pass_far, pieces[2].begin, tokens_copy.wait_recv)
    at(1, pieces[2].pass_far, pieces[3].begin)
    at(2, pieces[4].begin)
    at(3, pieces[3].pass_far, pieces[2].pass_near)
    at(4, pieces[4].pass_far)
    project(1, other)
    attend_to(rows // chunk, 2 * rows // chunk)
    for h in range(2):
        o_ref[HD * h : HD * h + HD, :] = (context[h] / total[h]).astype(BF)
        lse_ref[h : h + 1, :] = largest[h] * SCALE + jnp.log(total[h])
    at(0, pieces[1].pass_far, pieces[0].pass_near, turn_other)
    at(1, pieces[1].pass_near)
    at(4, pieces[3].pass_near)

    @pl.when(g == pairs - 1)
    def _():
        pieces[4].pass_near()
        for piece in pieces:
            piece.complete()
        qkv_copy.wait()
        for piece in [first, vectors] + pieces:
            piece.finish()
        tokens_copy.wait_send()


VECTOR_SIZES = (2, 1, 4, 1, 1, 1, 1, 1)
VECTOR_UNITS = (1, 2, 4)
LATER = ((0, 0, 1), (1, 0, 2), (1, 1, 2), (2, 0, 2), (2, 1, 2))


def forward(x, aug, vectors, w_qkv, w_out, w_up, w_down, depth):
    rows, width = x.shape
    pairs = width // 128
    keys = 2 * rows
    chunk = min(512, rows)
    shares = (w_out, w_up, w_down)
    later = [(n, part * (shares[n].shape[1] // of), shares[n].shape[1] // of) for n, part, of in LATER]
    whole = pl.BlockSpec(memory_space=pltpu.VMEM)
    there = pl.BlockSpec(memory_space=pl.ANY)
    down = lambda high: pl.BlockSpec((high, 128), lambda i: (0, i))
    across = lambda wide: pl.BlockSpec((128, wide), lambda i: (i, 0))
    fulls = [(depth, 2, 2) + s.shape for s in (w_qkv,) + shares]
    low = lambda *shape: jax.ShapeDtypeStruct(shape, BF)
    copies = (2 + len(later)) * 4 * depth + 1
    return pl.pallas_call(
        functools.partial(forward_kernel, depth, pairs, later, chunk),
        grid=(pairs,),
        in_specs=[whole, whole, there] + [whole] * len(vectors) + [there] * 3,
        out_specs=[
            down(rows),
            across(rows),
            down(keys),
            across(keys),
            down(keys),
            across(rows),
            pl.BlockSpec((None, 2, rows), lambda i: (i, 0, 0)),
            whole,
            whole,
            there,
            there,
            there,
            there,
        ],
        out_shape=[
            low(rows, width),
            low(width, rows),
            low(keys, width),
            low(width, keys),
            low(keys, width),
            low(width, rows),
            jax.ShapeDtypeStruct((pairs, 2, rows), F32),
            low(width, keys),
            jax.ShapeDtypeStruct((16, width), F32),
        ]
        + [low(*f) for f in fulls],
        scratch_shapes=[
            pltpu.VMEM(fulls[0], BF),
            pltpu.VMEM((depth, 2, 2, 16, width), BF),
            pltpu.VMEM((16, width), BF),
            pltpu.VMEM((rows, width), BF),
            pltpu.VMEM((128, keys), BF),
            pltpu.VMEM((pairs, 8, 128), F32),
            pltpu.VMEM((8, width), F32),
            pltpu.SemaphoreType.DMA((copies,)),
            pltpu.SemaphoreType.DMA((copies,)),
            pltpu.SemaphoreType.DMA((3 + len(later),)),
        ],
        compiler_params=pltpu.CompilerParams(vmem_limit_bytes=58 << 20, collective_id=2, has_side_effects=True),
        cost_estimate=pl.CostEstimate(
            flops=16 * rows * keys * width, transcendentals=rows * keys * 2 * pairs, bytes_accessed=2 * width * 10 * keys
        ),
        name="forward",
    )(x, aug, w_qkv, *[v.reshape(1, -1) for v in vectors], *shares)


def back_plain(k, kt, v, qt, q, grad_context, aug, lse, delta, full_qkv, both, grad_one, grads, sources, sizes):
    width = k.shape[1]
    rows = q.shape[0]

    def scatter(value):
        return lax.psum_scatter(value.astype(BF), "dp", scatter_dimension=0, tiled=True)

    def over_seq(value):
        value = value.astype(BF)
        return value.astype(F32) + lax.ppermute(value, "seq", [(0, 1), (1, 0)]).astype(F32)

    share_wout, share_wup, share_wdown = [scatter(s) for s in sources]
    dqt, dk, dv = attend_back(k, kt, v, qt, q, grad_context.T, grad_context, aug, lse, delta)
    dq = dqt.T
    partial = dot_nt(jnp.concatenate([dk[rows:], dv[rows:]], axis=1), full_qkv[:, width:])
    partial = lax.ppermute(partial.astype(BF), "seq", [(0, 1), (1, 0)])
    own = jnp.concatenate([dq, dk[:rows], dv[:rows]], axis=1)
    grad_wq, grad_wk, grad_wv = dot_tn(both[:rows], dq), dot_tn(both, dk), dot_tn(both, dv)
    grad_inputs = grad_one + dot_nt(own, full_qkv) + partial.astype(F32)
    grads = (jnp.concatenate([column_sum(dq), column_sum(dv)]),) + tuple(grads)
    extra = sum(g.shape[0] for g in grads) // width
    packed = jnp.concatenate([g.reshape(-1, size) for g, size in zip(grads, sizes)], axis=1).reshape(width, extra)
    packed = jnp.pad(packed, ((0, 0), (0, 128 - extra)))
    share_qkv = over_seq(scatter(jnp.concatenate([grad_wq, grad_wk, grad_wv, packed], axis=1)))
    packed = share_qkv[:, 3 * width : 3 * width + extra].reshape(-1)
    out_vectors, start = [], 0
    for size in sizes:
        out_vectors.append(packed[start : start + size])
        start += size
    return share_qkv[:, : 3 * width], over_seq(share_wout), over_seq(share_wup), over_seq(share_wdown), out_vectors, grad_inputs


def normalize(values):
    center = jnp.mean(values, axis=-1, keepdims=True)
    shifted = values - center
    spread = jnp.mean(shifted * shifted, axis=-1, keepdims=True)
    scale = lax.rsqrt(spread + EPS)
    return shifted * scale, scale


def normalize_back(grad, normal, scale):
    mean = jnp.mean(grad, axis=-1, keepdims=True)
    along = jnp.mean(grad * normal, axis=-1, keepdims=True)
    return (grad - mean - normal * along) * scale


def middle_kernel(*refs):
    x_ref, ot_ref, vec_ref, cot_hbm, wout_hbm, wup_hbm, wdown_hbm = refs[:7]
    result_hbm, one_hbm, g_hbm, gt_hbm, delta_ref, sums_ref, gdown_hbm, gup_hbm, gout_hbm = refs[7:16]
    wout, wup, wdown, cot_buf, acts, pres, hiddens, branches, projs, normals, grads, result, turned_buf, stage, sem = refs[16:]
    rows, width = x_ref.shape
    ff = wup.shape[1]
    wide = ff // FF_PARTS
    copies = [
        pltpu.make_async_copy(src, dst, sem.at[n])
        for n, (src, dst) in enumerate(((wout_hbm, wout), (wup_hbm, wup), (wdown_hbm, wdown), (cot_hbm, cot_buf)))
    ]
    for copy in copies:
        copy.start()

    def vector(n):
        return vec_ref[n : n + 1, :]

    ot = ot_ref[...]
    context = ot.T
    copies[0].wait()
    attn = dot_nn(context, wout[...]) + vector(2)
    normal_one, scale_one = normalize(x_ref[...].astype(F32) + attn)
    normals[...] = normal_one
    low = (normal_one * vector(8) + vector(9)).astype(BF)
    hiddens[...] = low
    copies[1].wait()
    copies[2].wait()
    grads[...] = normals[...] * vector(8) + (vector(9) + vector(7))
    for c in range(FF_PARTS):
        part = slice(c * wide, (c + 1) * wide)
        row, start = divmod(c * wide, width)
        pre = dot_nn(hiddens[...], wup[:, part]) + vec_ref[3 + row : 4 + row, start : start + wide]
        bell = 0.5 * (1.0 + lax.erf(pre * 0.7071067811865476))
        act = (pre * bell).astype(BF)
        pres[:, part] = (bell + pre * (jnp.exp(-0.5 * pre * pre) * 0.3989422804014327)).astype(BF)
        acts[:, part] = act
        grads[...] += dot_nn(act, wdown[part, :])
    normal_two, scale_two = normalize(grads[...])
    result[...] = (normal_two * vector(10) + vector(11)).astype(BF)
    out_result = pltpu.make_async_copy(result, result_hbm, sem.at[4])
    out_result.start()
    copies[3].wait()
    cot = cot_buf[...].astype(F32)
    sums_ref[...] = jnp.zeros_like(sums_ref)
    sums_ref[10:11, :] = total_rows(cot * normal_two)
    sums_ref[11:12, :] = total_rows(cot)
    grad_two = normalize_back(cot * vector(10), normal_two, scale_two)
    grads[...] = grad_two
    branch = grad_two.astype(BF)
    branches[...] = branch
    sums_ref[7:8, :] = total_rows(branch.astype(F32))
    for c in range(FF_PARTS):
        part = slice(c * wide, (c + 1) * wide)
        row, start = divmod(c * wide, width)
        grad_pre = (dot_nt(branches[...], wdown[part, :]) * pres[:, part].astype(F32)).astype(BF)
        pres[:, part] = grad_pre
        sums_ref[3 + row : 4 + row, start : start + wide] = total_rows(grad_pre.astype(F32))
        grads[...] += dot_nt(grad_pre, wup[:, part])
    grad_hidden = grads[...]
    normal_one = normals[...]
    sums_ref[8:9, :] = total_rows(grad_hidden * normal_one)
    sums_ref[9:10, :] = total_rows(grad_hidden)
    grad_one = normalize_back(grad_hidden * vector(8), normal_one, scale_one)
    grads[...] = grad_one
    out_one = pltpu.make_async_copy(grads, one_hbm, sem.at[5])
    out_one.start()
    proj = grad_one.astype(BF)
    projs[...] = proj
    sums_ref[2:3, :] = total_rows(proj.astype(F32))
    grad_context = dot_nt(projs[...], wout[...])
    out_result.wait()
    result[...] = grad_context.astype(BF)
    out_g = pltpu.make_async_copy(result, g_hbm, sem.at[4])
    out_g.start()
    turned = grad_context.T.astype(BF)
    turned_buf[...] = turned
    out_gt = pltpu.make_async_copy(turned_buf, gt_hbm, sem.at[6])
    out_gt.start()
    each = (turned.astype(F32) * ot.astype(F32)).reshape(width // HD, HD, rows)
    delta_ref[...] = jnp.sum(each, axis=1).reshape(delta_ref.shape)

    outs = []

    def put(value, target):
        n = len(outs)
        if n >= 2:
            outs[n - 2].wait()
        stage[n % 2] = value.astype(BF)
        outs.append(pltpu.make_async_copy(stage.at[n % 2], target, sem.at[7 + n % 2]))
        outs[n].start()

    for c in range(ff // width):
        part = slice(c * width, (c + 1) * width)
        put(dot_nn(acts[:, part].T, branches[...]), gdown_hbm.at[pl.ds(c * width, width)])
    turned = hiddens[...].T
    for c in range(ff // width):
        part = slice(c * width, (c + 1) * width)
        put(dot_nn(turned, pres[:, part]), gup_hbm.at[:, pl.ds(c * width, width)])
    put(dot_nn(ot_ref[...], projs[...]), gout_hbm)
    for copy in outs[-2:] + [out_one, out_g, out_gt]:
        copy.wait()


FF_PARTS = 4


def middle(x, cotangent, context_t, vectors, w_out, w_up, w_down):
    rows, width = x.shape
    ff = w_up.shape[1]
    pairs = width // 128
    whole = pl.BlockSpec(memory_space=pltpu.VMEM)
    there = pl.BlockSpec(memory_space=pl.ANY)
    shape = jax.ShapeDtypeStruct
    return pl.pallas_call(
        middle_kernel,
        in_specs=[whole, whole, whole, there, there, there, there],
        out_specs=[there, there, there, there, whole, whole, there, there, there],
        out_shape=[
            shape((rows, width), BF),
            shape((rows, width), F32),
            shape((rows, width), BF),
            shape((width, rows), BF),
            shape((pairs, 2, rows), F32),
            shape((16, width), F32),
            shape((ff, width), BF),
            shape((width, ff), BF),
            shape((width, width), BF),
        ],
        scratch_shapes=[
            pltpu.VMEM((width, width), BF),
            pltpu.VMEM((width, ff), BF),
            pltpu.VMEM((ff, width), BF),
            pltpu.VMEM((rows, width), BF),
            pltpu.VMEM((rows, ff), BF),
            pltpu.VMEM((rows, ff), BF),
            pltpu.VMEM((rows, width), BF),
            pltpu.VMEM((rows, width), BF),
            pltpu.VMEM((rows, width), BF),
            pltpu.VMEM((rows, width), F32),
            pltpu.VMEM((rows, width), F32),
            pltpu.VMEM((rows, width), BF),
            pltpu.VMEM((width, rows), BF),
            pltpu.VMEM((2, width, width), BF),
            pltpu.SemaphoreType.DMA((9,)),
        ],
        compiler_params=pltpu.CompilerParams(vmem_limit_bytes=58 << 20),
        cost_estimate=pl.CostEstimate(
            flops=6 * rows * width * (width + 2 * ff), transcendentals=2 * rows * ff, bytes_accessed=8 * width * (width + 2 * ff)
        ),
        name="middle",
    )(x, context_t, vectors, cotangent, w_out, w_up, w_down)


def forward_plain(x, aug, vectors, w_qkv):
    width = x.shape[1]
    other = lax.ppermute(x, "seq", [(0, 1), (1, 0)])
    sizes = [v.shape[0] for v in vectors]
    share = w_qkv.shape[0]
    extra = sum(sizes) // share
    beside = jnp.concatenate(vectors).reshape(share, extra)
    beside = jnp.concatenate([w_qkv, jnp.pad(beside, ((0, 0), (0, 128 - extra)))], axis=1)
    full_qkv = lax.all_gather(beside, "dp", axis=0, tiled=True)
    full_vectors = full_qkv[:, 3 * width : 3 * width + extra].reshape(-1, sum(sizes)).astype(F32)
    full_qkv = full_qkv[:, : 3 * width]
    full, start = [], 0
    for size in sizes:
        full.append(full_vectors[:, start : start + size].reshape(-1))
        start += size
    both = jnp.concatenate([x, other], axis=0)
    q = (dot_nn(x, full_qkv[:, :width]) + full[0][:width]).astype(BF)
    k = dot_nn(both, full_qkv[:, width : 2 * width]).astype(BF)
    v = (dot_nn(both, full_qkv[:, 2 * width :]) + full[0][width:]).astype(BF)
    qt, kt, vt = q.T, k.T, v.T
    context_t, lse = attend(k, qt, vt, aug)
    return q, qt, k, kt, v, both, context_t, lse, full_qkv, full[1:]


def plain(x, aug, vectors, w_qkv, w_out, w_up, w_down, upstream):
    rows, width = x.shape
    sizes = [v.shape[0] for v in vectors]
    q, qt, k, kt, v, both, context_t, lse, full_qkv, full = forward_plain(x, aug, vectors, w_qkv)
    full_bout, full_bup, full_bdown, gain_one, shift_one, gain_two, shift_two = full
    full_wout, full_wup, full_wdown = [lax.all_gather(w, "dp", axis=0, tiled=True) for w in (w_out, w_up, w_down)]
    context = context_t.T
    attn_branch = dot_nn(context, full_wout) + full_bout
    resid_one = x.astype(F32) + attn_branch
    hidden_one, first_pull = jax.vjp(layer_norm, resid_one, gain_one, shift_one)
    hidden_low = hidden_one.astype(BF)
    pre_act = dot_nn(hidden_low, full_wup) + full_bup
    activated, gelu_pull = jax.vjp(gelu_exact, pre_act)
    act_low = activated.astype(BF)
    ffn_branch = dot_nn(act_low, full_wdown) + full_bdown
    resid_two = hidden_one + ffn_branch
    output, second_pull = jax.vjp(layer_norm, resid_two, gain_two, shift_two)
    grad_two, grad_gain_two, grad_shift_two = second_pull(upstream.astype(F32))
    grad_branch = grad_two.astype(BF)
    grad_wdown = dot_tn(act_low, grad_branch)
    grad_bdown = column_sum(grad_branch)
    (grad_pre,) = gelu_pull(dot_nt(grad_branch, full_wdown))
    grad_pre_low = grad_pre.astype(BF)
    grad_wup = dot_tn(hidden_low, grad_pre_low)
    grad_bup = column_sum(grad_pre_low)
    grad_hidden = grad_two + dot_nt(grad_pre_low, full_wup)
    grad_one, grad_gain_one, grad_shift_one = first_pull(grad_hidden)
    grad_proj = grad_one.astype(BF)
    grad_wout = dot_tn(context, grad_proj)
    grad_bout = column_sum(grad_proj)
    grad_context = dot_nt(grad_proj, full_wout).astype(BF)
    delta = jnp.sum((grad_context.astype(F32) * context.astype(F32)).reshape(rows, HEADS, HD), axis=-1)
    delta = delta.T.reshape(HEADS // 2, 2, rows)

    grads = (grad_bout, grad_bup, grad_bdown, grad_gain_one, grad_shift_one, grad_gain_two, grad_shift_two)
    share_qkv, share_out, share_up, share_down, out_vectors, grad_inputs = back_plain(
        k, kt, v, qt, q, grad_context, aug, lse, delta, full_qkv, both, grad_one, grads, (grad_wout, grad_wup, grad_wdown), sizes
    )
    return output.astype(BF), grad_inputs, share_qkv, share_out, share_up, share_down, out_vectors


def local(
    tokens,
    lengths,
    w_qkv,
    bias_qv,
    w_out,
    bias_out,
    w_up,
    bias_up,
    w_down,
    bias_down,
    gain_attn,
    shift_attn,
    gain_ffn,
    shift_ffn,
    cotangent,
):
    x = tokens[0]
    rows, width = x.shape
    ff = w_up.shape[1]
    me = lax.axis_index("seq")
    parts = lax.axis_size("dp")
    aligned = parts % 4 == 0 and width % (16 * parts) == 0 and ff % (16 * parts) == 0
    vectors = (bias_qv, bias_out, bias_up, bias_down, gain_attn, shift_attn, gain_ffn, shift_ffn)
    sizes = [v.shape[0] for v in vectors]
    aligned = aligned and tuple(s * parts for s in sizes) == tuple(n * width for n in VECTOR_SIZES) and parts == 16

    slot = jnp.arange(2 * rows)
    slot = jnp.where(slot < rows, me * rows + slot, (1 - me) * rows + slot - rows)
    lane = jnp.arange(128)
    masked = jnp.where(slot < lengths[0], 0.0, MASK)
    aug = jnp.where(lane[None] == 0, masked[:, None], jnp.where(lane[None] < 4, -1.0, 0.0)).astype(BF)

    if aligned:
        q, qt, k, kt, v, context_t, lse, xt, summed, full_qkv, full_wout, full_wup, full_wdown = forward(
            x, aug, vectors, w_qkv, w_out, w_up, w_down, parts // 4
        )
        full_qkv = full_qkv.reshape(width, 3 * width)
        output, grad_one, grad_context, grad_context_t, delta, sums, grad_wdown, grad_wup, grad_wout = middle(
            x, cotangent[0], context_t, summed, full_wout.reshape(width, width), full_wup.reshape(width, ff), full_wdown.reshape(ff, width)
        )
        sources = (grad_wdown, grad_wup, grad_wout)
        share_qkv, share_down, share_up, share_out, sums, grad_inputs = back_reduce(
            k, kt, v, qt, q, grad_context_t, grad_context, aug, lse, delta, full_qkv, xt, grad_one, sums, sources, parts // 4
        )
        out_vectors, start = [], 0
        sums = sums.reshape(-1)
        for size in sizes:
            out_vectors.append(lax.dynamic_slice(sums, (start * parts + lax.axis_index("dp") * size,), (size,)))
            start += size
    else:
        output, grad_inputs, share_qkv, share_out, share_up, share_down, out_vectors = plain(
            x, aug, vectors, w_qkv, w_out, w_up, w_down, cotangent[0]
        )
    s_bqv, s_bout, s_bup, s_bdown, s_gain_one, s_shift_one, s_gain_two, s_shift_two = out_vectors
    return (
        output[None],
        grad_inputs[None],
        share_qkv,
        s_bqv,
        share_out,
        s_bout,
        share_up,
        s_bup,
        share_down,
        s_bdown,
        s_gain_one,
        s_shift_one,
        s_gain_two,
        s_shift_two,
    )


def solution(mesh):
    act, mat, vec = P("dp", "seq", None), P("dp", None), P("dp")
    in_specs = (act, vec, mat, vec, mat, vec, mat, vec, mat, vec, vec, vec, vec, vec, act)
    out_specs = (act, act, mat, vec, mat, vec, mat, vec, mat, vec, vec, vec, vec, vec)
    return jax.shard_map(local, mesh=mesh, in_specs=in_specs, out_specs=out_specs, check_vma=False)
```

```python
import functools

import jax
import jax.numpy as jnp
from jax import lax
from jax.experimental import pallas as pl
from jax.experimental.pallas import tpu as pltpu
from jax.sharding import PartitionSpec as P

HEADS = 12
HD = 64
EPS = 1e-05
BF = jnp.bfloat16
F32 = jnp.float32
SCALE = HD**-0.5
EXP2_SCALE = SCALE * 1.4426950408889634
MASK = -8e9


def dot_nn(a, b):
    return lax.dot_general(a, b, (((1,), (0,)), ((), ())), preferred_element_type=F32)


def dot_nt(a, b):
    return lax.dot_general(a, b, (((1,), (1,)), ((), ())), preferred_element_type=F32)


def dot_tn(a, b):
    return lax.dot_general(a, b, (((0,), (0,)), ((), ())), preferred_element_type=F32)


def layer_norm(values, gain, offset):
    center = jnp.mean(values, axis=-1, keepdims=True)
    shifted = values - center
    spread = jnp.mean(shifted * shifted, axis=-1, keepdims=True)
    return shifted * lax.rsqrt(spread + EPS) * gain + offset


def gelu_exact(values):
    return 0.5 * values * (1.0 + lax.erf(values * 0.7071067811865476))


def column_sum(values):
    return jnp.sum(values.astype(F32), axis=0)


def total_rows(values):
    return jnp.sum(values, axis=0, keepdims=True)


def attend_kernel(chunk, k_ref, qt_ref, vt_ref, aug_ref, o_ref, lse_ref, *scratch):
    keys = k_ref.shape[0]
    queries = qt_ref.shape[1]
    qt = qt_ref[...]
    row = lax.broadcasted_iota(jnp.int32, (128, queries), 0)
    tail = jnp.where(row == 0, 1.0, 0.0).astype(BF)
    for h in range(2):
        held = scratch[h]
        mine = jnp.where((row >= HD * h) & (row < HD * h + HD), qt, 0).astype(BF)
        query = jnp.concatenate([mine, tail], axis=0)
        largest = jnp.full((1, queries), -jnp.inf, F32)
        for c in range(keys // chunk):
            part = slice(c * chunk, (c + 1) * chunk)
            key = jnp.concatenate([k_ref[part, :], aug_ref[part, :]], axis=1)
            scores = dot_nn(key, query)
            held[part, :] = scores
            largest = jnp.maximum(largest, jnp.max(scores, axis=0, keepdims=True))
        total = jnp.zeros((1, queries), F32)
        context = jnp.zeros((HD, queries), F32)
        base = largest * EXP2_SCALE
        for c in range(keys // chunk):
            part = slice(c * chunk, (c + 1) * chunk)
            weight = jnp.exp2(held[part, :] * EXP2_SCALE - base)
            total = total + jnp.sum(weight, axis=0, keepdims=True)
            context = context + dot_nn(vt_ref[HD * h : HD * h + HD, part], weight.astype(BF))
        o_ref[HD * h : HD * h + HD, :] = (context / total).astype(BF)
        lse_ref[h : h + 1, :] = largest * SCALE + jnp.log(total)


def attend(k, qt, vt, aug):
    keys, width = k.shape
    queries = qt.shape[1]
    pairs = width // 128
    block = min(1024, queries)
    chunk = min(256, keys)
    return pl.pallas_call(
        functools.partial(attend_kernel, chunk),
        grid=(pairs, queries // block),
        in_specs=[
            pl.BlockSpec((keys, 128), lambda g, i: (0, g)),
            pl.BlockSpec((128, block), lambda g, i: (g, i)),
            pl.BlockSpec((128, keys), lambda g, i: (g, 0)),
            pl.BlockSpec((keys, 128), lambda g, i: (0, 0)),
        ],
        out_specs=[
            pl.BlockSpec((128, block), lambda g, i: (g, i)),
            pl.BlockSpec((None, 2, block), lambda g, i: (g, 0, i)),
        ],
        out_shape=[
            jax.ShapeDtypeStruct((width, queries), BF),
            jax.ShapeDtypeStruct((pairs, 2, queries), F32),
        ],
        scratch_shapes=[pltpu.VMEM((keys, block), F32)] * 2,
        compiler_params=pltpu.CompilerParams(vmem_limit_bytes=56 << 20),
        cost_estimate=pl.CostEstimate(
            flops=16 * queries * keys * width, transcendentals=queries * keys * 2 * pairs, bytes_accessed=2 * width * (queries + 2 * keys)
        ),
        name="attend",
    )(k, qt, vt, aug)


def three_terms(row, values):
    high = values.astype(BF).astype(F32)
    middle = (values - high).astype(BF).astype(F32)
    low = values - high - middle
    return jnp.where(row == 1, high, 0.0) + jnp.where(row == 2, middle, 0.0) + jnp.where(row == 3, low, 0.0)


def attend_back_kernel(
    chunk, k_ref, kt_ref, v_ref, qt_ref, q_ref, gt_ref, g_ref, aug_ref, lse_ref, delta_ref, dqt_ref, dk_ref, dv_ref, dk_sum, dv_sum
):
    step = pl.program_id(1)
    keys = k_ref.shape[0]
    queries = qt_ref.shape[1]

    @pl.when(step == 0)
    def _():
        dk_sum[...] = jnp.zeros_like(dk_sum)
        dv_sum[...] = jnp.zeros_like(dv_sum)

    qt = qt_ref[...]
    gt = gt_ref[...]
    q = q_ref[...]
    g = g_ref[...]
    row = lax.broadcasted_iota(jnp.int32, (128, queries), 0)
    lane = lax.broadcasted_iota(jnp.int32, (queries, 128), 1)
    query_cols, grad_cols, query_rows, grad_rows = [], [], [], []
    for h in range(2):
        down = (row >= HD * h) & (row < HD * h + HD)
        across = (lane >= HD * h) & (lane < HD * h + HD)
        tail = three_terms(row, lse_ref[h : h + 1, :] * (1.0 / SCALE)) + jnp.where(row == 0, 1.0, 0.0)
        query_cols.append(jnp.concatenate([jnp.where(down, qt, 0).astype(BF), tail.astype(BF)], axis=0))
        tail = three_terms(row, delta_ref[h : h + 1, :])
        grad_cols.append(jnp.concatenate([jnp.where(down, gt, 0).astype(BF), tail.astype(BF)], axis=0))
        query_rows.append(jnp.where(across, q, 0).astype(BF))
        grad_rows.append(jnp.where(across, g, 0).astype(BF))
    query_rows = jnp.concatenate(query_rows, axis=0)
    grad_rows = jnp.concatenate(grad_rows, axis=0)
    dq = [jnp.zeros((HD, queries), F32)] * 2
    for c in range(keys // chunk):
        part = slice(c * chunk, (c + 1) * chunk)
        aug = aug_ref[part, :]
        key = jnp.concatenate([k_ref[part, :], aug], axis=1)
        value = jnp.concatenate([v_ref[part, :], aug], axis=1)
        weights, grads = [], []
        for h in range(2):
            weight = jnp.exp2(dot_nn(key, query_cols[h]) * EXP2_SCALE)
            grad = (weight * dot_nn(value, grad_cols[h])).astype(BF)
            weights.append(weight.astype(BF))
            grads.append(grad)
            dq[h] = dq[h] + dot_nn(kt_ref[HD * h : HD * h + HD, part], grad)
        dv_sum[part, :] += dot_nn(jnp.concatenate(weights, axis=1), grad_rows)
        dk_sum[part, :] += dot_nn(jnp.concatenate(grads, axis=1), query_rows)
    for h in range(2):
        dqt_ref[HD * h : HD * h + HD, :] = (dq[h] * SCALE).astype(BF)

    @pl.when(step == pl.num_programs(1) - 1)
    def _():
        dk_ref[...] = (dk_sum[...] * SCALE).astype(BF)
        dv_ref[...] = dv_sum[...].astype(BF)


def attend_back(k, kt, v, qt, q, gt, g, aug, lse, delta):
    keys, width = k.shape
    queries = qt.shape[1]
    pairs = width // 128
    block = min(1024, queries)
    chunk = min(256, keys)
    key_rows = pl.BlockSpec((keys, 128), lambda g, i: (0, g))
    query_cols = pl.BlockSpec((128, block), lambda g, i: (g, i))
    query_rows = pl.BlockSpec((block, 128), lambda g, i: (i, g))
    stats = pl.BlockSpec((None, 2, block), lambda g, i: (g, 0, i))
    return pl.pallas_call(
        functools.partial(attend_back_kernel, chunk),
        grid=(pairs, queries // block),
        in_specs=[
            key_rows,
            pl.BlockSpec((128, keys), lambda g, i: (g, 0)),
            key_rows,
            query_cols,
            query_rows,
            query_cols,
            query_rows,
            pl.BlockSpec((keys, 128), lambda g, i: (0, 0)),
            stats,
            stats,
        ],
        out_specs=[query_cols, key_rows, key_rows],
        out_shape=[
            jax.ShapeDtypeStruct((width, queries), BF),
            jax.ShapeDtypeStruct((keys, width), BF),
            jax.ShapeDtypeStruct((keys, width), BF),
        ],
        scratch_shapes=[pltpu.VMEM((keys, 128), F32)] * 2,
        compiler_params=pltpu.CompilerParams(vmem_limit_bytes=56 << 20),
        cost_estimate=pl.CostEstimate(
            flops=40 * queries * keys * width, transcendentals=queries * keys * 2 * pairs, bytes_accessed=2 * width * (5 * queries + 5 * keys)
        ),
        name="attend_back",
    )(k, kt, v, qt, q, gt, g, aug, lse, delta)


MESH = pl.DeviceIdType.MESH


class Links:
    def __init__(self, depth, send_sem, recv_sem):
        index = lax.axis_index("dp")
        self.depth = depth
        self.core = index % 2
        self.near = (index // 2) % 2
        self.far = index // 4
        self.seq = lax.axis_index("seq")
        self.ring = [self.far] + [(self.far + k) % depth for k in range(1, depth)]
        if depth == 4:
            orders = ((0, 1, 2, 3), (1, 0, 2, 3), (2, 1, 3, 0), (3, 2, 1, 0))
            for n in range(1, 4):
                self.ring[n] = sum(jnp.where(self.far == place, orders[place][n], 0) for place in range(4))
        self.send_sem, self.recv_sem = send_sem, recv_sem

    def peer(self, core=None, near=None, far=None):
        core = self.core if core is None else core
        near = self.near if near is None else near
        far = self.far if far is None else far
        return {"dp": (far * 2 + near) * 2 + core}

    def to_core(self):
        return self.peer(core=1 - self.core)

    def to_near(self):
        return self.peer(near=1 - self.near)

    def to_far(self, k):
        return self.peer(far=(self.far + k) % self.depth)

    def to_seq(self):
        return {"seq": 1 - self.seq}

    def all_peers(self):
        return [self.to_core(), self.to_near(), self.to_seq()] + [self.to_far(k) for k in range(1, self.depth)]

    def barrier(self):
        semaphore = pltpu.get_barrier_semaphore()
        peers = self.all_peers()
        for peer in peers:
            pl.semaphore_signal(semaphore, inc=1, device_id=peer, device_id_type=MESH)
        pl.semaphore_wait(semaphore, len(peers))

    def copy(self, src, dst, index, peer):
        return self.copy_two(src, dst, index, index, peer)

    def copy_two(self, src, dst, send, recv, peer):
        return pltpu.make_async_remote_copy(
            src_ref=src, dst_ref=dst, send_sem=self.send_sem.at[send], recv_sem=self.recv_sem.at[recv], device_id=peer, device_id_type=MESH
        )


class Piece:
    def __init__(self, links, base, own, from_core, from_near, from_far, from_seq):
        self.links, self.base = links, base
        self.own, self.from_core, self.from_near, self.from_far, self.from_seq = own, from_core, from_near, from_far, from_seq

    def near_copy(self):
        k = self.links
        return k.copy(self.own.at[:, 1 - k.near], self.from_near, self.base + 1, k.to_near())

    def far_copy(self, distance):
        k = self.links
        target = (k.far + distance) % k.depth
        return k.copy(self.own.at[target, k.near], self.from_far.at[distance - 1], self.base + 2 + distance, k.to_far(distance))

    def seq_copy(self):
        k = self.links
        return k.copy(self.own.at[k.far, k.near], self.from_seq, self.base + 2, k.to_seq())

    def send_near(self):
        k = self.links
        for z in range(k.depth):
            total = self.own[z, 1 - k.near].astype(F32) + self.from_core[z, 1 - k.near].astype(F32)
            self.own[z, 1 - k.near] = total.astype(BF)
        self.near_copy().start()

    def send_far(self):
        k = self.links
        self.near_copy().wait_recv()
        for z in range(k.depth):
            total = self.own[z, k.near].astype(F32) + self.from_core[z, k.near].astype(F32) + self.from_near[z].astype(F32)
            self.own[z, k.near] = total.astype(BF)
        for distance in range(1, k.depth):
            self.far_copy(distance).start()

    def send_seq(self):
        k = self.links
        total = self.own[k.far, k.near].astype(F32)
        for distance in range(1, k.depth):
            self.far_copy(distance).wait_recv()
            total = total + self.from_far[distance - 1].astype(F32)
        self.own[k.far, k.near] = total.astype(BF)
        self.seq_copy().start()

    def result(self):
        k = self.links
        self.seq_copy().wait_recv()
        return self.own[k.far, k.near].astype(F32) + self.from_seq[...].astype(F32)

    def finish(self):
        self.near_copy().wait_send()
        for distance in range(1, self.links.depth):
            self.far_copy(distance).wait_send()
        self.seq_copy().wait_send()


def back_kernel(depth, pairs, early, chunk, *refs):
    k_ref, kt_ref, v_ref, qt_ref, q_ref, gt_ref, g_ref, aug_ref, lse_ref, delta_ref, w_ref, xt_ref, one_ref, sums_ref = refs[:14]
    n_src = 1 + max(source for source, _, _ in early)
    sources = refs[14 : 14 + n_src]
    refs = refs[14 + n_src :]
    share_qkv = refs[0]
    shares = refs[1 : 1 + n_src]
    sums_out, tokens_out = refs[1 + n_src : 3 + n_src]
    refs = refs[3 + n_src :]
    stage = [refs[5 * e : 5 * e + 5] for e in range(len(early))]
    refs = refs[5 * len(early) :]
    p_full, p_core, p_near, p_far, p_seq, acc, dq_sum, tok_send, tok_recv, dqkv = refs[:10]
    s_own, s_core, s_near, s_far, s_seq, send_sem, recv_sem, local_sem = refs[10:]

    step = pl.program_id(0)
    last = 2 * pairs - 1
    g = step % pairs
    rows = k_ref.shape[0]
    queries = qt_ref.shape[1]
    width = pairs * 128
    links = Links(depth, send_sem, recv_sem)
    span = depth + 2
    pieces = [Piece(links, e * span, *stage[e]) for e in range(len(early))]
    pair_base = len(early) * span
    sums_base = pair_base + pairs * span

    def pair_piece(index):
        own = p_full.at[index, :, :, links.core]
        return Piece(links, pair_base + index * span, own, p_core.at[index], p_near.at[index], p_far.at[index], p_seq.at[index])

    def pair_core_copy(index):
        return links.copy(p_full.at[index, :, :, 1 - links.core], p_core.at[index], pair_base + index * span, links.to_core())

    def early_core_copy(e):
        source, start, wide = early[e]
        part = sources[source].at[:, :, 1 - links.core, :, pl.ds(start, wide)]
        return links.copy(part, stage[e][1], e * span, links.to_core())

    def early_load(e):
        source, start, wide = early[e]
        part = sources[source].at[:, :, links.core, :, pl.ds(start, wide)]
        return pltpu.make_async_copy(part, stage[e][0], local_sem.at[e])

    one_copy = pltpu.make_async_copy(one_ref, acc, local_sem.at[len(early)])
    tokens_copy = links.copy(tok_send, tok_recv, sums_base + span, links.to_seq())

    def early_begin(e):
        early_core_copy(e).start()
        early_load(e).start()

    def early_near(e):
        early_load(e).wait()
        early_core_copy(e).wait_recv()
        pieces[e].send_near()

    def early_far(e):
        pieces[e].send_far()

    def early_seq(e):
        pieces[e].send_seq()

    def early_done(e):
        source, start, wide = early[e]
        shares[source][:, start : start + wide] = pieces[e].result()

    def pair_near(index):
        pair_core_copy(index).wait_recv()
        pair_piece(index).send_near()

    def pair_done(index):
        value = pair_piece(index).result()
        for third in range(3):
            at = pl.multiple_of((third * pairs + index) * 128, 128)
            share_qkv[:, pl.ds(at, 128)] = value[:, third * 128 : third * 128 + 128]

    @pl.when(step == 0)
    def _():
        links.barrier()
        early_begin(0)
        early_begin(1)
        one_copy.start()
        s_own[0] = sums_ref[...]

    def at(when, *actions):
        @pl.when(step == when)
        def _():
            for action, e in actions:
                action(e)

    lane = lax.broadcasted_iota(jnp.int32, (1, 128), 1)
    row = lax.broadcasted_iota(jnp.int32, (16, queries), 0)
    none = jnp.zeros((HD, queries), BF)
    rest = jnp.zeros((112, queries), BF)
    query_cols, grad_cols, query_rows, grad_rows = [], [], [], []
    for h in range(2):

        def placed(ref):
            half = ref[HD * h : HD * h + HD, :]
            return [half, none] if h == 0 else [none, half]

        tail = three_terms(row, lse_ref[h : h + 1, :] * (1.0 / SCALE)) + jnp.where(row == 0, 1.0, 0.0)
        query_cols.append(jnp.concatenate(placed(qt_ref) + [tail.astype(BF), rest], axis=0))
        tail = three_terms(row, delta_ref[h : h + 1, :])
        grad_cols.append(jnp.concatenate(placed(gt_ref) + [tail.astype(BF), rest], axis=0))
        mine = jnp.where((lane >= HD * h) & (lane < HD * h + HD), 1.0, 0.0).astype(BF)
        query_rows.append(q_ref[...] * mine)
        grad_rows.append(g_ref[...] * mine)
    query_rows = jnp.concatenate(query_rows, axis=0)
    grad_rows = jnp.concatenate(grad_rows, axis=0)
    nothing = jnp.zeros((HD, chunk), BF)
    dq = jnp.zeros((128, queries), F32)
    dv_total = jnp.zeros((1, 128), F32)

    def column(third):
        return pl.ds(pl.multiple_of((third * pairs + g) * 128, 128), 128)

    chunks = rows // chunk
    for c in range(chunks):
        part = slice(c * chunk, (c + 1) * chunk)
        aug = aug_ref[part, :]
        key = jnp.concatenate([k_ref[part, :], aug], axis=1)
        value = jnp.concatenate([v_ref[part, :], aug], axis=1)
        weights, grads = [], []
        for h in range(2):
            weight = jnp.exp2(dot_nn(key, query_cols[h]) * EXP2_SCALE)
            grads.append((weight * dot_nn(value, grad_cols[h])).astype(BF))
            weights.append(weight.astype(BF))
        upper = jnp.concatenate([kt_ref[0:HD, part], nothing], axis=1)
        lower = jnp.concatenate([nothing, kt_ref[HD : 2 * HD, part]], axis=1)
        dq = dq + dot_nn(jnp.concatenate([upper, lower], axis=0), jnp.concatenate(grads, axis=0))
        dv = dot_nn(jnp.concatenate(weights, axis=1), grad_rows)
        dk = dot_nn(jnp.concatenate(grads, axis=1), query_rows)
        dqkv[part, column(1)] = (dk * SCALE).astype(BF)
        dqkv[part, column(2)] = dv.astype(BF)
        dv_total = dv_total + total_rows(dv)
        if c == chunks // 2 - 1:
            at(0, (early_near, 0))
            at(3, (early_near, 2))
            at(5, (early_near, 3))
            at(6, (early_far, 2), (early_seq, 0))
            at(7, (early_near, 4))
            at(8, (early_far, 3))
            at(9, (early_far, 4), (early_seq, 1))

            @pl.when(step >= pairs + 1)
            def _():
                pair_near(step - pairs - 1)

            @pl.when(step >= pairs + 4)
            def _():
                pair_piece(2 * (step - pairs) - 7).send_far()

    @pl.when(step < pairs)
    def _():
        dq_sum[g] = dq
        pair = jnp.concatenate([dqkv[:, column(1)], dqkv[:, column(2)]], axis=1)
        half = dot_nn(xt_ref[...], pair)
        p_full[g, :, :, :, :, 128:384] = half.astype(BF).reshape(p_full.shape[1:5] + (256,))
        s_own[0, 1:2, column(0)] = dv_total

    @pl.when(step == pairs - 1)
    def _():
        tok_send[...] = dot_nt(dqkv[:, width:], w_ref[:, width:]).astype(BF)
        tokens_copy.start()

    @pl.when(step >= pairs)
    def _():
        turned = ((dq_sum[g] + dq) * SCALE).T
        low = turned.astype(BF)
        dqkv[:, column(0)] = low
        s_own[0, 0:1, column(0)] = total_rows(turned)
        s_own[0, 1:2, column(0)] += dv_total
        product = dot_nn(xt_ref[...], jnp.concatenate([low, dqkv[:, column(1)], dqkv[:, column(2)]], axis=1))
        shape = p_full.shape[1:5]
        before = p_full[g, :, :, :, :, 128:384].astype(F32)
        p_full[g, :, :, :, :, 0:128] = product[:, 0:128].astype(BF).reshape(shape + (128,))
        p_full[g, :, :, :, :, 128:384] = (product[:, 128:384].reshape(shape + (256,)) + before).astype(BF)
        pair_core_copy(g).start()

    at(0, (early_near, 1), (early_begin, 2), (early_begin, 3), (early_begin, 4))
    at(2, (early_far, 0))
    at(4, (early_far, 1))
    at(10, (early_seq, 2))

    @pl.when((step >= pairs + 3) & (step < last))
    def _():
        pair_piece(2 * (step - pairs) - 6).send_far()

    @pl.when(step == last)
    def _():
        final = pairs - 1
        hops = [(s_core, 0, links.to_core()), (s_near, 1, links.to_near())]
        hops += [(s_far.at[k - 1], 2 + k, links.to_far(k)) for k in range(1, depth)]
        hops += [(s_seq, 2, links.to_seq())]
        level = [0, 1] + [2] * (depth - 1) + [3]
        sums = [links.copy(s_own.at[n], dst, sums_base + index, peer) for n, (dst, index, peer) in zip(level, hops)]
        sums[0].start()
        out_copies = []

        def tokens(n):
            part = pl.ds(n * (rows // 4), rows // 4)
            acc[part, :] += dot_nt(dqkv[part, :], w_ref[...]) + tok_recv[part, :].astype(F32)
            out_copies.append(pltpu.make_async_copy(acc.at[part], tokens_out.at[part], local_sem.at[len(early) + 1 + n]))
            out_copies[-1].start()

        pair_piece(final - 1).send_far()
        early_seq(3)
        tokens_copy.wait_recv()
        one_copy.wait()
        tokens(0)
        pair_near(final)
        sums[0].wait_recv()
        s_own[1] = s_own[0] + s_core[...]
        sums[1].start()
        early_seq(4)
        tokens(1)
        pair_piece(0).send_seq()
        pair_piece(1).send_seq()
        tokens(2)
        pair_piece(2).send_seq()
        pair_piece(final).send_far()
        sums[1].wait_recv()
        s_own[2] = s_own[1] + s_near[...]
        for n in range(2, depth + 1):
            sums[n].start()
        tokens(3)
        for e in range(4):
            early_done(e)
        pair_piece(3).send_seq()
        pair_piece(4).send_seq()
        pair_piece(final).send_seq()
        total = s_own[2]
        for n in range(2, depth + 1):
            sums[n].wait_recv()
            total = total + s_far[n - 2]
        s_own[3] = total
        sums[depth + 1].start()
        early_done(4)
        for index in range(pairs):
            pair_done(index)
        sums[depth + 1].wait_recv()
        sums_out[...] = s_own[3] + s_seq[...]
        for n in range(4):
            out_copies[n].wait()
        for item in sums:
            item.wait_send()
        tokens_copy.wait_send()
        for e in range(len(early)):
            early_core_copy(e).wait_send()
            pieces[e].finish()
        for index in range(pairs):
            pair_core_copy(index).wait_send()
            pair_piece(index).finish()


EARLY = ((0, 0, 2), (0, 1, 2), (1, 0, 2), (1, 1, 2), (2, 0, 1))


def back_reduce(k, kt, v, qt, q, gt, g, aug, lse, delta, full_qkv, xt, grad_one, sums, sources, depth):
    keys, width = k.shape
    rows = keys // 2
    pairs = width // 128
    chunk = min(512, rows // 2)
    share = width // (4 * depth)
    views = [s.reshape(depth, 2, 2, s.shape[0] // (4 * depth), s.shape[1]) for s in sources]
    early = [(n, part * (views[n].shape[-1] // of), views[n].shape[-1] // of) for n, part, of in EARLY]
    key_rows = pl.BlockSpec((rows, 128), lambda i: (1 - i // pairs, i % pairs))
    query_cols = pl.BlockSpec((128, rows), lambda i: (i % pairs, 0))
    query_rows = pl.BlockSpec((rows, 128), lambda i: (0, i % pairs))
    stats = pl.BlockSpec((None, 2, rows), lambda i: (i % pairs, 0, 0))
    whole = pl.BlockSpec(memory_space=pltpu.VMEM)
    there = pl.BlockSpec(memory_space=pl.ANY)
    stages = []
    for n, _, wide in early:
        high = views[n].shape[3]
        stages += [
            pltpu.VMEM((depth, 2, high, wide), BF),
            pltpu.VMEM((depth, 2, high, wide), BF),
            pltpu.VMEM((depth, high, wide), BF),
            pltpu.VMEM((depth - 1, high, wide), BF),
            pltpu.VMEM((high, wide), BF),
        ]
    copies = (len(early) + pairs + 1) * (depth + 2) + 1
    return pl.pallas_call(
        functools.partial(back_kernel, depth, pairs, early, chunk),
        grid=(2 * pairs,),
        in_specs=[
            key_rows,
            pl.BlockSpec((128, rows), lambda i: (i % pairs, 1 - i // pairs)),
            key_rows,
            query_cols,
            query_rows,
            query_cols,
            query_rows,
            pl.BlockSpec((rows, 128), lambda i: (1 - i // pairs, 0)),
            stats,
            stats,
            whole,
            pl.BlockSpec((width, rows), lambda i: (0, 1 - i // pairs)),
            there,
            whole,
        ]
        + [there] * len(views),
        out_specs=[whole] * (2 + len(views)) + [there],
        out_shape=[jax.ShapeDtypeStruct((share, 3 * width), F32)]
        + [jax.ShapeDtypeStruct(s.shape[3:], F32) for s in views]
        + [jax.ShapeDtypeStruct(sums.shape, F32), jax.ShapeDtypeStruct((rows, width), F32)],
        scratch_shapes=stages
        + [
            pltpu.VMEM((pairs, depth, 2, 2, share, 384), BF),
            pltpu.VMEM((pairs, depth, 2, share, 384), BF),
            pltpu.VMEM((pairs, depth, share, 384), BF),
            pltpu.VMEM((pairs, depth - 1, share, 384), BF),
            pltpu.VMEM((pairs, share, 384), BF),
            pltpu.VMEM((rows, width), F32),
            pltpu.VMEM((pairs, 128, rows), F32),
            pltpu.VMEM((rows, width), BF),
            pltpu.VMEM((rows, width), BF),
            pltpu.VMEM((rows, 3 * width), BF),
            pltpu.VMEM((4,) + sums.shape, F32),
            pltpu.VMEM(sums.shape, F32),
            pltpu.VMEM(sums.shape, F32),
            pltpu.VMEM((depth - 1,) + sums.shape, F32),
            pltpu.VMEM(sums.shape, F32),
            pltpu.SemaphoreType.DMA((copies,)),
            pltpu.SemaphoreType.DMA((copies,)),
            pltpu.SemaphoreType.DMA((len(early) + 5,)),
        ],
        compiler_params=pltpu.CompilerParams(vmem_limit_bytes=61 << 20, collective_id=1, has_side_effects=True),
        cost_estimate=pl.CostEstimate(
            flops=40 * rows * keys * width, transcendentals=rows * keys * 2 * pairs, bytes_accessed=2 * width * 20 * rows
        ),
        name="back_reduce",
    )(k, kt, v, qt, q, gt, g, aug, lse, delta, full_qkv, xt, grad_one, sums, *views)


class Spread:
    def __init__(self, links, base, share, full, local):
        self.links, self.share, self.full = links, share, full
        self.send_base = base * (4 * links.depth + 2)
        self.recv_base = base * (4 * links.depth + 2)
        k = links
        self.local = pltpu.make_async_copy(share, full.at[k.far, k.near, k.core], local)

    def index(self, far, near, core):
        return self.recv_base + (far * 2 + near) * 2 + core

    def copy(self, src, slot, send, peer):
        return self.links.copy_two(src, self.full.at[slot], self.send_base + send, self.index(*slot), peer)

    def source(self, k):
        return self.links.ring[k]

    def far_copy(self, k):
        links = self.links
        return self.copy(self.share, (links.far, links.near, links.core), k - 1, links.peer(far=links.ring[k]))

    def near_copy(self, k):
        links = self.links
        slot = (self.source(k), links.near, links.core)
        return self.copy(self.share if k == 0 else self.full.at[slot], slot, links.depth - 1 + k, links.to_near())

    def core_copy(self, k, across):
        links = self.links
        slot = (self.source(k), 1 - links.near if across else links.near, links.core)
        src = self.share if k == 0 and not across else self.full.at[slot]
        return self.copy(src, slot, 2 * links.depth - 1 + 2 * k + across, links.to_core())

    def arrive(self, far, near, core):
        self.copy(self.share, (far, near, core), 0, self.links.to_core()).wait_recv()

    def begin(self):
        self.local.start()
        for k in range(1, self.links.depth):
            self.far_copy(k).start()
        self.near_copy(0).start()
        self.core_copy(0, 0).start()

    def pass_far(self):
        links = self.links
        for k in range(1, links.depth):
            self.arrive(self.source(k), links.near, links.core)
            self.near_copy(k).start()
            self.core_copy(k, 0).start()

    def pass_near(self):
        links = self.links
        for k in range(links.depth):
            self.arrive(self.source(k), 1 - links.near, links.core)
            self.core_copy(k, 1).start()

    def complete(self):
        links = self.links
        for k in range(links.depth):
            for near in range(2):
                self.arrive(self.source(k), near, 1 - links.core)
        self.local.wait()

    def finish(self):
        for k in range(self.links.depth):
            if k:
                self.far_copy(k).wait_send()
            self.near_copy(k).wait_send()
            self.core_copy(k, 0).wait_send()
            self.core_copy(k, 1).wait_send()


class SpreadHalf(Spread):
    def __init__(self, links, base, share, full, local):
        high = share.shape[0] // 2
        mine, others = pl.ds(links.seq * high, high), pl.ds((1 - links.seq) * high, high)
        super().__init__(links, base, share.at[mine], full.at[:, :, :, mine], local)
        self.mine = full.at[:, :, links.core, mine]
        self.others = full.at[:, :, links.core, others]
        self.across = full.at[:, :, 1 - links.core, others]

    def seq_copy(self):
        n = self.recv_base + 4 * self.links.depth
        return self.links.copy_two(self.mine, self.mine, n, n, self.links.to_seq())

    def seq_arrive(self):
        n = self.recv_base + 4 * self.links.depth
        self.links.copy_two(self.others, self.others, n, n, self.links.to_seq()).wait_recv()

    def other_copy(self):
        n = self.recv_base + 4 * self.links.depth + 1
        return self.links.copy_two(self.others, self.others, n, n, self.links.to_core())

    def pass_near(self):
        super().pass_near()
        self.local.wait()
        self.seq_copy().start()

    def pass_seq(self):
        self.seq_arrive()
        self.other_copy().start()

    def complete(self):
        links = self.links
        for k in range(links.depth):
            for near in range(2):
                self.arrive(self.source(k), near, 1 - links.core)
        n = self.recv_base + 4 * links.depth + 1
        links.copy_two(self.across, self.across, n, n, links.to_core()).wait_recv()

    def finish(self):
        super().finish()
        self.seq_copy().wait_send()
        self.other_copy().wait_send()


ROWS = (0, 2, 3, 7, 8, 9, 10, 11)


def forward_kernel(depth, pairs, later, chunk, *refs):
    x_ref, aug_ref, qkv_share = refs[:3]
    vec_refs = refs[3 : 3 + len(ROWS)]
    refs = refs[3 + len(ROWS) :]
    n_src = 1 + max(piece[0] for piece in later)
    shares = refs[:n_src]
    refs = refs[n_src:]
    q_ref, qt_ref, k_ref, kt_ref, v_ref, o_ref, lse_ref, xt_ref, sums_ref, qkv_out = refs[:10]
    fulls = refs[10 : 10 + n_src]
    w_own, w_all, v_all, v_own, other, vt, bias, qt_all, held, stats, send_sem, recv_sem, local_sem = refs[10 + n_src :]
    step = pl.program_id(0)
    g = step % pairs
    rows, width = x_ref.shape
    links = Links(depth, send_sem, recv_sem)
    groups = [Spread(links, n, w_own.at[n], w_all.at[n], local_sem.at[n]) for n in range(GROUPS)]
    vectors = Spread(links, GROUPS, v_own, v_all, local_sem.at[GROUPS])
    base = GROUPS + 1
    pieces = []
    for n, (source, start, wide, halved) in enumerate(later):
        part = pl.ds(start, wide)
        kind = SpreadHalf if halved else Spread
        pieces.append(kind(links, base + n, shares[source].at[:, part], fulls[source].at[:, :, :, :, part], local_sem.at[base + n]))
    spare = (base + len(later)) * (4 * depth + 2)
    tokens_copy = links.copy_two(x_ref, other, spare, spare, links.to_seq())
    span = width // GROUPS
    in_copies, out_copies = [], []
    for n in range(GROUPS):
        for third in range(3):
            mine, theirs = pl.ds(third * span, span), pl.ds(third * width + n * span, span)
            index = base + len(later) + 3 * n + third
            in_copies.append(pltpu.make_async_copy(qkv_share.at[:, theirs], w_own.at[n, :, mine], local_sem.at[index]))
            out_copies.append(
                pltpu.make_async_copy(w_all.at[n, :, :, :, :, mine], qkv_out.at[:, :, :, :, theirs], local_sem.at[index])
            )

    @pl.when(step == 0)
    def _():
        for copy in in_copies:
            copy.start()
        v_own[...] = jnp.zeros_like(v_own)
        for n, ref in enumerate(vec_refs):
            v_own[n : n + 1, 0 : ref.shape[1]] = ref[...]
        links.barrier()
        for copy in in_copies[:3]:
            copy.wait()
        groups[0].begin()
        tokens_copy.start()
        vectors.begin()
        for copy in in_copies[3:]:
            copy.wait()
        for n in range(1, GROUPS):
            groups[n].begin()
        xt_ref[:, 0:rows] = x_ref[...].T
        groups[0].pass_far()
        vectors.pass_far()
        groups[0].pass_near()
        vectors.pass_near()
        groups[1].pass_far()
        vectors.complete()
        target = lax.broadcasted_iota(jnp.int32, (16, width), 0)
        total = jnp.zeros((16, width), F32)
        blank = jnp.zeros((8, width - v_own.shape[1]), F32)
        for place in range(4 * depth):
            values = v_all[place // 4, place // 2 % 2, place % 2].astype(F32)
            values = jnp.concatenate([values, blank], axis=1)
            fitted = {}
            for size in VECTOR_UNITS:
                shift = place % (4 * depth // size) * (width * size // (4 * depth))
                fitted[size] = pltpu.roll(values, shift, 1) if shift else values
            for n, (first, size) in enumerate(zip(ROWS, VECTOR_SIZES)):
                row = first + place // (4 * depth // size)
                total = total + jnp.where(target == row, fitted[size][n : n + 1, :], 0.0)
        sums_ref[...] = total
        for n in range(pairs):
            bias[n, 0:2, :] = total[0:2, n * 128 : n * 128 + 128]
        groups[0].complete()

    def at(when, *actions):
        @pl.when(step == when)
        def _():
            for action in actions:
                action()

    group, place = g * GROUPS // pairs, g % (pairs // GROUPS)

    def weight(third):
        column = pl.ds(pl.multiple_of(third * span + place * 128, 128), 128)
        return w_all[group, :, :, :, :, column].reshape(width, 128)

    def project(tokens):
        kv = dot_nn(tokens[...], jnp.concatenate([weight(1), weight(2)], axis=1))
        k = kv[:, 0:128]
        v = kv[:, 128:256] + bias[g, 1:2, :]
        k_ref[...] = k.astype(BF)
        kt_ref[...] = k.T.astype(BF)
        v_ref[...] = v.astype(BF)
        vt[...] = v.T.astype(BF)

    here = pl.ds(pl.multiple_of(g * 128, 128), 128)

    @pl.when(step < pairs)
    def _():
        q = dot_nn(x_ref[...], weight(0)) + bias[g, 0:1, :]
        q_ref[...] = q.astype(BF)
        turned = q.T.astype(BF)
        qt_ref[...] = turned
        qt_all[here, :] = turned
        project(x_ref)
        held[g] = jnp.zeros(held.shape[1:], F32)
        stats[g, 0:2, :] = jnp.full((2, rows), -jnp.inf, F32)
        stats[g, 2:4, :] = jnp.zeros((2, rows), F32)

    @pl.when(step >= pairs)
    def _():
        @pl.when(step == pairs)
        def _():
            tokens_copy.wait_recv()
            xt_ref[:, rows : 2 * rows] = other[...].T

        project(other)

    row = lax.broadcasted_iota(jnp.int32, (16, rows), 0)
    tail = jnp.where(row == 0, 1.0, 0.0).astype(BF)
    none = jnp.zeros((HD, rows), BF)
    rest = jnp.zeros((112, rows), BF)
    qt = qt_all[here, :]
    queries = [
        jnp.concatenate([qt[0:HD, :], none, tail, rest], axis=0),
        jnp.concatenate([none, qt[HD : 2 * HD, :], tail, rest], axis=0),
    ]
    largest = [stats[g, h : h + 1, :] for h in range(2)]
    total = [stats[g, 2 + h : 3 + h, :] for h in range(2)]
    context = [held[g, HD * h : HD * h + HD, :] for h in range(2)]

    def score(c, h):
        part = slice(c * chunk, (c + 1) * chunk)
        return dot_nn(jnp.concatenate([k_ref[part, :], aug_ref[part, :]], axis=1), queries[h])

    ahead = [score(0, h) for h in range(2)]
    chunks = rows // chunk
    for c in range(chunks):
        part = slice(c * chunk, (c + 1) * chunk)
        for h in range(2):
            scores = ahead[h]
            if c + 1 < chunks:
                ahead[h] = score(c + 1, h)
            top = jnp.maximum(largest[h], jnp.max(scores, axis=0, keepdims=True))
            fade = jnp.exp2((largest[h] - top) * EXP2_SCALE)
            weights = jnp.exp2((scores - top) * EXP2_SCALE)
            largest[h] = top
            total[h] = total[h] * fade + total_rows(weights)
            context[h] = context[h] * fade + dot_nn(vt[HD * h : HD * h + HD, part], weights.astype(BF))

    @pl.when(step < pairs)
    def _():
        for h in range(2):
            stats[g, h : h + 1, :] = largest[h]
            stats[g, 2 + h : 3 + h, :] = total[h]
            held[g, HD * h : HD * h + HD, :] = context[h]

    @pl.when(step >= pairs)
    def _():
        for h in range(2):
            o_ref[HD * h : HD * h + HD, :] = (context[h] / total[h]).astype(BF)
            lse_ref[h : h + 1, :] = largest[h] * SCALE + jnp.log(total[h])

    at(0, groups[2].pass_far, *[piece.begin for piece in pieces])
    at(1, groups[1].pass_near, groups[1].complete)
    at(3, groups[2].pass_near, groups[2].complete, pieces[0].pass_far)
    at(4, pieces[1].pass_far)
    at(5, pieces[2].pass_far)
    at(6, pieces[0].pass_near)
    at(7, pieces[1].pass_near, pieces[3].pass_far)
    at(8, pieces[2].pass_near)
    at(9, pieces[4].pass_far)
    at(10, pieces[3].pass_near, pieces[5].pass_far)

    @pl.when(step == 2 * pairs - 1)
    def _():
        for copy in out_copies:
            copy.start()
        pieces[4].pass_near()
        pieces[5].pass_near()
        for piece in pieces:
            if isinstance(piece, SpreadHalf):
                piece.pass_seq()
        for piece in pieces:
            piece.complete()
        for piece in groups + [vectors] + pieces:
            piece.finish()
        tokens_copy.wait_send()
        for copy in out_copies:
            copy.wait()


GROUPS = 3
VECTOR_SIZES = (2, 1, 4, 1, 1, 1, 1, 1)
VECTOR_UNITS = (1, 2, 4)
LATER = ((2, 0, 2, 1), (2, 1, 2, 1), (0, 0, 1, 0), (1, 0, 3, 0), (1, 1, 3, 0), (1, 2, 3, 0))


def forward(x, aug, vectors, w_qkv, w_out, w_up, w_down, depth):
    rows, width = x.shape
    pairs = width // 128
    keys = 2 * rows
    chunk = min(512, rows)
    shares = (w_out, w_up, w_down)
    later = [(n, part * (shares[n].shape[1] // of), shares[n].shape[1] // of, halved) for n, part, of, halved in LATER]
    whole = pl.BlockSpec(memory_space=pltpu.VMEM)
    there = pl.BlockSpec(memory_space=pl.ANY)
    half_rows = pl.BlockSpec((rows, 128), lambda i: (i // pairs, i % pairs))
    fulls = [(depth, 2, 2) + s.shape for s in (w_qkv,) + shares]
    low = lambda *shape: jax.ShapeDtypeStruct(shape, BF)
    copies = (1 + GROUPS + len(later)) * (4 * depth + 2) + 1
    return pl.pallas_call(
        functools.partial(forward_kernel, depth, pairs, later, chunk),
        grid=(2 * pairs,),
        in_specs=[whole, pl.BlockSpec((rows, 128), lambda i: (i // pairs, 0)), there] + [whole] * len(vectors) + [there] * 3,
        out_specs=[
            pl.BlockSpec((rows, 128), lambda i: (0, jnp.minimum(i, pairs - 1))),
            pl.BlockSpec((128, rows), lambda i: (jnp.minimum(i, pairs - 1), 0)),
            half_rows,
            pl.BlockSpec((128, rows), lambda i: (i % pairs, i // pairs)),
            half_rows,
            pl.BlockSpec((128, rows), lambda i: (jnp.maximum(i - pairs, 0), 0)),
            pl.BlockSpec((None, 2, rows), lambda i: (jnp.maximum(i - pairs, 0), 0, 0)),
            whole,
            whole,
            there,
            there,
            there,
            there,
        ],
        out_shape=[
            low(rows, width),
            low(width, rows),
            low(keys, width),
            low(width, keys),
            low(keys, width),
            low(width, rows),
            jax.ShapeDtypeStruct((pairs, 2, rows), F32),
            low(width, keys),
            jax.ShapeDtypeStruct((16, width), F32),
        ]
        + [low(*f) for f in fulls],
        scratch_shapes=[
            pltpu.VMEM((GROUPS, w_qkv.shape[0], 3 * width // GROUPS), BF),
            pltpu.VMEM((GROUPS, depth, 2, 2, w_qkv.shape[0], 3 * width // GROUPS), BF),
            pltpu.VMEM((depth, 2, 2, 8, 256), BF),
            pltpu.VMEM((8, 256), BF),
            pltpu.VMEM((rows, width), BF),
            pltpu.VMEM((128, rows), BF),
            pltpu.VMEM((pairs, 8, 128), F32),
            pltpu.VMEM((width, rows), BF),
            pltpu.VMEM((pairs, 128, rows), F32),
            pltpu.VMEM((pairs, 8, rows), F32),
            pltpu.SemaphoreType.DMA((copies,)),
            pltpu.SemaphoreType.DMA((copies,)),
            pltpu.SemaphoreType.DMA((1 + 4 * GROUPS + len(later),)),
        ],
        compiler_params=pltpu.CompilerParams(vmem_limit_bytes=58 << 20, collective_id=2, has_side_effects=True),
        cost_estimate=pl.CostEstimate(
            flops=16 * rows * keys * width, transcendentals=rows * keys * 2 * pairs, bytes_accessed=2 * width * 10 * keys
        ),
        name="forward",
    )(x, aug, w_qkv, *[v.reshape(1, -1) for v in vectors], *shares)


def back_plain(k, kt, v, qt, q, grad_context, aug, lse, delta, full_qkv, both, grad_one, grads, sources, sizes):
    width = k.shape[1]
    rows = q.shape[0]

    def scatter(value):
        return lax.psum_scatter(value.astype(BF), "dp", scatter_dimension=0, tiled=True)

    def over_seq(value):
        value = value.astype(BF)
        return value.astype(F32) + lax.ppermute(value, "seq", [(0, 1), (1, 0)]).astype(F32)

    share_wout, share_wup, share_wdown = [scatter(s) for s in sources]
    dqt, dk, dv = attend_back(k, kt, v, qt, q, grad_context.T, grad_context, aug, lse, delta)
    dq = dqt.T
    partial = dot_nt(jnp.concatenate([dk[rows:], dv[rows:]], axis=1), full_qkv[:, width:])
    partial = lax.ppermute(partial.astype(BF), "seq", [(0, 1), (1, 0)])
    own = jnp.concatenate([dq, dk[:rows], dv[:rows]], axis=1)
    grad_wq, grad_wk, grad_wv = dot_tn(both[:rows], dq), dot_tn(both, dk), dot_tn(both, dv)
    grad_inputs = grad_one + dot_nt(own, full_qkv) + partial.astype(F32)
    grads = (jnp.concatenate([column_sum(dq), column_sum(dv)]),) + tuple(grads)
    extra = sum(g.shape[0] for g in grads) // width
    packed = jnp.concatenate([g.reshape(-1, size) for g, size in zip(grads, sizes)], axis=1).reshape(width, extra)
    packed = jnp.pad(packed, ((0, 0), (0, 128 - extra)))
    share_qkv = over_seq(scatter(jnp.concatenate([grad_wq, grad_wk, grad_wv, packed], axis=1)))
    packed = share_qkv[:, 3 * width : 3 * width + extra].reshape(-1)
    out_vectors, start = [], 0
    for size in sizes:
        out_vectors.append(packed[start : start + size])
        start += size
    return share_qkv[:, : 3 * width], over_seq(share_wout), over_seq(share_wup), over_seq(share_wdown), out_vectors, grad_inputs


def normalize(values):
    center = jnp.mean(values, axis=-1, keepdims=True)
    shifted = values - center
    spread = jnp.mean(shifted * shifted, axis=-1, keepdims=True)
    scale = lax.rsqrt(spread + EPS)
    return shifted * scale, scale


def normalize_back(grad, normal, scale):
    mean = jnp.mean(grad, axis=-1, keepdims=True)
    along = jnp.mean(grad * normal, axis=-1, keepdims=True)
    return (grad - mean - normal * along) * scale


def middle_kernel(*refs):
    x_ref, ot_ref, vec_ref, cot_hbm, wout_hbm, wup_hbm, wdown_hbm = refs[:7]
    result_hbm, one_hbm, g_hbm, gt_hbm, delta_ref, sums_ref, gdown_hbm, gup_hbm, gout_hbm = refs[7:16]
    wout, wup, wdown, cot_buf, acts, pres, hiddens, branches, projs, normals, grads, result, turned_buf, stage, sem = refs[16:]
    rows, width = x_ref.shape
    ff = wup.shape[1]
    copies = [
        pltpu.make_async_copy(src, dst, sem.at[n])
        for n, (src, dst) in enumerate(((wout_hbm, wout), (wup_hbm, wup), (wdown_hbm, wdown), (cot_hbm, cot_buf)))
    ]
    for copy in copies:
        copy.start()

    def vector(n):
        return vec_ref[n : n + 1, :]

    ot = ot_ref[...]
    context = ot.T
    copies[0].wait()
    attn = dot_nn(context, wout[...]) + vector(2)
    normal_one, scale_one = normalize(x_ref[...].astype(F32) + attn)
    normals[...] = normal_one
    low = (normal_one * vector(8) + vector(9)).astype(BF)
    hiddens[...] = low
    copies[1].wait()
    copies[2].wait()
    grads[...] = normals[...] * vector(8) + (vector(9) + vector(7))
    def up_and_down(c, _):
        part = pl.ds(pl.multiple_of(c * width, width), width)
        pre = dot_nn(hiddens[...], wup[:, part]) + vec_ref[pl.ds(3 + c, 1), :]
        bell = 0.5 * (1.0 + lax.erf(pre * 0.7071067811865476))
        act = (pre * bell).astype(BF)
        pres[:, part] = (bell + pre * (jnp.exp(-0.5 * pre * pre) * 0.3989422804014327)).astype(BF)
        acts[:, part] = act
        grads[...] += dot_nn(act, wdown[part, :])
        return 0

    lax.fori_loop(0, ff // width, up_and_down, 0)
    normal_two, scale_two = normalize(grads[...])
    result[...] = (normal_two * vector(10) + vector(11)).astype(BF)
    out_result = pltpu.make_async_copy(result, result_hbm, sem.at[4])
    out_result.start()
    copies[3].wait()
    cot = cot_buf[...].astype(F32)
    sums_ref[...] = jnp.zeros_like(sums_ref)
    sums_ref[10:11, :] = total_rows(cot * normal_two)
    sums_ref[11:12, :] = total_rows(cot)
    grad_two = normalize_back(cot * vector(10), normal_two, scale_two)
    grads[...] = grad_two
    branch = grad_two.astype(BF)
    branches[...] = branch
    sums_ref[7:8, :] = total_rows(branch.astype(F32))
    def back_down_and_up(c, _):
        part = pl.ds(pl.multiple_of(c * width, width), width)
        grad_pre = (dot_nt(branches[...], wdown[part, :]) * pres[:, part].astype(F32)).astype(BF)
        pres[:, part] = grad_pre
        sums_ref[pl.ds(3 + c, 1), :] = total_rows(grad_pre.astype(F32))
        grads[...] += dot_nt(grad_pre, wup[:, part])
        return 0

    lax.fori_loop(0, ff // width, back_down_and_up, 0)
    grad_hidden = grads[...]
    normal_one = normals[...]
    sums_ref[8:9, :] = total_rows(grad_hidden * normal_one)
    sums_ref[9:10, :] = total_rows(grad_hidden)
    grad_one = normalize_back(grad_hidden * vector(8), normal_one, scale_one)
    grads[...] = grad_one
    out_one = pltpu.make_async_copy(grads, one_hbm, sem.at[5])
    out_one.start()
    proj = grad_one.astype(BF)
    projs[...] = proj
    sums_ref[2:3, :] = total_rows(proj.astype(F32))
    grad_context = dot_nt(projs[...], wout[...])
    out_result.wait()
    result[...] = grad_context.astype(BF)
    out_g = pltpu.make_async_copy(result, g_hbm, sem.at[4])
    out_g.start()
    turned = grad_context.T.astype(BF)
    turned_buf[...] = turned
    out_gt = pltpu.make_async_copy(turned_buf, gt_hbm, sem.at[6])
    out_gt.start()
    each = (turned.astype(F32) * ot.astype(F32)).reshape(width // HD, HD, rows)
    delta_ref[...] = jnp.sum(each, axis=1).reshape(delta_ref.shape)

    def put(n, value, target):
        slot = n % 2
        copy = pltpu.make_async_copy(stage.at[slot], target, sem.at[7 + slot])

        @pl.when(n >= 2)
        def _():
            copy.wait()

        stage[slot] = value.astype(BF)
        copy.start()

    def down_weights(c, _):
        part = pl.ds(pl.multiple_of(c * width, width), width)
        put(c, dot_nn(acts[:, part].T, branches[...]), gdown_hbm.at[part])
        return 0

    def up_weights(c, _):
        part = pl.ds(pl.multiple_of(c * width, width), width)
        put(c + ff // width, dot_nn(turned_buf[...], pres[:, part]), gup_hbm.at[:, part])
        return 0

    lax.fori_loop(0, ff // width, down_weights, 0)
    out_gt.wait()
    turned_buf[...] = hiddens[...].T
    lax.fori_loop(0, ff // width, up_weights, 0)
    put(jnp.int32(2 * (ff // width)), dot_nn(ot_ref[...], projs[...]), gout_hbm)
    for slot in range(2):
        pltpu.make_async_copy(stage.at[slot], gout_hbm, sem.at[7 + slot]).wait()
    out_one.wait()
    out_g.wait()


def middle(x, cotangent, context_t, vectors, w_out, w_up, w_down):
    rows, width = x.shape
    ff = w_up.shape[1]
    pairs = width // 128
    whole = pl.BlockSpec(memory_space=pltpu.VMEM)
    there = pl.BlockSpec(memory_space=pl.ANY)
    shape = jax.ShapeDtypeStruct
    return pl.pallas_call(
        middle_kernel,
        in_specs=[whole, whole, whole, there, there, there, there],
        out_specs=[there, there, there, there, whole, whole, there, there, there],
        out_shape=[
            shape((rows, width), BF),
            shape((rows, width), F32),
            shape((rows, width), BF),
            shape((width, rows), BF),
            shape((pairs, 2, rows), F32),
            shape((16, width), F32),
            shape((ff, width), BF),
            shape((width, ff), BF),
            shape((width, width), BF),
        ],
        scratch_shapes=[
            pltpu.VMEM((width, width), BF),
            pltpu.VMEM((width, ff), BF),
            pltpu.VMEM((ff, width), BF),
            pltpu.VMEM((rows, width), BF),
            pltpu.VMEM((rows, ff), BF),
            pltpu.VMEM((rows, ff), BF),
            pltpu.VMEM((rows, width), BF),
            pltpu.VMEM((rows, width), BF),
            pltpu.VMEM((rows, width), BF),
            pltpu.VMEM((rows, width), F32),
            pltpu.VMEM((rows, width), F32),
            pltpu.VMEM((rows, width), BF),
            pltpu.VMEM((width, rows), BF),
            pltpu.VMEM((2, width, width), BF),
            pltpu.SemaphoreType.DMA((9,)),
        ],
        compiler_params=pltpu.CompilerParams(vmem_limit_bytes=58 << 20),
        cost_estimate=pl.CostEstimate(
            flops=6 * rows * width * (width + 2 * ff), transcendentals=2 * rows * ff, bytes_accessed=8 * width * (width + 2 * ff)
        ),
        name="middle",
    )(x, context_t, vectors, cotangent, w_out, w_up, w_down)


def finish_kernel(parts, *refs):
    count = (len(refs) - 2 - len(ROWS)) // 2
    sums_ref, sources, targets, small = refs[0], refs[1 : 1 + count], refs[1 + count : 1 + 2 * count], refs[1 + 2 * count : -1]
    targets[0][...] = sources[0][...]
    pairs = enumerate(zip(sources[1:], targets[1:]))
    copies = [pltpu.make_async_copy(source, target, refs[-1].at[n]) for n, (source, target) in pairs]

    @pl.when(pl.program_id(0) == pl.num_programs(0) - 1)
    def _():
        for copy in copies:
            copy.wait()

    @pl.when(pl.program_id(0) == 0)
    def _():
        for copy in copies:
            copy.start()
        width = sums_ref.shape[1]
        place = lax.axis_index("dp")
        picked = []
        for base, size in zip(ROWS, VECTOR_SIZES):
            picked.append(sums_ref[pl.ds(base + place // (parts // size), 1), :])
        picked = jnp.concatenate(picked, axis=0)
        for size in VECTOR_UNITS:
            shift = (place % (parts // size)) * (width * size // parts)
            turned = pltpu.roll(picked, (width - shift) % width, 1)
            for n in range(len(ROWS)):
                if VECTOR_SIZES[n] == size:
                    small[n][...] = turned[n : n + 1, 0 : small[n].shape[1]]


def finish(sums, tokens, shares, parts):
    whole = pl.BlockSpec(memory_space=pltpu.VMEM)
    width = sums.shape[1]
    rows = tokens.shape[0] // 4
    block = pl.BlockSpec((rows, width), lambda i: (i, 0))
    shapes = [jax.ShapeDtypeStruct(x.shape, x.dtype) for x in (tokens,) + shares]
    small = [jax.ShapeDtypeStruct((1, width * size // parts), F32) for size in VECTOR_SIZES]
    out = pl.pallas_call(
        functools.partial(finish_kernel, parts),
        grid=(4,),
        in_specs=[whole, block] + [pl.BlockSpec(memory_space=pl.ANY)] * len(shares),
        out_specs=[block] + [whole] * (len(shares) + len(small)),
        out_shape=shapes + small,
        scratch_shapes=[pltpu.SemaphoreType.DMA((len(shares),))],
        compiler_params=pltpu.CompilerParams(vmem_limit_bytes=58 << 20),
        name="finish",
    )(sums, tokens, *shares)
    count = 1 + len(shares)
    return out[:count], [v.reshape(-1) for v in out[count:]]


def forward_plain(x, aug, vectors, w_qkv):
    width = x.shape[1]
    other = lax.ppermute(x, "seq", [(0, 1), (1, 0)])
    sizes = [v.shape[0] for v in vectors]
    share = w_qkv.shape[0]
    extra = sum(sizes) // share
    beside = jnp.concatenate(vectors).reshape(share, extra)
    beside = jnp.concatenate([w_qkv, jnp.pad(beside, ((0, 0), (0, 128 - extra)))], axis=1)
    full_qkv = lax.all_gather(beside, "dp", axis=0, tiled=True)
    full_vectors = full_qkv[:, 3 * width : 3 * width + extra].reshape(-1, sum(sizes)).astype(F32)
    full_qkv = full_qkv[:, : 3 * width]
    full, start = [], 0
    for size in sizes:
        full.append(full_vectors[:, start : start + size].reshape(-1))
        start += size
    both = jnp.concatenate([x, other], axis=0)
    q = (dot_nn(x, full_qkv[:, :width]) + full[0][:width]).astype(BF)
    k = dot_nn(both, full_qkv[:, width : 2 * width]).astype(BF)
    v = (dot_nn(both, full_qkv[:, 2 * width :]) + full[0][width:]).astype(BF)
    qt, kt, vt = q.T, k.T, v.T
    context_t, lse = attend(k, qt, vt, aug)
    return q, qt, k, kt, v, both, context_t, lse, full_qkv, full[1:]


def plain(x, aug, vectors, w_qkv, w_out, w_up, w_down, upstream):
    rows, width = x.shape
    sizes = [v.shape[0] for v in vectors]
    q, qt, k, kt, v, both, context_t, lse, full_qkv, full = forward_plain(x, aug, vectors, w_qkv)
    full_bout, full_bup, full_bdown, gain_one, shift_one, gain_two, shift_two = full
    full_wout, full_wup, full_wdown = [lax.all_gather(w, "dp", axis=0, tiled=True) for w in (w_out, w_up, w_down)]
    context = context_t.T
    attn_branch = dot_nn(context, full_wout) + full_bout
    resid_one = x.astype(F32) + attn_branch
    hidden_one, first_pull = jax.vjp(layer_norm, resid_one, gain_one, shift_one)
    hidden_low = hidden_one.astype(BF)
    pre_act = dot_nn(hidden_low, full_wup) + full_bup
    activated, gelu_pull = jax.vjp(gelu_exact, pre_act)
    act_low = activated.astype(BF)
    ffn_branch = dot_nn(act_low, full_wdown) + full_bdown
    resid_two = hidden_one + ffn_branch
    output, second_pull = jax.vjp(layer_norm, resid_two, gain_two, shift_two)
    grad_two, grad_gain_two, grad_shift_two = second_pull(upstream.astype(F32))
    grad_branch = grad_two.astype(BF)
    grad_wdown = dot_tn(act_low, grad_branch)
    grad_bdown = column_sum(grad_branch)
    (grad_pre,) = gelu_pull(dot_nt(grad_branch, full_wdown))
    grad_pre_low = grad_pre.astype(BF)
    grad_wup = dot_tn(hidden_low, grad_pre_low)
    grad_bup = column_sum(grad_pre_low)
    grad_hidden = grad_two + dot_nt(grad_pre_low, full_wup)
    grad_one, grad_gain_one, grad_shift_one = first_pull(grad_hidden)
    grad_proj = grad_one.astype(BF)
    grad_wout = dot_tn(context, grad_proj)
    grad_bout = column_sum(grad_proj)
    grad_context = dot_nt(grad_proj, full_wout).astype(BF)
    delta = jnp.sum((grad_context.astype(F32) * context.astype(F32)).reshape(rows, HEADS, HD), axis=-1)
    delta = delta.T.reshape(HEADS // 2, 2, rows)

    grads = (grad_bout, grad_bup, grad_bdown, grad_gain_one, grad_shift_one, grad_gain_two, grad_shift_two)
    share_qkv, share_out, share_up, share_down, out_vectors, grad_inputs = back_plain(
        k, kt, v, qt, q, grad_context, aug, lse, delta, full_qkv, both, grad_one, grads, (grad_wout, grad_wup, grad_wdown), sizes
    )
    return output.astype(BF), grad_inputs, share_qkv, share_out, share_up, share_down, out_vectors


def local(
    tokens,
    lengths,
    w_qkv,
    bias_qv,
    w_out,
    bias_out,
    w_up,
    bias_up,
    w_down,
    bias_down,
    gain_attn,
    shift_attn,
    gain_ffn,
    shift_ffn,
    cotangent,
):
    x = tokens[0]
    rows, width = x.shape
    ff = w_up.shape[1]
    me = lax.axis_index("seq")
    parts = lax.axis_size("dp")
    aligned = parts % 4 == 0 and width % (16 * parts) == 0 and ff % (16 * parts) == 0
    vectors = (bias_qv, bias_out, bias_up, bias_down, gain_attn, shift_attn, gain_ffn, shift_ffn)
    sizes = [v.shape[0] for v in vectors]
    aligned = aligned and tuple(s * parts for s in sizes) == tuple(n * width for n in VECTOR_SIZES) and parts == 16

    slot = jnp.arange(2 * rows)
    slot = jnp.where(slot < rows, me * rows + slot, (1 - me) * rows + slot - rows)
    lane = jnp.arange(128)
    masked = jnp.where(slot < lengths[0], 0.0, MASK)
    aug = jnp.where(lane[None] == 0, masked[:, None], jnp.where(lane[None] < 4, -1.0, 0.0)).astype(BF)

    if aligned:
        q, qt, k, kt, v, context_t, lse, xt, summed, full_qkv, full_wout, full_wup, full_wdown = forward(
            x, aug, vectors, w_qkv, w_out, w_up, w_down, parts // 4
        )
        full_qkv = full_qkv.reshape(width, 3 * width)
        output, grad_one, grad_context, grad_context_t, delta, sums, grad_wdown, grad_wup, grad_wout = middle(
            x, cotangent[0], context_t, summed, full_wout.reshape(width, width), full_wup.reshape(width, ff), full_wdown.reshape(ff, width)
        )
        sources = (grad_wdown, grad_wup, grad_wout)
        share_qkv, share_down, share_up, share_out, sums, grad_inputs = back_reduce(
            k, kt, v, qt, q, grad_context_t, grad_context, aug, lse, delta, full_qkv, xt, grad_one, sums, sources, parts // 4
        )
        large, out_vectors = finish(sums, grad_inputs, (share_qkv, share_out, share_up, share_down), parts)
        grad_inputs, share_qkv, share_out, share_up, share_down = large
    else:
        output, grad_inputs, share_qkv, share_out, share_up, share_down, out_vectors = plain(
            x, aug, vectors, w_qkv, w_out, w_up, w_down, cotangent[0]
        )
    s_bqv, s_bout, s_bup, s_bdown, s_gain_one, s_shift_one, s_gain_two, s_shift_two = out_vectors
    return (
        output[None],
        grad_inputs[None],
        share_qkv,
        s_bqv,
        share_out,
        s_bout,
        share_up,
        s_bup,
        share_down,
        s_bdown,
        s_gain_one,
        s_shift_one,
        s_gain_two,
        s_shift_two,
    )


def solution(mesh):
    act, mat, vec = P("dp", "seq", None), P("dp", None), P("dp")
    in_specs = (act, vec, mat, vec, mat, vec, mat, vec, mat, vec, vec, vec, vec, vec, act)
    out_specs = (act, act, mat, vec, mat, vec, mat, vec, mat, vec, vec, vec, vec, vec)
    return jax.shard_map(local, mesh=mesh, in_specs=in_specs, out_specs=out_specs, check_vma=False)
```

```python
import functools

import jax
import jax.numpy as jnp
from jax import lax
from jax.experimental import pallas as pl
from jax.experimental.pallas import tpu as pltpu
from jax.sharding import PartitionSpec as P

HEADS = 12
HD = 64
EPS = 1e-05
BF = jnp.bfloat16
F32 = jnp.float32
SCALE = HD**-0.5
EXP2_SCALE = SCALE * 1.4426950408889634
MASK = -8e9


def dot_nn(a, b):
    return lax.dot_general(a, b, (((1,), (0,)), ((), ())), preferred_element_type=F32)


def dot_nt(a, b):
    return lax.dot_general(a, b, (((1,), (1,)), ((), ())), preferred_element_type=F32)


def dot_tn(a, b):
    return lax.dot_general(a, b, (((0,), (0,)), ((), ())), preferred_element_type=F32)


def layer_norm(values, gain, offset):
    center = jnp.mean(values, axis=-1, keepdims=True)
    shifted = values - center
    spread = jnp.mean(shifted * shifted, axis=-1, keepdims=True)
    return shifted * lax.rsqrt(spread + EPS) * gain + offset


def gelu_exact(values):
    return 0.5 * values * (1.0 + lax.erf(values * 0.7071067811865476))


def column_sum(values):
    return jnp.sum(values.astype(F32), axis=0)


def total_rows(values):
    return jnp.sum(values, axis=0, keepdims=True)


def attend_kernel(chunk, k_ref, qt_ref, vt_ref, aug_ref, o_ref, lse_ref, *scratch):
    keys = k_ref.shape[0]
    queries = qt_ref.shape[1]
    qt = qt_ref[...]
    row = lax.broadcasted_iota(jnp.int32, (128, queries), 0)
    tail = jnp.where(row == 0, 1.0, 0.0).astype(BF)
    for h in range(2):
        held = scratch[h]
        mine = jnp.where((row >= HD * h) & (row < HD * h + HD), qt, 0).astype(BF)
        query = jnp.concatenate([mine, tail], axis=0)
        largest = jnp.full((1, queries), -jnp.inf, F32)
        for c in range(keys // chunk):
            part = slice(c * chunk, (c + 1) * chunk)
            key = jnp.concatenate([k_ref[part, :], aug_ref[part, :]], axis=1)
            scores = dot_nn(key, query)
            held[part, :] = scores
            largest = jnp.maximum(largest, jnp.max(scores, axis=0, keepdims=True))
        total = jnp.zeros((1, queries), F32)
        context = jnp.zeros((HD, queries), F32)
        base = largest * EXP2_SCALE
        for c in range(keys // chunk):
            part = slice(c * chunk, (c + 1) * chunk)
            weight = jnp.exp2(held[part, :] * EXP2_SCALE - base)
            total = total + jnp.sum(weight, axis=0, keepdims=True)
            context = context + dot_nn(vt_ref[HD * h : HD * h + HD, part], weight.astype(BF))
        o_ref[HD * h : HD * h + HD, :] = (context / total).astype(BF)
        lse_ref[h : h + 1, :] = largest * SCALE + jnp.log(total)


def attend(k, qt, vt, aug):
    keys, width = k.shape
    queries = qt.shape[1]
    pairs = width // 128
    block = min(1024, queries)
    chunk = min(256, keys)
    return pl.pallas_call(
        functools.partial(attend_kernel, chunk),
        grid=(pairs, queries // block),
        in_specs=[
            pl.BlockSpec((keys, 128), lambda g, i: (0, g)),
            pl.BlockSpec((128, block), lambda g, i: (g, i)),
            pl.BlockSpec((128, keys), lambda g, i: (g, 0)),
            pl.BlockSpec((keys, 128), lambda g, i: (0, 0)),
        ],
        out_specs=[
            pl.BlockSpec((128, block), lambda g, i: (g, i)),
            pl.BlockSpec((None, 2, block), lambda g, i: (g, 0, i)),
        ],
        out_shape=[
            jax.ShapeDtypeStruct((width, queries), BF),
            jax.ShapeDtypeStruct((pairs, 2, queries), F32),
        ],
        scratch_shapes=[pltpu.VMEM((keys, block), F32)] * 2,
        compiler_params=pltpu.CompilerParams(vmem_limit_bytes=56 << 20),
        cost_estimate=pl.CostEstimate(
            flops=16 * queries * keys * width, transcendentals=queries * keys * 2 * pairs, bytes_accessed=2 * width * (queries + 2 * keys)
        ),
        name="attend",
    )(k, qt, vt, aug)


def three_terms(row, values):
    high = values.astype(BF).astype(F32)
    middle = (values - high).astype(BF).astype(F32)
    low = values - high - middle
    return jnp.where(row == 1, high, 0.0) + jnp.where(row == 2, middle, 0.0) + jnp.where(row == 3, low, 0.0)


def attend_back_kernel(
    chunk, k_ref, kt_ref, v_ref, qt_ref, q_ref, gt_ref, g_ref, aug_ref, lse_ref, delta_ref, dqt_ref, dk_ref, dv_ref, dk_sum, dv_sum
):
    step = pl.program_id(1)
    keys = k_ref.shape[0]
    queries = qt_ref.shape[1]

    @pl.when(step == 0)
    def _():
        dk_sum[...] = jnp.zeros_like(dk_sum)
        dv_sum[...] = jnp.zeros_like(dv_sum)

    qt = qt_ref[...]
    gt = gt_ref[...]
    q = q_ref[...]
    g = g_ref[...]
    row = lax.broadcasted_iota(jnp.int32, (128, queries), 0)
    lane = lax.broadcasted_iota(jnp.int32, (queries, 128), 1)
    query_cols, grad_cols, query_rows, grad_rows = [], [], [], []
    for h in range(2):
        down = (row >= HD * h) & (row < HD * h + HD)
        across = (lane >= HD * h) & (lane < HD * h + HD)
        tail = three_terms(row, lse_ref[h : h + 1, :] * (1.0 / SCALE)) + jnp.where(row == 0, 1.0, 0.0)
        query_cols.append(jnp.concatenate([jnp.where(down, qt, 0).astype(BF), tail.astype(BF)], axis=0))
        tail = three_terms(row, delta_ref[h : h + 1, :])
        grad_cols.append(jnp.concatenate([jnp.where(down, gt, 0).astype(BF), tail.astype(BF)], axis=0))
        query_rows.append(jnp.where(across, q, 0).astype(BF))
        grad_rows.append(jnp.where(across, g, 0).astype(BF))
    query_rows = jnp.concatenate(query_rows, axis=0)
    grad_rows = jnp.concatenate(grad_rows, axis=0)
    dq = [jnp.zeros((HD, queries), F32)] * 2
    for c in range(keys // chunk):
        part = slice(c * chunk, (c + 1) * chunk)
        aug = aug_ref[part, :]
        key = jnp.concatenate([k_ref[part, :], aug], axis=1)
        value = jnp.concatenate([v_ref[part, :], aug], axis=1)
        weights, grads = [], []
        for h in range(2):
            weight = jnp.exp2(dot_nn(key, query_cols[h]) * EXP2_SCALE)
            grad = (weight * dot_nn(value, grad_cols[h])).astype(BF)
            weights.append(weight.astype(BF))
            grads.append(grad)
            dq[h] = dq[h] + dot_nn(kt_ref[HD * h : HD * h + HD, part], grad)
        dv_sum[part, :] += dot_nn(jnp.concatenate(weights, axis=1), grad_rows)
        dk_sum[part, :] += dot_nn(jnp.concatenate(grads, axis=1), query_rows)
    for h in range(2):
        dqt_ref[HD * h : HD * h + HD, :] = (dq[h] * SCALE).astype(BF)

    @pl.when(step == pl.num_programs(1) - 1)
    def _():
        dk_ref[...] = (dk_sum[...] * SCALE).astype(BF)
        dv_ref[...] = dv_sum[...].astype(BF)


def attend_back(k, kt, v, qt, q, gt, g, aug, lse, delta):
    keys, width = k.shape
    queries = qt.shape[1]
    pairs = width // 128
    block = min(1024, queries)
    chunk = min(256, keys)
    key_rows = pl.BlockSpec((keys, 128), lambda g, i: (0, g))
    query_cols = pl.BlockSpec((128, block), lambda g, i: (g, i))
    query_rows = pl.BlockSpec((block, 128), lambda g, i: (i, g))
    stats = pl.BlockSpec((None, 2, block), lambda g, i: (g, 0, i))
    return pl.pallas_call(
        functools.partial(attend_back_kernel, chunk),
        grid=(pairs, queries // block),
        in_specs=[
            key_rows,
            pl.BlockSpec((128, keys), lambda g, i: (g, 0)),
            key_rows,
            query_cols,
            query_rows,
            query_cols,
            query_rows,
            pl.BlockSpec((keys, 128), lambda g, i: (0, 0)),
            stats,
            stats,
        ],
        out_specs=[query_cols, key_rows, key_rows],
        out_shape=[
            jax.ShapeDtypeStruct((width, queries), BF),
            jax.ShapeDtypeStruct((keys, width), BF),
            jax.ShapeDtypeStruct((keys, width), BF),
        ],
        scratch_shapes=[pltpu.VMEM((keys, 128), F32)] * 2,
        compiler_params=pltpu.CompilerParams(vmem_limit_bytes=56 << 20),
        cost_estimate=pl.CostEstimate(
            flops=40 * queries * keys * width, transcendentals=queries * keys * 2 * pairs, bytes_accessed=2 * width * (5 * queries + 5 * keys)
        ),
        name="attend_back",
    )(k, kt, v, qt, q, gt, g, aug, lse, delta)


MESH = pl.DeviceIdType.MESH


class Links:
    def __init__(self, depth, send_sem, recv_sem):
        index = lax.axis_index("dp")
        self.depth = depth
        self.core = index % 2
        self.near = (index // 2) % 2
        self.far = index // 4
        self.seq = lax.axis_index("seq")
        self.ring = [self.far] + [(self.far + k) % depth for k in range(1, depth)]
        if depth == 4:
            orders = ((0, 1, 2, 3), (1, 0, 2, 3), (2, 1, 3, 0), (3, 2, 1, 0))
            for n in range(1, 4):
                self.ring[n] = sum(jnp.where(self.far == place, orders[place][n], 0) for place in range(4))
        self.send_sem, self.recv_sem = send_sem, recv_sem

    def peer(self, core=None, near=None, far=None):
        core = self.core if core is None else core
        near = self.near if near is None else near
        far = self.far if far is None else far
        return {"dp": (far * 2 + near) * 2 + core}

    def to_core(self):
        return self.peer(core=1 - self.core)

    def to_near(self):
        return self.peer(near=1 - self.near)

    def to_far(self, k):
        return self.peer(far=(self.far + k) % self.depth)

    def to_seq(self):
        return {"seq": 1 - self.seq}

    def all_peers(self):
        return [self.to_core(), self.to_near(), self.to_seq()] + [self.to_far(k) for k in range(1, self.depth)]

    def barrier(self):
        semaphore = pltpu.get_barrier_semaphore()
        peers = self.all_peers()
        for peer in peers:
            pl.semaphore_signal(semaphore, inc=1, device_id=peer, device_id_type=MESH)
        pl.semaphore_wait(semaphore, len(peers))

    def copy(self, src, dst, index, peer):
        return self.copy_two(src, dst, index, index, peer)

    def copy_two(self, src, dst, send, recv, peer):
        return pltpu.make_async_remote_copy(
            src_ref=src, dst_ref=dst, send_sem=self.send_sem.at[send], recv_sem=self.recv_sem.at[recv], device_id=peer, device_id_type=MESH
        )


class Piece:
    def __init__(self, links, base, own, from_core, from_near, from_far, from_seq):
        self.links, self.base = links, base
        self.own, self.from_core, self.from_near, self.from_far, self.from_seq = own, from_core, from_near, from_far, from_seq

    def near_copy(self):
        k = self.links
        return k.copy(self.own.at[:, 1 - k.near], self.from_near, self.base + 1, k.to_near())

    def far_copy(self, distance):
        k = self.links
        target = (k.far + distance) % k.depth
        return k.copy(self.own.at[target, k.near], self.from_far.at[distance - 1], self.base + 2 + distance, k.to_far(distance))

    def seq_copy(self):
        k = self.links
        return k.copy(self.own.at[k.far, k.near], self.from_seq, self.base + 2, k.to_seq())

    def send_near(self):
        k = self.links
        for z in range(k.depth):
            total = self.own[z, 1 - k.near].astype(F32) + self.from_core[z, 1 - k.near].astype(F32)
            self.own[z, 1 - k.near] = total.astype(BF)
        self.near_copy().start()

    def send_far(self):
        k = self.links
        self.near_copy().wait_recv()
        for z in range(k.depth):
            total = self.own[z, k.near].astype(F32) + self.from_core[z, k.near].astype(F32) + self.from_near[z].astype(F32)
            self.own[z, k.near] = total.astype(BF)
        for distance in range(1, k.depth):
            self.far_copy(distance).start()

    def send_seq(self):
        k = self.links
        total = self.own[k.far, k.near].astype(F32)
        for distance in range(1, k.depth):
            self.far_copy(distance).wait_recv()
            total = total + self.from_far[distance - 1].astype(F32)
        self.own[k.far, k.near] = total.astype(BF)
        self.seq_copy().start()

    def result(self):
        k = self.links
        self.seq_copy().wait_recv()
        return self.own[k.far, k.near].astype(F32) + self.from_seq[...].astype(F32)

    def finish(self):
        self.near_copy().wait_send()
        for distance in range(1, self.links.depth):
            self.far_copy(distance).wait_send()
        self.seq_copy().wait_send()


def back_kernel(depth, pairs, early, chunk, *refs):
    k_ref, kt_ref, v_ref, qt_ref, q_ref, gt_ref, g_ref, aug_ref, lse_ref, delta_ref, w_ref, xt_ref, one_ref, sums_ref = refs[:14]
    n_src = 1 + max(source for source, _, _ in early)
    sources = refs[14 : 14 + n_src]
    refs = refs[14 + n_src :]
    share_qkv = refs[0]
    shares = refs[1 : 1 + n_src]
    sums_out, tokens_out = refs[1 + n_src : 3 + n_src]
    refs = refs[3 + n_src :]
    stage = [refs[5 * e : 5 * e + 5] for e in range(len(early))]
    refs = refs[5 * len(early) :]
    p_full, p_core, p_near, p_far, p_seq, acc, dq_sum, tok_send, tok_recv, dqkv = refs[:10]
    s_own, s_core, s_near, s_far, s_seq, send_sem, recv_sem, local_sem = refs[10:]

    step = pl.program_id(0)
    last = 2 * pairs - 1
    g = step % pairs
    rows = k_ref.shape[0]
    queries = qt_ref.shape[1]
    width = pairs * 128
    links = Links(depth, send_sem, recv_sem)
    span = depth + 2
    pieces = [Piece(links, e * span, *stage[e]) for e in range(len(early))]
    pair_base = len(early) * span
    sums_base = pair_base + pairs * span

    def pair_piece(index):
        own = p_full.at[index, :, :, links.core]
        return Piece(links, pair_base + index * span, own, p_core.at[index], p_near.at[index], p_far.at[index], p_seq.at[index])

    def pair_core_copy(index):
        return links.copy(p_full.at[index, :, :, 1 - links.core], p_core.at[index], pair_base + index * span, links.to_core())

    def early_core_copy(e):
        source, start, wide = early[e]
        part = sources[source].at[:, :, 1 - links.core, :, pl.ds(start, wide)]
        return links.copy(part, stage[e][1], e * span, links.to_core())

    def early_load(e):
        source, start, wide = early[e]
        part = sources[source].at[:, :, links.core, :, pl.ds(start, wide)]
        return pltpu.make_async_copy(part, stage[e][0], local_sem.at[e])

    one_copy = pltpu.make_async_copy(one_ref, acc, local_sem.at[len(early)])
    tokens_copy = links.copy(tok_send, tok_recv, sums_base + span, links.to_seq())

    def early_begin(e):
        early_core_copy(e).start()
        early_load(e).start()

    def early_near(e):
        early_load(e).wait()
        early_core_copy(e).wait_recv()
        pieces[e].send_near()

    def early_far(e):
        pieces[e].send_far()

    def early_seq(e):
        pieces[e].send_seq()

    def early_done(e):
        source, start, wide = early[e]
        shares[source][:, start : start + wide] = pieces[e].result()

    def pair_near(index):
        pair_core_copy(index).wait_recv()
        pair_piece(index).send_near()

    def pair_done(index):
        value = pair_piece(index).result()
        for third in range(3):
            at = pl.multiple_of((third * pairs + index) * 128, 128)
            share_qkv[:, pl.ds(at, 128)] = value[:, third * 128 : third * 128 + 128]

    @pl.when(step == 0)
    def _():
        links.barrier()
        early_begin(0)
        early_begin(1)
        one_copy.start()
        s_own[0] = sums_ref[...]

    def at(when, *actions):
        @pl.when(step == when)
        def _():
            for action, e in actions:
                action(e)

    lane = lax.broadcasted_iota(jnp.int32, (1, 128), 1)
    row = lax.broadcasted_iota(jnp.int32, (16, queries), 0)
    none = jnp.zeros((HD, queries), BF)
    rest = jnp.zeros((112, queries), BF)
    query_cols, grad_cols, query_rows, grad_rows = [], [], [], []
    for h in range(2):

        def placed(ref):
            half = ref[HD * h : HD * h + HD, :]
            return [half, none] if h == 0 else [none, half]

        tail = three_terms(row, lse_ref[h : h + 1, :] * (1.0 / SCALE)) + jnp.where(row == 0, 1.0, 0.0)
        query_cols.append(jnp.concatenate(placed(qt_ref) + [tail.astype(BF), rest], axis=0))
        tail = three_terms(row, delta_ref[h : h + 1, :])
        grad_cols.append(jnp.concatenate(placed(gt_ref) + [tail.astype(BF), rest], axis=0))
        mine = jnp.where((lane >= HD * h) & (lane < HD * h + HD), 1.0, 0.0).astype(BF)
        query_rows.append(q_ref[...] * mine)
        grad_rows.append(g_ref[...] * mine)
    query_rows = jnp.concatenate(query_rows, axis=0)
    grad_rows = jnp.concatenate(grad_rows, axis=0)
    nothing = jnp.zeros((HD, chunk), BF)
    dq = jnp.zeros((128, queries), F32)
    dv_total = jnp.zeros((1, 128), F32)

    def column(third):
        return pl.ds(pl.multiple_of((third * pairs + g) * 128, 128), 128)

    chunks = rows // chunk
    for c in range(chunks):
        part = slice(c * chunk, (c + 1) * chunk)
        aug = aug_ref[part, :]
        key = jnp.concatenate([k_ref[part, :], aug], axis=1)
        value = jnp.concatenate([v_ref[part, :], aug], axis=1)
        weights, grads = [], []
        for h in range(2):
            weight = jnp.exp2(dot_nn(key, query_cols[h]) * EXP2_SCALE)
            grads.append((weight * dot_nn(value, grad_cols[h])).astype(BF))
            weights.append(weight.astype(BF))
        upper = jnp.concatenate([kt_ref[0:HD, part], nothing], axis=1)
        lower = jnp.concatenate([nothing, kt_ref[HD : 2 * HD, part]], axis=1)
        dq = dq + dot_nn(jnp.concatenate([upper, lower], axis=0), jnp.concatenate(grads, axis=0))
        dv = dot_nn(jnp.concatenate(weights, axis=1), grad_rows)
        dk = dot_nn(jnp.concatenate(grads, axis=1), query_rows)
        dqkv[part, column(1)] = (dk * SCALE).astype(BF)
        dqkv[part, column(2)] = dv.astype(BF)
        dv_total = dv_total + total_rows(dv)
        if c == chunks // 2 - 1:
            at(0, (early_near, 0))
            at(3, (early_near, 2))
            at(5, (early_near, 3))
            at(6, (early_far, 2), (early_seq, 0))
            at(7, (early_near, 4))
            at(8, (early_far, 3))
            at(9, (early_far, 4), (early_seq, 1))

            @pl.when(step >= pairs + 1)
            def _():
                pair_near(step - pairs - 1)

            @pl.when(step >= pairs + 4)
            def _():
                pair_piece(2 * (step - pairs) - 7).send_far()

    @pl.when(step < pairs)
    def _():
        dq_sum[g] = dq
        pair = jnp.concatenate([dqkv[:, column(1)], dqkv[:, column(2)]], axis=1)
        half = dot_nn(xt_ref[...], pair)
        p_full[g, :, :, :, :, 128:384] = half.astype(BF).reshape(p_full.shape[1:5] + (256,))
        s_own[0, 1:2, column(0)] = dv_total

    @pl.when(step == pairs - 1)
    def _():
        tok_send[...] = dot_nt(dqkv[:, width:], w_ref[:, width:]).astype(BF)
        tokens_copy.start()

    @pl.when(step >= pairs)
    def _():
        turned = ((dq_sum[g] + dq) * SCALE).T
        low = turned.astype(BF)
        dqkv[:, column(0)] = low
        s_own[0, 0:1, column(0)] = total_rows(turned)
        s_own[0, 1:2, column(0)] += dv_total
        product = dot_nn(xt_ref[...], jnp.concatenate([low, dqkv[:, column(1)], dqkv[:, column(2)]], axis=1))
        shape = p_full.shape[1:5]
        before = p_full[g, :, :, :, :, 128:384].astype(F32)
        p_full[g, :, :, :, :, 0:128] = product[:, 0:128].astype(BF).reshape(shape + (128,))
        p_full[g, :, :, :, :, 128:384] = (product[:, 128:384].reshape(shape + (256,)) + before).astype(BF)
        pair_core_copy(g).start()

    at(0, (early_near, 1), (early_begin, 2), (early_begin, 3), (early_begin, 4))
    at(2, (early_far, 0))
    at(4, (early_far, 1))
    at(10, (early_seq, 2))

    @pl.when((step >= pairs + 3) & (step < last))
    def _():
        pair_piece(2 * (step - pairs) - 6).send_far()

    @pl.when(step == last)
    def _():
        final = pairs - 1
        hops = [(s_core, 0, links.to_core()), (s_near, 1, links.to_near())]
        hops += [(s_far.at[k - 1], 2 + k, links.to_far(k)) for k in range(1, depth)]
        hops += [(s_seq, 2, links.to_seq())]
        level = [0, 1] + [2] * (depth - 1) + [3]
        sums = [links.copy(s_own.at[n], dst, sums_base + index, peer) for n, (dst, index, peer) in zip(level, hops)]
        sums[0].start()
        out_copies = []

        def tokens(n):
            part = pl.ds(n * (rows // 4), rows // 4)
            acc[part, :] += dot_nt(dqkv[part, :], w_ref[...]) + tok_recv[part, :].astype(F32)
            out_copies.append(pltpu.make_async_copy(acc.at[part], tokens_out.at[part], local_sem.at[len(early) + 1 + n]))
            out_copies[-1].start()

        pair_piece(final - 1).send_far()
        early_seq(3)
        tokens_copy.wait_recv()
        one_copy.wait()
        tokens(0)
        pair_near(final)
        sums[0].wait_recv()
        s_own[1] = s_own[0] + s_core[...]
        sums[1].start()
        early_seq(4)
        tokens(1)
        pair_piece(0).send_seq()
        pair_piece(1).send_seq()
        tokens(2)
        pair_piece(2).send_seq()
        pair_piece(final).send_far()
        sums[1].wait_recv()
        s_own[2] = s_own[1] + s_near[...]
        for n in range(2, depth + 1):
            sums[n].start()
        tokens(3)
        for e in range(4):
            early_done(e)
        pair_piece(3).send_seq()
        pair_piece(4).send_seq()
        pair_piece(final).send_seq()
        total = s_own[2]
        for n in range(2, depth + 1):
            sums[n].wait_recv()
            total = total + s_far[n - 2]
        s_own[3] = total
        sums[depth + 1].start()
        early_done(4)
        for index in range(pairs):
            pair_done(index)
        sums[depth + 1].wait_recv()
        sums_out[...] = s_own[3] + s_seq[...]
        for n in range(4):
            out_copies[n].wait()
        for item in sums:
            item.wait_send()
        tokens_copy.wait_send()
        for e in range(len(early)):
            early_core_copy(e).wait_send()
            pieces[e].finish()
        for index in range(pairs):
            pair_core_copy(index).wait_send()
            pair_piece(index).finish()


EARLY = ((0, 0, 2), (0, 1, 2), (1, 0, 2), (1, 1, 2), (2, 0, 1))


def back_reduce(k, kt, v, qt, q, gt, g, aug, lse, delta, full_qkv, xt, grad_one, sums, sources, depth):
    keys, width = k.shape
    rows = keys // 2
    pairs = width // 128
    chunk = min(512, rows // 2)
    share = width // (4 * depth)
    views = [s.reshape(depth, 2, 2, s.shape[0] // (4 * depth), s.shape[1]) for s in sources]
    early = [(n, part * (views[n].shape[-1] // of), views[n].shape[-1] // of) for n, part, of in EARLY]
    key_rows = pl.BlockSpec((rows, 128), lambda i: (1 - i // pairs, i % pairs))
    query_cols = pl.BlockSpec((128, rows), lambda i: (i % pairs, 0))
    query_rows = pl.BlockSpec((rows, 128), lambda i: (0, i % pairs))
    stats = pl.BlockSpec((None, 2, rows), lambda i: (i % pairs, 0, 0))
    whole = pl.BlockSpec(memory_space=pltpu.VMEM)
    there = pl.BlockSpec(memory_space=pl.ANY)
    stages = []
    for n, _, wide in early:
        high = views[n].shape[3]
        stages += [
            pltpu.VMEM((depth, 2, high, wide), BF),
            pltpu.VMEM((depth, 2, high, wide), BF),
            pltpu.VMEM((depth, high, wide), BF),
            pltpu.VMEM((depth - 1, high, wide), BF),
            pltpu.VMEM((high, wide), BF),
        ]
    copies = (len(early) + pairs + 1) * (depth + 2) + 1
    return pl.pallas_call(
        functools.partial(back_kernel, depth, pairs, early, chunk),
        grid=(2 * pairs,),
        in_specs=[
            key_rows,
            pl.BlockSpec((128, rows), lambda i: (i % pairs, 1 - i // pairs)),
            key_rows,
            query_cols,
            query_rows,
            query_cols,
            query_rows,
            pl.BlockSpec((rows, 128), lambda i: (1 - i // pairs, 0)),
            stats,
            stats,
            whole,
            pl.BlockSpec((width, rows), lambda i: (0, 1 - i // pairs)),
            there,
            whole,
        ]
        + [there] * len(views),
        out_specs=[whole] * (2 + len(views)) + [there],
        out_shape=[jax.ShapeDtypeStruct((share, 3 * width), F32)]
        + [jax.ShapeDtypeStruct(s.shape[3:], F32) for s in views]
        + [jax.ShapeDtypeStruct(sums.shape, F32), jax.ShapeDtypeStruct((rows, width), F32)],
        scratch_shapes=stages
        + [
            pltpu.VMEM((pairs, depth, 2, 2, share, 384), BF),
            pltpu.VMEM((pairs, depth, 2, share, 384), BF),
            pltpu.VMEM((pairs, depth, share, 384), BF),
            pltpu.VMEM((pairs, depth - 1, share, 384), BF),
            pltpu.VMEM((pairs, share, 384), BF),
            pltpu.VMEM((rows, width), F32),
            pltpu.VMEM((pairs, 128, rows), F32),
            pltpu.VMEM((rows, width), BF),
            pltpu.VMEM((rows, width), BF),
            pltpu.VMEM((rows, 3 * width), BF),
            pltpu.VMEM((4,) + sums.shape, F32),
            pltpu.VMEM(sums.shape, F32),
            pltpu.VMEM(sums.shape, F32),
            pltpu.VMEM((depth - 1,) + sums.shape, F32),
            pltpu.VMEM(sums.shape, F32),
            pltpu.SemaphoreType.DMA((copies,)),
            pltpu.SemaphoreType.DMA((copies,)),
            pltpu.SemaphoreType.DMA((len(early) + 5,)),
        ],
        compiler_params=pltpu.CompilerParams(vmem_limit_bytes=61 << 20, collective_id=1, has_side_effects=True),
        cost_estimate=pl.CostEstimate(
            flops=40 * rows * keys * width, transcendentals=rows * keys * 2 * pairs, bytes_accessed=2 * width * 20 * rows
        ),
        name="back_reduce",
    )(k, kt, v, qt, q, gt, g, aug, lse, delta, full_qkv, xt, grad_one, sums, *views)


class Spread:
    def __init__(self, links, base, share, full, local):
        self.links, self.share, self.full = links, share, full
        self.send_base = base * (4 * links.depth + 2)
        self.recv_base = base * (4 * links.depth + 2)
        k = links
        self.local = pltpu.make_async_copy(share, full.at[k.far, k.near, k.core], local)

    def index(self, far, near, core):
        return self.recv_base + (far * 2 + near) * 2 + core

    def copy(self, src, slot, send, peer):
        return self.links.copy_two(src, self.full.at[slot], self.send_base + send, self.index(*slot), peer)

    def source(self, k):
        return self.links.ring[k]

    def far_copy(self, k):
        links = self.links
        return self.copy(self.share, (links.far, links.near, links.core), k - 1, links.peer(far=links.ring[k]))

    def near_copy(self, k):
        links = self.links
        slot = (self.source(k), links.near, links.core)
        return self.copy(self.share if k == 0 else self.full.at[slot], slot, links.depth - 1 + k, links.to_near())

    def core_copy(self, k, across):
        links = self.links
        slot = (self.source(k), 1 - links.near if across else links.near, links.core)
        src = self.share if k == 0 and not across else self.full.at[slot]
        return self.copy(src, slot, 2 * links.depth - 1 + 2 * k + across, links.to_core())

    def arrive(self, far, near, core):
        self.copy(self.share, (far, near, core), 0, self.links.to_core()).wait_recv()

    def begin(self):
        self.local.start()
        for k in range(1, self.links.depth):
            self.far_copy(k).start()
        self.near_copy(0).start()
        self.core_copy(0, 0).start()

    def pass_far(self):
        links = self.links
        for k in range(1, links.depth):
            self.arrive(self.source(k), links.near, links.core)
            self.near_copy(k).start()
            self.core_copy(k, 0).start()

    def pass_near(self):
        links = self.links
        for k in range(links.depth):
            self.arrive(self.source(k), 1 - links.near, links.core)
            self.core_copy(k, 1).start()

    def complete(self):
        links = self.links
        for k in range(links.depth):
            for near in range(2):
                self.arrive(self.source(k), near, 1 - links.core)
        self.local.wait()

    def finish(self):
        for k in range(self.links.depth):
            if k:
                self.far_copy(k).wait_send()
            self.near_copy(k).wait_send()
            self.core_copy(k, 0).wait_send()
            self.core_copy(k, 1).wait_send()


class SpreadHalf(Spread):
    def __init__(self, links, base, share, full, local):
        high = share.shape[0] // 2
        mine, others = pl.ds(links.seq * high, high), pl.ds((1 - links.seq) * high, high)
        super().__init__(links, base, share.at[mine], full.at[:, :, :, mine], local)
        self.mine = full.at[:, :, links.core, mine]
        self.others = full.at[:, :, links.core, others]
        self.across = full.at[:, :, 1 - links.core, others]

    def seq_copy(self):
        n = self.recv_base + 4 * self.links.depth
        return self.links.copy_two(self.mine, self.mine, n, n, self.links.to_seq())

    def seq_arrive(self):
        n = self.recv_base + 4 * self.links.depth
        self.links.copy_two(self.others, self.others, n, n, self.links.to_seq()).wait_recv()

    def other_copy(self):
        n = self.recv_base + 4 * self.links.depth + 1
        return self.links.copy_two(self.others, self.others, n, n, self.links.to_core())

    def pass_near(self):
        super().pass_near()
        self.local.wait()
        self.seq_copy().start()

    def pass_seq(self):
        self.seq_arrive()
        self.other_copy().start()

    def complete(self):
        links = self.links
        for k in range(links.depth):
            for near in range(2):
                self.arrive(self.source(k), near, 1 - links.core)
        n = self.recv_base + 4 * links.depth + 1
        links.copy_two(self.across, self.across, n, n, links.to_core()).wait_recv()

    def finish(self):
        super().finish()
        self.seq_copy().wait_send()
        self.other_copy().wait_send()


ROWS = (0, 2, 3, 7, 8, 9, 10, 11)


def forward_kernel(depth, pairs, later, chunk, *refs):
    x_ref, aug_ref, qkv_share = refs[:3]
    vec_refs = refs[3 : 3 + len(ROWS)]
    refs = refs[3 + len(ROWS) :]
    n_src = 1 + max(piece[0] for piece in later)
    shares = refs[:n_src]
    refs = refs[n_src:]
    q_ref, qt_ref, k_ref, kt_ref, v_ref, o_ref, lse_ref, xt_ref, sums_ref, qkv_out = refs[:10]
    fulls = refs[10 : 10 + n_src]
    w_own, w_all, v_all, v_own, other, vt, bias, qt_all, held, stats, send_sem, recv_sem, local_sem = refs[10 + n_src :]
    step = pl.program_id(0)
    g = step % pairs
    rows, width = x_ref.shape
    links = Links(depth, send_sem, recv_sem)
    groups = [Spread(links, n, w_own.at[n], w_all.at[n], local_sem.at[n]) for n in range(GROUPS)]
    vectors = Spread(links, GROUPS, v_own, v_all, local_sem.at[GROUPS])
    base = GROUPS + 1
    pieces = []
    for n, (source, start, wide, halved) in enumerate(later):
        part = pl.ds(start, wide)
        kind = SpreadHalf if halved else Spread
        pieces.append(kind(links, base + n, shares[source].at[:, part], fulls[source].at[:, :, :, :, part], local_sem.at[base + n]))
    spare = (base + len(later)) * (4 * depth + 2)
    tokens_copy = links.copy_two(x_ref, other, spare, spare, links.to_seq())
    span = width // GROUPS
    in_copies, out_copies = [], []
    for n in range(GROUPS):
        for third in range(3):
            mine, theirs = pl.ds(third * span, span), pl.ds(third * width + n * span, span)
            index = base + len(later) + 3 * n + third
            in_copies.append(pltpu.make_async_copy(qkv_share.at[:, theirs], w_own.at[n, :, mine], local_sem.at[index]))
            out_copies.append(
                pltpu.make_async_copy(w_all.at[n, :, :, :, :, mine], qkv_out.at[:, :, :, :, theirs], local_sem.at[index])
            )

    @pl.when(step == 0)
    def _():
        for copy in in_copies:
            copy.start()
        v_own[...] = jnp.zeros_like(v_own)
        for n, ref in enumerate(vec_refs):
            v_own[n : n + 1, 0 : ref.shape[1]] = ref[...]
        links.barrier()
        for copy in in_copies[:3]:
            copy.wait()
        groups[0].begin()
        tokens_copy.start()
        vectors.begin()
        for copy in in_copies[3:]:
            copy.wait()
        for n in range(1, GROUPS):
            groups[n].begin()
        xt_ref[:, 0:rows] = x_ref[...].T
        groups[0].pass_far()
        vectors.pass_far()
        groups[0].pass_near()
        vectors.pass_near()
        groups[1].pass_far()
        vectors.complete()
        target = lax.broadcasted_iota(jnp.int32, (16, width), 0)
        total = jnp.zeros((16, width), F32)
        blank = jnp.zeros((8, width - v_own.shape[1]), F32)
        for place in range(4 * depth):
            values = v_all[place // 4, place // 2 % 2, place % 2].astype(F32)
            values = jnp.concatenate([values, blank], axis=1)
            fitted = {}
            for size in VECTOR_UNITS:
                shift = place % (4 * depth // size) * (width * size // (4 * depth))
                fitted[size] = pltpu.roll(values, shift, 1) if shift else values
            for n, (first, size) in enumerate(zip(ROWS, VECTOR_SIZES)):
                row = first + place // (4 * depth // size)
                total = total + jnp.where(target == row, fitted[size][n : n + 1, :], 0.0)
        sums_ref[...] = total
        for n in range(pairs):
            bias[n, 0:2, :] = total[0:2, n * 128 : n * 128 + 128]
        groups[0].complete()

    def at(when, *actions):
        @pl.when(step == when)
        def _():
            for action in actions:
                action()

    group, place = g * GROUPS // pairs, g % (pairs // GROUPS)

    def weight(third):
        column = pl.ds(pl.multiple_of(third * span + place * 128, 128), 128)
        return w_all[group, :, :, :, :, column].reshape(width, 128)

    def project(tokens):
        kv = dot_nn(tokens[...], jnp.concatenate([weight(1), weight(2)], axis=1))
        k = kv[:, 0:128]
        v = kv[:, 128:256] + bias[g, 1:2, :]
        k_ref[...] = k.astype(BF)
        kt_ref[...] = k.T.astype(BF)
        v_ref[...] = v.astype(BF)
        vt[...] = v.T.astype(BF)

    here = pl.ds(pl.multiple_of(g * 128, 128), 128)

    @pl.when(step < pairs)
    def _():
        q = dot_nn(x_ref[...], weight(0)) + bias[g, 0:1, :]
        q_ref[...] = q.astype(BF)
        turned = q.T.astype(BF)
        qt_ref[...] = turned
        qt_all[here, :] = turned
        project(x_ref)
        held[g] = jnp.zeros(held.shape[1:], F32)
        stats[g, 0:2, :] = jnp.full((2, rows), -jnp.inf, F32)
        stats[g, 2:4, :] = jnp.zeros((2, rows), F32)

    @pl.when(step >= pairs)
    def _():
        @pl.when(step == pairs)
        def _():
            tokens_copy.wait_recv()
            xt_ref[:, rows : 2 * rows] = other[...].T

        project(other)

    row = lax.broadcasted_iota(jnp.int32, (16, rows), 0)
    tail = jnp.where(row == 0, 1.0, 0.0).astype(BF)
    none = jnp.zeros((HD, rows), BF)
    rest = jnp.zeros((112, rows), BF)
    qt = qt_all[here, :]
    queries = [
        jnp.concatenate([qt[0:HD, :], none, tail, rest], axis=0),
        jnp.concatenate([none, qt[HD : 2 * HD, :], tail, rest], axis=0),
    ]
    largest = [stats[g, h : h + 1, :] for h in range(2)]
    total = [stats[g, 2 + h : 3 + h, :] for h in range(2)]
    context = [held[g, HD * h : HD * h + HD, :] for h in range(2)]

    def score(c, h):
        part = slice(c * chunk, (c + 1) * chunk)
        return dot_nn(jnp.concatenate([k_ref[part, :], aug_ref[part, :]], axis=1), queries[h])

    ahead = [score(0, h) for h in range(2)]
    chunks = rows // chunk
    for c in range(chunks):
        part = slice(c * chunk, (c + 1) * chunk)
        for h in range(2):
            scores = ahead[h]
            if c + 1 < chunks:
                ahead[h] = score(c + 1, h)
            top = jnp.maximum(largest[h], jnp.max(scores, axis=0, keepdims=True))
            fade = jnp.exp2((largest[h] - top) * EXP2_SCALE)
            weights = jnp.exp2((scores - top) * EXP2_SCALE)
            largest[h] = top
            total[h] = total[h] * fade + total_rows(weights)
            context[h] = context[h] * fade + dot_nn(vt[HD * h : HD * h + HD, part], weights.astype(BF))

    @pl.when(step < pairs)
    def _():
        for h in range(2):
            stats[g, h : h + 1, :] = largest[h]
            stats[g, 2 + h : 3 + h, :] = total[h]
            held[g, HD * h : HD * h + HD, :] = context[h]

    @pl.when(step >= pairs)
    def _():
        for h in range(2):
            o_ref[HD * h : HD * h + HD, :] = (context[h] / total[h]).astype(BF)
            lse_ref[h : h + 1, :] = largest[h] * SCALE + jnp.log(total[h])

    at(0, groups[2].pass_far, *[piece.begin for piece in pieces])
    at(1, groups[1].pass_near, groups[1].complete)
    at(3, groups[2].pass_near, groups[2].complete, pieces[0].pass_far)
    at(4, pieces[1].pass_far)
    at(5, pieces[2].pass_far)
    at(6, pieces[0].pass_near)
    at(7, pieces[1].pass_near, pieces[3].pass_far)
    at(8, pieces[2].pass_near)
    at(9, pieces[4].pass_far)
    at(10, pieces[3].pass_near, pieces[5].pass_far)

    @pl.when(step == 2 * pairs - 1)
    def _():
        for copy in out_copies:
            copy.start()
        pieces[4].pass_near()
        pieces[5].pass_near()
        for piece in pieces:
            if isinstance(piece, SpreadHalf):
                piece.pass_seq()
        for piece in pieces:
            piece.complete()
        for piece in groups + [vectors] + pieces:
            piece.finish()
        tokens_copy.wait_send()
        for copy in out_copies:
            copy.wait()


GROUPS = 3
VECTOR_SIZES = (2, 1, 4, 1, 1, 1, 1, 1)
VECTOR_UNITS = (1, 2, 4)
LATER = ((2, 0, 2, 1), (2, 1, 2, 1), (0, 0, 1, 0), (1, 0, 3, 0), (1, 1, 3, 0), (1, 2, 3, 0))


def forward(x, aug, vectors, w_qkv, w_out, w_up, w_down, depth):
    rows, width = x.shape
    pairs = width // 128
    keys = 2 * rows
    chunk = min(512, rows)
    shares = (w_out, w_up, w_down)
    later = [(n, part * (shares[n].shape[1] // of), shares[n].shape[1] // of, halved) for n, part, of, halved in LATER]
    whole = pl.BlockSpec(memory_space=pltpu.VMEM)
    there = pl.BlockSpec(memory_space=pl.ANY)
    half_rows = pl.BlockSpec((rows, 128), lambda i: (i // pairs, i % pairs))
    fulls = [(depth, 2, 2) + s.shape for s in (w_qkv,) + shares]
    low = lambda *shape: jax.ShapeDtypeStruct(shape, BF)
    copies = (1 + GROUPS + len(later)) * (4 * depth + 2) + 1
    return pl.pallas_call(
        functools.partial(forward_kernel, depth, pairs, later, chunk),
        grid=(2 * pairs,),
        in_specs=[whole, pl.BlockSpec((rows, 128), lambda i: (i // pairs, 0)), there] + [whole] * len(vectors) + [there] * 3,
        out_specs=[
            pl.BlockSpec((rows, 128), lambda i: (0, jnp.minimum(i, pairs - 1))),
            pl.BlockSpec((128, rows), lambda i: (jnp.minimum(i, pairs - 1), 0)),
            half_rows,
            pl.BlockSpec((128, rows), lambda i: (i % pairs, i // pairs)),
            half_rows,
            pl.BlockSpec((128, rows), lambda i: (jnp.maximum(i - pairs, 0), 0)),
            pl.BlockSpec((None, 2, rows), lambda i: (jnp.maximum(i - pairs, 0), 0, 0)),
            whole,
            whole,
            there,
            there,
            there,
            there,
        ],
        out_shape=[
            low(rows, width),
            low(width, rows),
            low(keys, width),
            low(width, keys),
            low(keys, width),
            low(width, rows),
            jax.ShapeDtypeStruct((pairs, 2, rows), F32),
            low(width, keys),
            jax.ShapeDtypeStruct((16, width), F32),
        ]
        + [low(*f) for f in fulls],
        scratch_shapes=[
            pltpu.VMEM((GROUPS, w_qkv.shape[0], 3 * width // GROUPS), BF),
            pltpu.VMEM((GROUPS, depth, 2, 2, w_qkv.shape[0], 3 * width // GROUPS), BF),
            pltpu.VMEM((depth, 2, 2, 8, 256), BF),
            pltpu.VMEM((8, 256), BF),
            pltpu.VMEM((rows, width), BF),
            pltpu.VMEM((128, rows), BF),
            pltpu.VMEM((pairs, 8, 128), F32),
            pltpu.VMEM((width, rows), BF),
            pltpu.VMEM((pairs, 128, rows), F32),
            pltpu.VMEM((pairs, 8, rows), F32),
            pltpu.SemaphoreType.DMA((copies,)),
            pltpu.SemaphoreType.DMA((copies,)),
            pltpu.SemaphoreType.DMA((1 + 4 * GROUPS + len(later),)),
        ],
        compiler_params=pltpu.CompilerParams(vmem_limit_bytes=58 << 20, collective_id=2, has_side_effects=True),
        cost_estimate=pl.CostEstimate(
            flops=16 * rows * keys * width, transcendentals=rows * keys * 2 * pairs, bytes_accessed=2 * width * 10 * keys
        ),
        name="forward",
    )(x, aug, w_qkv, *[v.reshape(1, -1) for v in vectors], *shares)


def back_plain(k, kt, v, qt, q, grad_context, aug, lse, delta, full_qkv, both, grad_one, grads, sources, sizes):
    width = k.shape[1]
    rows = q.shape[0]

    def scatter(value):
        return lax.psum_scatter(value.astype(BF), "dp", scatter_dimension=0, tiled=True)

    def over_seq(value):
        value = value.astype(BF)
        return value.astype(F32) + lax.ppermute(value, "seq", [(0, 1), (1, 0)]).astype(F32)

    share_wout, share_wup, share_wdown = [scatter(s) for s in sources]
    dqt, dk, dv = attend_back(k, kt, v, qt, q, grad_context.T, grad_context, aug, lse, delta)
    dq = dqt.T
    partial = dot_nt(jnp.concatenate([dk[rows:], dv[rows:]], axis=1), full_qkv[:, width:])
    partial = lax.ppermute(partial.astype(BF), "seq", [(0, 1), (1, 0)])
    own = jnp.concatenate([dq, dk[:rows], dv[:rows]], axis=1)
    grad_wq, grad_wk, grad_wv = dot_tn(both[:rows], dq), dot_tn(both, dk), dot_tn(both, dv)
    grad_inputs = grad_one + dot_nt(own, full_qkv) + partial.astype(F32)
    grads = (jnp.concatenate([column_sum(dq), column_sum(dv)]),) + tuple(grads)
    extra = sum(g.shape[0] for g in grads) // width
    packed = jnp.concatenate([g.reshape(-1, size) for g, size in zip(grads, sizes)], axis=1).reshape(width, extra)
    packed = jnp.pad(packed, ((0, 0), (0, 128 - extra)))
    share_qkv = over_seq(scatter(jnp.concatenate([grad_wq, grad_wk, grad_wv, packed], axis=1)))
    packed = share_qkv[:, 3 * width : 3 * width + extra].reshape(-1)
    out_vectors, start = [], 0
    for size in sizes:
        out_vectors.append(packed[start : start + size])
        start += size
    return share_qkv[:, : 3 * width], over_seq(share_wout), over_seq(share_wup), over_seq(share_wdown), out_vectors, grad_inputs


def normalize(values):
    center = jnp.mean(values, axis=-1, keepdims=True)
    shifted = values - center
    spread = jnp.mean(shifted * shifted, axis=-1, keepdims=True)
    scale = lax.rsqrt(spread + EPS)
    return shifted * scale, scale


def normalize_back(grad, normal, scale):
    mean = jnp.mean(grad, axis=-1, keepdims=True)
    along = jnp.mean(grad * normal, axis=-1, keepdims=True)
    return (grad - mean - normal * along) * scale


def middle_kernel(*refs):
    x_ref, ot_ref, vec_ref, cot_hbm, wout_hbm, wup_hbm, wdown_hbm = refs[:7]
    result_hbm, one_hbm, g_hbm, gt_hbm, delta_ref, sums_ref, gdown_hbm, gup_hbm, gout_hbm = refs[7:16]
    wout, wup, wdown, cot_buf, acts, pres, hiddens, branches, projs, normals, grads, result, turned_buf, stage, sem = refs[16:]
    rows, width = x_ref.shape
    ff = wup.shape[1]
    wide = ff // FF_PARTS
    copies = [
        pltpu.make_async_copy(src, dst, sem.at[n])
        for n, (src, dst) in enumerate(((wout_hbm, wout), (wup_hbm, wup), (wdown_hbm, wdown), (cot_hbm, cot_buf)))
    ]
    for copy in copies:
        copy.start()

    def vector(n):
        return vec_ref[n : n + 1, :]

    ot = ot_ref[...]
    context = ot.T
    copies[0].wait()
    attn = dot_nn(context, wout[...]) + vector(2)
    normal_one, scale_one = normalize(x_ref[...].astype(F32) + attn)
    normals[...] = normal_one
    low = (normal_one * vector(8) + vector(9)).astype(BF)
    hiddens[...] = low
    copies[1].wait()
    copies[2].wait()
    grads[...] = normals[...] * vector(8) + (vector(9) + vector(7))
    for c in range(FF_PARTS):
        part = slice(c * wide, (c + 1) * wide)
        row, start = divmod(c * wide, width)
        pre = dot_nn(hiddens[...], wup[:, part]) + vec_ref[3 + row : 4 + row, start : start + wide]
        bell = 0.5 * (1.0 + lax.erf(pre * 0.7071067811865476))
        act = (pre * bell).astype(BF)
        pres[:, part] = (bell + pre * (jnp.exp(-0.5 * pre * pre) * 0.3989422804014327)).astype(BF)
        acts[:, part] = act
        grads[...] += dot_nn(act, wdown[part, :])
    normal_two, scale_two = normalize(grads[...])
    result[...] = (normal_two * vector(10) + vector(11)).astype(BF)
    out_result = pltpu.make_async_copy(result, result_hbm, sem.at[4])
    out_result.start()
    copies[3].wait()
    cot = cot_buf[...].astype(F32)
    sums_ref[...] = jnp.zeros_like(sums_ref)
    sums_ref[10:11, :] = total_rows(cot * normal_two)
    sums_ref[11:12, :] = total_rows(cot)
    grad_two = normalize_back(cot * vector(10), normal_two, scale_two)
    grads[...] = grad_two
    branch = grad_two.astype(BF)
    branches[...] = branch
    sums_ref[7:8, :] = total_rows(branch.astype(F32))
    for c in range(FF_PARTS):
        part = slice(c * wide, (c + 1) * wide)
        row, start = divmod(c * wide, width)
        grad_pre = (dot_nt(branches[...], wdown[part, :]) * pres[:, part].astype(F32)).astype(BF)
        pres[:, part] = grad_pre
        sums_ref[3 + row : 4 + row, start : start + wide] = total_rows(grad_pre.astype(F32))
        grads[...] += dot_nt(grad_pre, wup[:, part])
    grad_hidden = grads[...]
    normal_one = normals[...]
    sums_ref[8:9, :] = total_rows(grad_hidden * normal_one)
    sums_ref[9:10, :] = total_rows(grad_hidden)
    grad_one = normalize_back(grad_hidden * vector(8), normal_one, scale_one)
    grads[...] = grad_one
    out_one = pltpu.make_async_copy(grads, one_hbm, sem.at[5])
    out_one.start()
    proj = grad_one.astype(BF)
    projs[...] = proj
    sums_ref[2:3, :] = total_rows(proj.astype(F32))
    grad_context = dot_nt(projs[...], wout[...])
    out_result.wait()
    result[...] = grad_context.astype(BF)
    out_g = pltpu.make_async_copy(result, g_hbm, sem.at[4])
    out_g.start()
    turned = grad_context.T.astype(BF)
    turned_buf[...] = turned
    out_gt = pltpu.make_async_copy(turned_buf, gt_hbm, sem.at[6])
    out_gt.start()
    each = (turned.astype(F32) * ot.astype(F32)).reshape(width // HD, HD, rows)
    delta_ref[...] = jnp.sum(each, axis=1).reshape(delta_ref.shape)

    outs = []

    def put(value, target):
        n = len(outs)
        if n >= 2:
            outs[n - 2].wait()
        stage[n % 2] = value.astype(BF)
        outs.append(pltpu.make_async_copy(stage.at[n % 2], target, sem.at[7 + n % 2]))
        outs[n].start()

    for c in range(ff // width):
        part = slice(c * width, (c + 1) * width)
        put(dot_nn(acts[:, part].T, branches[...]), gdown_hbm.at[pl.ds(c * width, width)])
    turned = hiddens[...].T
    for c in range(ff // width):
        part = slice(c * width, (c + 1) * width)
        put(dot_nn(turned, pres[:, part]), gup_hbm.at[:, pl.ds(c * width, width)])
    put(dot_nn(ot_ref[...], projs[...]), gout_hbm)
    for copy in outs[-2:] + [out_one, out_g, out_gt]:
        copy.wait()


FF_PARTS = 4


def middle(x, cotangent, context_t, vectors, w_out, w_up, w_down):
    rows, width = x.shape
    ff = w_up.shape[1]
    pairs = width // 128
    whole = pl.BlockSpec(memory_space=pltpu.VMEM)
    there = pl.BlockSpec(memory_space=pl.ANY)
    shape = jax.ShapeDtypeStruct
    return pl.pallas_call(
        middle_kernel,
        in_specs=[whole, whole, whole, there, there, there, there],
        out_specs=[there, there, there, there, whole, whole, there, there, there],
        out_shape=[
            shape((rows, width), BF),
            shape((rows, width), F32),
            shape((rows, width), BF),
            shape((width, rows), BF),
            shape((pairs, 2, rows), F32),
            shape((16, width), F32),
            shape((ff, width), BF),
            shape((width, ff), BF),
            shape((width, width), BF),
        ],
        scratch_shapes=[
            pltpu.VMEM((width, width), BF),
            pltpu.VMEM((width, ff), BF),
            pltpu.VMEM((ff, width), BF),
            pltpu.VMEM((rows, width), BF),
            pltpu.VMEM((rows, ff), BF),
            pltpu.VMEM((rows, ff), BF),
            pltpu.VMEM((rows, width), BF),
            pltpu.VMEM((rows, width), BF),
            pltpu.VMEM((rows, width), BF),
            pltpu.VMEM((rows, width), F32),
            pltpu.VMEM((rows, width), F32),
            pltpu.VMEM((rows, width), BF),
            pltpu.VMEM((width, rows), BF),
            pltpu.VMEM((2, width, width), BF),
            pltpu.SemaphoreType.DMA((9,)),
        ],
        compiler_params=pltpu.CompilerParams(vmem_limit_bytes=58 << 20),
        cost_estimate=pl.CostEstimate(
            flops=6 * rows * width * (width + 2 * ff), transcendentals=2 * rows * ff, bytes_accessed=8 * width * (width + 2 * ff)
        ),
        name="middle",
    )(x, context_t, vectors, cotangent, w_out, w_up, w_down)


def finish_kernel(parts, *refs):
    count = (len(refs) - 2 - len(ROWS)) // 3
    sums_ref, sources = refs[0], refs[1 : 1 + count]
    targets, small = refs[1 + count : 1 + 2 * count], refs[1 + 2 * count : 1 + 2 * count + len(ROWS)]
    held, sem = refs[-1 - count : -1], refs[-1]
    rows = sources[0].shape[0] // 4
    cuts = [(0, pl.ds(n * rows, rows)) for n in range(4)] + [(n, slice(None)) for n in range(1, count)]
    loads, stores = [], []
    for index, (n, part) in enumerate(cuts):
        loads.append(pltpu.make_async_copy(sources[n].at[part], held[n].at[part], sem.at[index]))
        stores.append(pltpu.make_async_copy(held[n].at[part], targets[n].at[part], sem.at[len(cuts) + index]))
    for copy in loads:
        copy.start()
    width = sums_ref.shape[1]
    place = lax.axis_index("dp")
    picked = []
    for base, size in zip(ROWS, VECTOR_SIZES):
        picked.append(sums_ref[pl.ds(base + place // (parts // size), 1), :])
    picked = jnp.concatenate(picked, axis=0)
    for size in VECTOR_UNITS:
        shift = (place % (parts // size)) * (width * size // parts)
        turned = pltpu.roll(picked, (width - shift) % width, 1)
        for n in range(len(ROWS)):
            if VECTOR_SIZES[n] == size:
                small[n][...] = turned[n : n + 1, 0 : small[n].shape[1]]
    for load, store in zip(loads, stores):
        load.wait()
        store.start()
    for store in stores:
        store.wait()


def finish(sums, tokens, shares, parts):
    whole = pl.BlockSpec(memory_space=pltpu.VMEM)
    there = pl.BlockSpec(memory_space=pl.ANY)
    width = sums.shape[1]
    large = (tokens,) + shares
    small = [jax.ShapeDtypeStruct((1, width * size // parts), F32) for size in VECTOR_SIZES]
    out = pl.pallas_call(
        functools.partial(finish_kernel, parts),
        in_specs=[whole] + [there] * len(large),
        out_specs=[there] * len(large) + [whole] * len(small),
        out_shape=[jax.ShapeDtypeStruct(x.shape, x.dtype) for x in large] + small,
        scratch_shapes=[pltpu.VMEM(x.shape, x.dtype) for x in large] + [pltpu.SemaphoreType.DMA((2 * (len(shares) + 4),))],
        compiler_params=pltpu.CompilerParams(vmem_limit_bytes=58 << 20),
        name="finish",
    )(sums, *large)
    return out[: len(large)], [v.reshape(-1) for v in out[len(large) :]]


def forward_plain(x, aug, vectors, w_qkv):
    width = x.shape[1]
    other = lax.ppermute(x, "seq", [(0, 1), (1, 0)])
    sizes = [v.shape[0] for v in vectors]
    share = w_qkv.shape[0]
    extra = sum(sizes) // share
    beside = jnp.concatenate(vectors).reshape(share, extra)
    beside = jnp.concatenate([w_qkv, jnp.pad(beside, ((0, 0), (0, 128 - extra)))], axis=1)
    full_qkv = lax.all_gather(beside, "dp", axis=0, tiled=True)
    full_vectors = full_qkv[:, 3 * width : 3 * width + extra].reshape(-1, sum(sizes)).astype(F32)
    full_qkv = full_qkv[:, : 3 * width]
    full, start = [], 0
    for size in sizes:
        full.append(full_vectors[:, start : start + size].reshape(-1))
        start += size
    both = jnp.concatenate([x, other], axis=0)
    q = (dot_nn(x, full_qkv[:, :width]) + full[0][:width]).astype(BF)
    k = dot_nn(both, full_qkv[:, width : 2 * width]).astype(BF)
    v = (dot_nn(both, full_qkv[:, 2 * width :]) + full[0][width:]).astype(BF)
    qt, kt, vt = q.T, k.T, v.T
    context_t, lse = attend(k, qt, vt, aug)
    return q, qt, k, kt, v, both, context_t, lse, full_qkv, full[1:]


def plain(x, aug, vectors, w_qkv, w_out, w_up, w_down, upstream):
    rows, width = x.shape
    sizes = [v.shape[0] for v in vectors]
    q, qt, k, kt, v, both, context_t, lse, full_qkv, full = forward_plain(x, aug, vectors, w_qkv)
    full_bout, full_bup, full_bdown, gain_one, shift_one, gain_two, shift_two = full
    full_wout, full_wup, full_wdown = [lax.all_gather(w, "dp", axis=0, tiled=True) for w in (w_out, w_up, w_down)]
    context = context_t.T
    attn_branch = dot_nn(context, full_wout) + full_bout
    resid_one = x.astype(F32) + attn_branch
    hidden_one, first_pull = jax.vjp(layer_norm, resid_one, gain_one, shift_one)
    hidden_low = hidden_one.astype(BF)
    pre_act = dot_nn(hidden_low, full_wup) + full_bup
    activated, gelu_pull = jax.vjp(gelu_exact, pre_act)
    act_low = activated.astype(BF)
    ffn_branch = dot_nn(act_low, full_wdown) + full_bdown
    resid_two = hidden_one + ffn_branch
    output, second_pull = jax.vjp(layer_norm, resid_two, gain_two, shift_two)
    grad_two, grad_gain_two, grad_shift_two = second_pull(upstream.astype(F32))
    grad_branch = grad_two.astype(BF)
    grad_wdown = dot_tn(act_low, grad_branch)
    grad_bdown = column_sum(grad_branch)
    (grad_pre,) = gelu_pull(dot_nt(grad_branch, full_wdown))
    grad_pre_low = grad_pre.astype(BF)
    grad_wup = dot_tn(hidden_low, grad_pre_low)
    grad_bup = column_sum(grad_pre_low)
    grad_hidden = grad_two + dot_nt(grad_pre_low, full_wup)
    grad_one, grad_gain_one, grad_shift_one = first_pull(grad_hidden)
    grad_proj = grad_one.astype(BF)
    grad_wout = dot_tn(context, grad_proj)
    grad_bout = column_sum(grad_proj)
    grad_context = dot_nt(grad_proj, full_wout).astype(BF)
    delta = jnp.sum((grad_context.astype(F32) * context.astype(F32)).reshape(rows, HEADS, HD), axis=-1)
    delta = delta.T.reshape(HEADS // 2, 2, rows)

    grads = (grad_bout, grad_bup, grad_bdown, grad_gain_one, grad_shift_one, grad_gain_two, grad_shift_two)
    share_qkv, share_out, share_up, share_down, out_vectors, grad_inputs = back_plain(
        k, kt, v, qt, q, grad_context, aug, lse, delta, full_qkv, both, grad_one, grads, (grad_wout, grad_wup, grad_wdown), sizes
    )
    return output.astype(BF), grad_inputs, share_qkv, share_out, share_up, share_down, out_vectors


def local(
    tokens,
    lengths,
    w_qkv,
    bias_qv,
    w_out,
    bias_out,
    w_up,
    bias_up,
    w_down,
    bias_down,
    gain_attn,
    shift_attn,
    gain_ffn,
    shift_ffn,
    cotangent,
):
    x = tokens[0]
    rows, width = x.shape
    ff = w_up.shape[1]
    me = lax.axis_index("seq")
    parts = lax.axis_size("dp")
    aligned = parts % 4 == 0 and width % (16 * parts) == 0 and ff % (16 * parts) == 0
    vectors = (bias_qv, bias_out, bias_up, bias_down, gain_attn, shift_attn, gain_ffn, shift_ffn)
    sizes = [v.shape[0] for v in vectors]
    aligned = aligned and tuple(s * parts for s in sizes) == tuple(n * width for n in VECTOR_SIZES) and parts == 16

    slot = jnp.arange(2 * rows)
    slot = jnp.where(slot < rows, me * rows + slot, (1 - me) * rows + slot - rows)
    lane = jnp.arange(128)
    masked = jnp.where(slot < lengths[0], 0.0, MASK)
    aug = jnp.where(lane[None] == 0, masked[:, None], jnp.where(lane[None] < 4, -1.0, 0.0)).astype(BF)

    if aligned:
        q, qt, k, kt, v, context_t, lse, xt, summed, full_qkv, full_wout, full_wup, full_wdown = forward(
            x, aug, vectors, w_qkv, w_out, w_up, w_down, parts // 4
        )
        full_qkv = full_qkv.reshape(width, 3 * width)
        output, grad_one, grad_context, grad_context_t, delta, sums, grad_wdown, grad_wup, grad_wout = middle(
            x, cotangent[0], context_t, summed, full_wout.reshape(width, width), full_wup.reshape(width, ff), full_wdown.reshape(ff, width)
        )
        sources = (grad_wdown, grad_wup, grad_wout)
        share_qkv, share_down, share_up, share_out, sums, grad_inputs = back_reduce(
            k, kt, v, qt, q, grad_context_t, grad_context, aug, lse, delta, full_qkv, xt, grad_one, sums, sources, parts // 4
        )
        large, out_vectors = finish(sums, grad_inputs, (share_qkv, share_out, share_up, share_down), parts)
        grad_inputs, share_qkv, share_out, share_up, share_down = large
    else:
        output, grad_inputs, share_qkv, share_out, share_up, share_down, out_vectors = plain(
            x, aug, vectors, w_qkv, w_out, w_up, w_down, cotangent[0]
        )
    s_bqv, s_bout, s_bup, s_bdown, s_gain_one, s_shift_one, s_gain_two, s_shift_two = out_vectors
    return (
        output[None],
        grad_inputs[None],
        share_qkv,
        s_bqv,
        share_out,
        s_bout,
        share_up,
        s_bup,
        share_down,
        s_bdown,
        s_gain_one,
        s_shift_one,
        s_gain_two,
        s_shift_two,
    )


def solution(mesh):
    act, mat, vec = P("dp", "seq", None), P("dp", None), P("dp")
    in_specs = (act, vec, mat, vec, mat, vec, mat, vec, mat, vec, vec, vec, vec, vec, act)
    out_specs = (act, act, mat, vec, mat, vec, mat, vec, mat, vec, vec, vec, vec, vec)
    return jax.shard_map(local, mesh=mesh, in_specs=in_specs, out_specs=out_specs, check_vma=False)
```

```python
import functools

import jax
import jax.numpy as jnp
from jax import lax
from jax.experimental import pallas as pl
from jax.experimental.pallas import tpu as pltpu
from jax.sharding import PartitionSpec as P

HEADS = 12
HD = 64
EPS = 1e-05
BF = jnp.bfloat16
F32 = jnp.float32
SCALE = HD**-0.5
EXP2_SCALE = SCALE * 1.4426950408889634
MASK = -8e9


def dot_nn(a, b):
    return lax.dot_general(a, b, (((1,), (0,)), ((), ())), preferred_element_type=F32)


def dot_nt(a, b):
    return lax.dot_general(a, b, (((1,), (1,)), ((), ())), preferred_element_type=F32)


def dot_tn(a, b):
    return lax.dot_general(a, b, (((0,), (0,)), ((), ())), preferred_element_type=F32)


def layer_norm(values, gain, offset):
    center = jnp.mean(values, axis=-1, keepdims=True)
    shifted = values - center
    spread = jnp.mean(shifted * shifted, axis=-1, keepdims=True)
    return shifted * lax.rsqrt(spread + EPS) * gain + offset


def gelu_exact(values):
    return 0.5 * values * (1.0 + lax.erf(values * 0.7071067811865476))


def column_sum(values):
    return jnp.sum(values.astype(F32), axis=0)


def total_rows(values):
    return jnp.sum(values, axis=0, keepdims=True)


def attend_kernel(chunk, k_ref, qt_ref, vt_ref, aug_ref, o_ref, lse_ref, *scratch):
    keys = k_ref.shape[0]
    queries = qt_ref.shape[1]
    qt = qt_ref[...]
    row = lax.broadcasted_iota(jnp.int32, (128, queries), 0)
    tail = jnp.where(row == 0, 1.0, 0.0).astype(BF)
    for h in range(2):
        held = scratch[h]
        mine = jnp.where((row >= HD * h) & (row < HD * h + HD), qt, 0).astype(BF)
        query = jnp.concatenate([mine, tail], axis=0)
        largest = jnp.full((1, queries), -jnp.inf, F32)
        for c in range(keys // chunk):
            part = slice(c * chunk, (c + 1) * chunk)
            key = jnp.concatenate([k_ref[part, :], aug_ref[part, :]], axis=1)
            scores = dot_nn(key, query)
            held[part, :] = scores
            largest = jnp.maximum(largest, jnp.max(scores, axis=0, keepdims=True))
        total = jnp.zeros((1, queries), F32)
        context = jnp.zeros((HD, queries), F32)
        base = largest * EXP2_SCALE
        for c in range(keys // chunk):
            part = slice(c * chunk, (c + 1) * chunk)
            weight = jnp.exp2(held[part, :] * EXP2_SCALE - base)
            total = total + jnp.sum(weight, axis=0, keepdims=True)
            context = context + dot_nn(vt_ref[HD * h : HD * h + HD, part], weight.astype(BF))
        o_ref[HD * h : HD * h + HD, :] = (context / total).astype(BF)
        lse_ref[h : h + 1, :] = largest * SCALE + jnp.log(total)


def attend(k, qt, vt, aug):
    keys, width = k.shape
    queries = qt.shape[1]
    pairs = width // 128
    block = min(1024, queries)
    chunk = min(256, keys)
    return pl.pallas_call(
        functools.partial(attend_kernel, chunk),
        grid=(pairs, queries // block),
        in_specs=[
            pl.BlockSpec((keys, 128), lambda g, i: (0, g)),
            pl.BlockSpec((128, block), lambda g, i: (g, i)),
            pl.BlockSpec((128, keys), lambda g, i: (g, 0)),
            pl.BlockSpec((keys, 128), lambda g, i: (0, 0)),
        ],
        out_specs=[
            pl.BlockSpec((128, block), lambda g, i: (g, i)),
            pl.BlockSpec((None, 2, block), lambda g, i: (g, 0, i)),
        ],
        out_shape=[
            jax.ShapeDtypeStruct((width, queries), BF),
            jax.ShapeDtypeStruct((pairs, 2, queries), F32),
        ],
        scratch_shapes=[pltpu.VMEM((keys, block), F32)] * 2,
        compiler_params=pltpu.CompilerParams(vmem_limit_bytes=56 << 20),
        cost_estimate=pl.CostEstimate(
            flops=16 * queries * keys * width, transcendentals=queries * keys * 2 * pairs, bytes_accessed=2 * width * (queries + 2 * keys)
        ),
        name="attend",
    )(k, qt, vt, aug)


def three_terms(row, values):
    high = values.astype(BF).astype(F32)
    middle = (values - high).astype(BF).astype(F32)
    low = values - high - middle
    return jnp.where(row == 1, high, 0.0) + jnp.where(row == 2, middle, 0.0) + jnp.where(row == 3, low, 0.0)


def attend_back_kernel(
    chunk, k_ref, kt_ref, v_ref, qt_ref, q_ref, gt_ref, g_ref, aug_ref, lse_ref, delta_ref, dqt_ref, dk_ref, dv_ref, dk_sum, dv_sum
):
    step = pl.program_id(1)
    keys = k_ref.shape[0]
    queries = qt_ref.shape[1]

    @pl.when(step == 0)
    def _():
        dk_sum[...] = jnp.zeros_like(dk_sum)
        dv_sum[...] = jnp.zeros_like(dv_sum)

    qt = qt_ref[...]
    gt = gt_ref[...]
    q = q_ref[...]
    g = g_ref[...]
    row = lax.broadcasted_iota(jnp.int32, (128, queries), 0)
    lane = lax.broadcasted_iota(jnp.int32, (queries, 128), 1)
    query_cols, grad_cols, query_rows, grad_rows = [], [], [], []
    for h in range(2):
        down = (row >= HD * h) & (row < HD * h + HD)
        across = (lane >= HD * h) & (lane < HD * h + HD)
        tail = three_terms(row, lse_ref[h : h + 1, :] * (1.0 / SCALE)) + jnp.where(row == 0, 1.0, 0.0)
        query_cols.append(jnp.concatenate([jnp.where(down, qt, 0).astype(BF), tail.astype(BF)], axis=0))
        tail = three_terms(row, delta_ref[h : h + 1, :])
        grad_cols.append(jnp.concatenate([jnp.where(down, gt, 0).astype(BF), tail.astype(BF)], axis=0))
        query_rows.append(jnp.where(across, q, 0).astype(BF))
        grad_rows.append(jnp.where(across, g, 0).astype(BF))
    query_rows = jnp.concatenate(query_rows, axis=0)
    grad_rows = jnp.concatenate(grad_rows, axis=0)
    dq = [jnp.zeros((HD, queries), F32)] * 2
    for c in range(keys // chunk):
        part = slice(c * chunk, (c + 1) * chunk)
        aug = aug_ref[part, :]
        key = jnp.concatenate([k_ref[part, :], aug], axis=1)
        value = jnp.concatenate([v_ref[part, :], aug], axis=1)
        weights, grads = [], []
        for h in range(2):
            weight = jnp.exp2(dot_nn(key, query_cols[h]) * EXP2_SCALE)
            grad = (weight * dot_nn(value, grad_cols[h])).astype(BF)
            weights.append(weight.astype(BF))
            grads.append(grad)
            dq[h] = dq[h] + dot_nn(kt_ref[HD * h : HD * h + HD, part], grad)
        dv_sum[part, :] += dot_nn(jnp.concatenate(weights, axis=1), grad_rows)
        dk_sum[part, :] += dot_nn(jnp.concatenate(grads, axis=1), query_rows)
    for h in range(2):
        dqt_ref[HD * h : HD * h + HD, :] = (dq[h] * SCALE).astype(BF)

    @pl.when(step == pl.num_programs(1) - 1)
    def _():
        dk_ref[...] = (dk_sum[...] * SCALE).astype(BF)
        dv_ref[...] = dv_sum[...].astype(BF)


def attend_back(k, kt, v, qt, q, gt, g, aug, lse, delta):
    keys, width = k.shape
    queries = qt.shape[1]
    pairs = width // 128
    block = min(1024, queries)
    chunk = min(256, keys)
    key_rows = pl.BlockSpec((keys, 128), lambda g, i: (0, g))
    query_cols = pl.BlockSpec((128, block), lambda g, i: (g, i))
    query_rows = pl.BlockSpec((block, 128), lambda g, i: (i, g))
    stats = pl.BlockSpec((None, 2, block), lambda g, i: (g, 0, i))
    return pl.pallas_call(
        functools.partial(attend_back_kernel, chunk),
        grid=(pairs, queries // block),
        in_specs=[
            key_rows,
            pl.BlockSpec((128, keys), lambda g, i: (g, 0)),
            key_rows,
            query_cols,
            query_rows,
            query_cols,
            query_rows,
            pl.BlockSpec((keys, 128), lambda g, i: (0, 0)),
            stats,
            stats,
        ],
        out_specs=[query_cols, key_rows, key_rows],
        out_shape=[
            jax.ShapeDtypeStruct((width, queries), BF),
            jax.ShapeDtypeStruct((keys, width), BF),
            jax.ShapeDtypeStruct((keys, width), BF),
        ],
        scratch_shapes=[pltpu.VMEM((keys, 128), F32)] * 2,
        compiler_params=pltpu.CompilerParams(vmem_limit_bytes=56 << 20),
        cost_estimate=pl.CostEstimate(
            flops=40 * queries * keys * width, transcendentals=queries * keys * 2 * pairs, bytes_accessed=2 * width * (5 * queries + 5 * keys)
        ),
        name="attend_back",
    )(k, kt, v, qt, q, gt, g, aug, lse, delta)


MESH = pl.DeviceIdType.MESH


class Links:
    def __init__(self, depth, send_sem, recv_sem):
        index = lax.axis_index("dp")
        self.depth = depth
        self.core = index % 2
        self.near = (index // 2) % 2
        self.far = index // 4
        self.seq = lax.axis_index("seq")
        self.ring = [self.far] + [(self.far + k) % depth for k in range(1, depth)]
        if depth == 4:
            orders = ((0, 1, 2, 3), (1, 0, 2, 3), (2, 1, 3, 0), (3, 2, 1, 0))
            for n in range(1, 4):
                self.ring[n] = sum(jnp.where(self.far == place, orders[place][n], 0) for place in range(4))
        self.send_sem, self.recv_sem = send_sem, recv_sem

    def peer(self, core=None, near=None, far=None):
        core = self.core if core is None else core
        near = self.near if near is None else near
        far = self.far if far is None else far
        return {"dp": (far * 2 + near) * 2 + core}

    def to_core(self):
        return self.peer(core=1 - self.core)

    def to_near(self):
        return self.peer(near=1 - self.near)

    def to_far(self, k):
        return self.peer(far=(self.far + k) % self.depth)

    def to_seq(self):
        return {"seq": 1 - self.seq}

    def all_peers(self):
        return [self.to_core(), self.to_near(), self.to_seq()] + [self.to_far(k) for k in range(1, self.depth)]

    def barrier(self):
        semaphore = pltpu.get_barrier_semaphore()
        peers = self.all_peers()
        for peer in peers:
            pl.semaphore_signal(semaphore, inc=1, device_id=peer, device_id_type=MESH)
        pl.semaphore_wait(semaphore, len(peers))

    def copy(self, src, dst, index, peer):
        return self.copy_two(src, dst, index, index, peer)

    def copy_two(self, src, dst, send, recv, peer):
        return pltpu.make_async_remote_copy(
            src_ref=src, dst_ref=dst, send_sem=self.send_sem.at[send], recv_sem=self.recv_sem.at[recv], device_id=peer, device_id_type=MESH
        )


class Piece:
    def __init__(self, links, base, own, from_core, from_near, from_far, from_seq):
        self.links, self.base = links, base
        self.own, self.from_core, self.from_near, self.from_far, self.from_seq = own, from_core, from_near, from_far, from_seq

    def near_copy(self):
        k = self.links
        return k.copy(self.own.at[:, 1 - k.near], self.from_near, self.base + 1, k.to_near())

    def far_copy(self, distance):
        k = self.links
        target = (k.far + distance) % k.depth
        return k.copy(self.own.at[target, k.near], self.from_far.at[distance - 1], self.base + 2 + distance, k.to_far(distance))

    def seq_copy(self):
        k = self.links
        return k.copy(self.own.at[k.far, k.near], self.from_seq, self.base + 2, k.to_seq())

    def send_near(self):
        k = self.links
        for z in range(k.depth):
            total = self.own[z, 1 - k.near].astype(F32) + self.from_core[z, 1 - k.near].astype(F32)
            self.own[z, 1 - k.near] = total.astype(BF)
        self.near_copy().start()

    def send_far(self):
        k = self.links
        self.near_copy().wait_recv()
        for z in range(k.depth):
            total = self.own[z, k.near].astype(F32) + self.from_core[z, k.near].astype(F32) + self.from_near[z].astype(F32)
            self.own[z, k.near] = total.astype(BF)
        for distance in range(1, k.depth):
            self.far_copy(distance).start()

    def send_seq(self):
        k = self.links
        total = self.own[k.far, k.near].astype(F32)
        for distance in range(1, k.depth):
            self.far_copy(distance).wait_recv()
            total = total + self.from_far[distance - 1].astype(F32)
        self.own[k.far, k.near] = total.astype(BF)
        self.seq_copy().start()

    def result(self):
        k = self.links
        self.seq_copy().wait_recv()
        return self.own[k.far, k.near].astype(F32) + self.from_seq[...].astype(F32)

    def finish(self):
        self.near_copy().wait_send()
        for distance in range(1, self.links.depth):
            self.far_copy(distance).wait_send()
        self.seq_copy().wait_send()


def back_kernel(depth, pairs, early, chunk, *refs):
    k_ref, kt_ref, v_ref, qt_ref, q_ref, gt_ref, g_ref, aug_ref, lse_ref, delta_ref, w_ref, xt_ref, one_ref, sums_ref = refs[:14]
    n_src = 1 + max(source for source, _, _ in early)
    sources = refs[14 : 14 + n_src]
    refs = refs[14 + n_src :]
    share_qkv = refs[0]
    shares = refs[1 : 1 + n_src]
    sums_out, tokens_out = refs[1 + n_src : 3 + n_src]
    refs = refs[3 + n_src :]
    stage = [refs[5 * e : 5 * e + 5] for e in range(len(early))]
    refs = refs[5 * len(early) :]
    p_full, p_core, p_near, p_far, p_seq, acc, dq_sum, tok_send, tok_recv, dqkv = refs[:10]
    s_own, s_core, s_near, s_far, s_seq, send_sem, recv_sem, local_sem = refs[10:]

    step = pl.program_id(0)
    last = 2 * pairs - 1
    g = step % pairs
    rows = k_ref.shape[0]
    queries = qt_ref.shape[1]
    width = pairs * 128
    links = Links(depth, send_sem, recv_sem)
    span = depth + 2
    pieces = [Piece(links, e * span, *stage[e]) for e in range(len(early))]
    pair_base = len(early) * span
    sums_base = pair_base + pairs * span

    def pair_piece(index):
        own = p_full.at[index, :, :, links.core]
        return Piece(links, pair_base + index * span, own, p_core.at[index], p_near.at[index], p_far.at[index], p_seq.at[index])

    def pair_core_copy(index):
        return links.copy(p_full.at[index, :, :, 1 - links.core], p_core.at[index], pair_base + index * span, links.to_core())

    def early_core_copy(e):
        source, start, wide = early[e]
        part = sources[source].at[:, :, 1 - links.core, :, pl.ds(start, wide)]
        return links.copy(part, stage[e][1], e * span, links.to_core())

    def early_load(e):
        source, start, wide = early[e]
        part = sources[source].at[:, :, links.core, :, pl.ds(start, wide)]
        return pltpu.make_async_copy(part, stage[e][0], local_sem.at[e])

    one_copy = pltpu.make_async_copy(one_ref, acc, local_sem.at[len(early)])
    tokens_copy = links.copy(tok_send, tok_recv, sums_base + span, links.to_seq())

    def early_begin(e):
        early_core_copy(e).start()
        early_load(e).start()

    def early_near(e):
        early_load(e).wait()
        early_core_copy(e).wait_recv()
        pieces[e].send_near()

    def early_far(e):
        pieces[e].send_far()

    def early_seq(e):
        pieces[e].send_seq()

    def early_done(e):
        source, start, wide = early[e]
        shares[source][:, start : start + wide] = pieces[e].result()

    def pair_near(index):
        pair_core_copy(index).wait_recv()
        pair_piece(index).send_near()

    def pair_done(index):
        value = pair_piece(index).result()
        for third in range(3):
            at = pl.multiple_of((third * pairs + index) * 128, 128)
            share_qkv[:, pl.ds(at, 128)] = value[:, third * 128 : third * 128 + 128]

    @pl.when(step == 0)
    def _():
        links.barrier()
        early_begin(0)
        early_begin(1)
        one_copy.start()
        s_own[0] = sums_ref[...]

    def at(when, *actions):
        @pl.when(step == when)
        def _():
            for action, e in actions:
                action(e)

    lane = lax.broadcasted_iota(jnp.int32, (1, 128), 1)
    row = lax.broadcasted_iota(jnp.int32, (16, queries), 0)
    none = jnp.zeros((HD, queries), BF)
    rest = jnp.zeros((112, queries), BF)
    query_cols, grad_cols, query_rows, grad_rows = [], [], [], []
    for h in range(2):

        def placed(ref):
            half = ref[HD * h : HD * h + HD, :]
            return [half, none] if h == 0 else [none, half]

        tail = three_terms(row, lse_ref[h : h + 1, :] * (1.0 / SCALE)) + jnp.where(row == 0, 1.0, 0.0)
        query_cols.append(jnp.concatenate(placed(qt_ref) + [tail.astype(BF), rest], axis=0))
        tail = three_terms(row, delta_ref[h : h + 1, :])
        grad_cols.append(jnp.concatenate(placed(gt_ref) + [tail.astype(BF), rest], axis=0))
        mine = jnp.where((lane >= HD * h) & (lane < HD * h + HD), 1.0, 0.0).astype(BF)
        query_rows.append(q_ref[...] * mine)
        grad_rows.append(g_ref[...] * mine)
    query_rows = jnp.concatenate(query_rows, axis=0)
    grad_rows = jnp.concatenate(grad_rows, axis=0)
    nothing = jnp.zeros((HD, chunk), BF)
    dq = jnp.zeros((128, queries), F32)
    dv_total = jnp.zeros((1, 128), F32)

    def column(third):
        return pl.ds(pl.multiple_of((third * pairs + g) * 128, 128), 128)

    chunks = rows // chunk
    for c in range(chunks):
        part = slice(c * chunk, (c + 1) * chunk)
        aug = aug_ref[part, :]
        key = jnp.concatenate([k_ref[part, :], aug], axis=1)
        value = jnp.concatenate([v_ref[part, :], aug], axis=1)
        weights, grads = [], []
        for h in range(2):
            weight = jnp.exp2(dot_nn(key, query_cols[h]) * EXP2_SCALE)
            grads.append((weight * dot_nn(value, grad_cols[h])).astype(BF))
            weights.append(weight.astype(BF))
        upper = jnp.concatenate([kt_ref[0:HD, part], nothing], axis=1)
        lower = jnp.concatenate([nothing, kt_ref[HD : 2 * HD, part]], axis=1)
        dq = dq + dot_nn(jnp.concatenate([upper, lower], axis=0), jnp.concatenate(grads, axis=0))
        dv = dot_nn(jnp.concatenate(weights, axis=1), grad_rows)
        dk = dot_nn(jnp.concatenate(grads, axis=1), query_rows)
        dqkv[part, column(1)] = (dk * SCALE).astype(BF)
        dqkv[part, column(2)] = dv.astype(BF)
        dv_total = dv_total + total_rows(dv)
        if c == chunks // 2 - 1:
            at(0, (early_near, 0))
            at(3, (early_near, 2))
            at(5, (early_near, 3))
            at(6, (early_far, 2), (early_seq, 0))
            at(7, (early_near, 4))
            at(8, (early_far, 3))
            at(9, (early_far, 4), (early_seq, 1))

            @pl.when(step >= pairs + 1)
            def _():
                pair_near(step - pairs - 1)

            @pl.when(step >= pairs + 4)
            def _():
                pair_piece(2 * (step - pairs) - 7).send_far()

    @pl.when(step < pairs)
    def _():
        dq_sum[g] = dq
        pair = jnp.concatenate([dqkv[:, column(1)], dqkv[:, column(2)]], axis=1)
        half = dot_nn(xt_ref[...], pair)
        p_full[g, :, :, :, :, 128:384] = half.astype(BF).reshape(p_full.shape[1:5] + (256,))
        s_own[0, 1:2, column(0)] = dv_total

    @pl.when(step == pairs - 1)
    def _():
        tok_send[...] = dot_nt(dqkv[:, width:], w_ref[:, width:]).astype(BF)
        tokens_copy.start()

    @pl.when(step >= pairs)
    def _():
        turned = ((dq_sum[g] + dq) * SCALE).T
        low = turned.astype(BF)
        dqkv[:, column(0)] = low
        s_own[0, 0:1, column(0)] = total_rows(turned)
        s_own[0, 1:2, column(0)] += dv_total
        product = dot_nn(xt_ref[...], jnp.concatenate([low, dqkv[:, column(1)], dqkv[:, column(2)]], axis=1))
        shape = p_full.shape[1:5]
        before = p_full[g, :, :, :, :, 128:384].astype(F32)
        p_full[g, :, :, :, :, 0:128] = product[:, 0:128].astype(BF).reshape(shape + (128,))
        p_full[g, :, :, :, :, 128:384] = (product[:, 128:384].reshape(shape + (256,)) + before).astype(BF)
        pair_core_copy(g).start()

    at(0, (early_near, 1), (early_begin, 2), (early_begin, 3), (early_begin, 4))
    at(2, (early_far, 0))
    at(4, (early_far, 1))
    at(10, (early_seq, 2))

    @pl.when((step >= pairs + 3) & (step < last))
    def _():
        pair_piece(2 * (step - pairs) - 6).send_far()

    @pl.when(step == last)
    def _():
        final = pairs - 1
        hops = [(s_core, 0, links.to_core()), (s_near, 1, links.to_near())]
        hops += [(s_far.at[k - 1], 2 + k, links.to_far(k)) for k in range(1, depth)]
        hops += [(s_seq, 2, links.to_seq())]
        level = [0, 1] + [2] * (depth - 1) + [3]
        sums = [links.copy(s_own.at[n], dst, sums_base + index, peer) for n, (dst, index, peer) in zip(level, hops)]
        sums[0].start()
        out_copies = []

        def tokens(n):
            part = pl.ds(n * (rows // 4), rows // 4)
            acc[part, :] += dot_nt(dqkv[part, :], w_ref[...]) + tok_recv[part, :].astype(F32)
            out_copies.append(pltpu.make_async_copy(acc.at[part], tokens_out.at[part], local_sem.at[len(early) + 1 + n]))
            out_copies[-1].start()

        pair_piece(final - 1).send_far()
        early_seq(3)
        tokens_copy.wait_recv()
        one_copy.wait()
        tokens(0)
        pair_near(final)
        sums[0].wait_recv()
        s_own[1] = s_own[0] + s_core[...]
        sums[1].start()
        early_seq(4)
        tokens(1)
        pair_piece(0).send_seq()
        pair_piece(1).send_seq()
        tokens(2)
        pair_piece(2).send_seq()
        pair_piece(final).send_far()
        sums[1].wait_recv()
        s_own[2] = s_own[1] + s_near[...]
        for n in range(2, depth + 1):
            sums[n].start()
        tokens(3)
        for e in range(4):
            early_done(e)
        pair_piece(3).send_seq()
        pair_piece(4).send_seq()
        pair_piece(final).send_seq()
        total = s_own[2]
        for n in range(2, depth + 1):
            sums[n].wait_recv()
            total = total + s_far[n - 2]
        s_own[3] = total
        sums[depth + 1].start()
        early_done(4)
        for index in range(pairs):
            pair_done(index)
        sums[depth + 1].wait_recv()
        sums_out[...] = s_own[3] + s_seq[...]
        for n in range(4):
            out_copies[n].wait()
        for item in sums:
            item.wait_send()
        tokens_copy.wait_send()
        for e in range(len(early)):
            early_core_copy(e).wait_send()
            pieces[e].finish()
        for index in range(pairs):
            pair_core_copy(index).wait_send()
            pair_piece(index).finish()


EARLY = ((0, 0, 2), (0, 1, 2), (1, 0, 2), (1, 1, 2), (2, 0, 1))


def back_reduce(k, kt, v, qt, q, gt, g, aug, lse, delta, full_qkv, xt, grad_one, sums, sources, depth):
    keys, width = k.shape
    rows = keys // 2
    pairs = width // 128
    chunk = min(512, rows // 2)
    share = width // (4 * depth)
    views = [s.reshape(depth, 2, 2, s.shape[0] // (4 * depth), s.shape[1]) for s in sources]
    early = [(n, part * (views[n].shape[-1] // of), views[n].shape[-1] // of) for n, part, of in EARLY]
    key_rows = pl.BlockSpec((rows, 128), lambda i: (1 - i // pairs, i % pairs))
    query_cols = pl.BlockSpec((128, rows), lambda i: (i % pairs, 0))
    query_rows = pl.BlockSpec((rows, 128), lambda i: (0, i % pairs))
    stats = pl.BlockSpec((None, 2, rows), lambda i: (i % pairs, 0, 0))
    whole = pl.BlockSpec(memory_space=pltpu.VMEM)
    there = pl.BlockSpec(memory_space=pl.ANY)
    stages = []
    for n, _, wide in early:
        high = views[n].shape[3]
        stages += [
            pltpu.VMEM((depth, 2, high, wide), BF),
            pltpu.VMEM((depth, 2, high, wide), BF),
            pltpu.VMEM((depth, high, wide), BF),
            pltpu.VMEM((depth - 1, high, wide), BF),
            pltpu.VMEM((high, wide), BF),
        ]
    copies = (len(early) + pairs + 1) * (depth + 2) + 1
    return pl.pallas_call(
        functools.partial(back_kernel, depth, pairs, early, chunk),
        grid=(2 * pairs,),
        in_specs=[
            key_rows,
            pl.BlockSpec((128, rows), lambda i: (i % pairs, 1 - i // pairs)),
            key_rows,
            query_cols,
            query_rows,
            query_cols,
            query_rows,
            pl.BlockSpec((rows, 128), lambda i: (1 - i // pairs, 0)),
            stats,
            stats,
            whole,
            pl.BlockSpec((width, rows), lambda i: (0, 1 - i // pairs)),
            there,
            whole,
        ]
        + [there] * len(views),
        out_specs=[whole] * (2 + len(views)) + [there],
        out_shape=[jax.ShapeDtypeStruct((share, 3 * width), F32)]
        + [jax.ShapeDtypeStruct(s.shape[3:], F32) for s in views]
        + [jax.ShapeDtypeStruct(sums.shape, F32), jax.ShapeDtypeStruct((rows, width), F32)],
        scratch_shapes=stages
        + [
            pltpu.VMEM((pairs, depth, 2, 2, share, 384), BF),
            pltpu.VMEM((pairs, depth, 2, share, 384), BF),
            pltpu.VMEM((pairs, depth, share, 384), BF),
            pltpu.VMEM((pairs, depth - 1, share, 384), BF),
            pltpu.VMEM((pairs, share, 384), BF),
            pltpu.VMEM((rows, width), F32),
            pltpu.VMEM((pairs, 128, rows), F32),
            pltpu.VMEM((rows, width), BF),
            pltpu.VMEM((rows, width), BF),
            pltpu.VMEM((rows, 3 * width), BF),
            pltpu.VMEM((4,) + sums.shape, F32),
            pltpu.VMEM(sums.shape, F32),
            pltpu.VMEM(sums.shape, F32),
            pltpu.VMEM((depth - 1,) + sums.shape, F32),
            pltpu.VMEM(sums.shape, F32),
            pltpu.SemaphoreType.DMA((copies,)),
            pltpu.SemaphoreType.DMA((copies,)),
            pltpu.SemaphoreType.DMA((len(early) + 5,)),
        ],
        compiler_params=pltpu.CompilerParams(vmem_limit_bytes=61 << 20, collective_id=1, has_side_effects=True),
        cost_estimate=pl.CostEstimate(
            flops=40 * rows * keys * width, transcendentals=rows * keys * 2 * pairs, bytes_accessed=2 * width * 20 * rows
        ),
        name="back_reduce",
    )(k, kt, v, qt, q, gt, g, aug, lse, delta, full_qkv, xt, grad_one, sums, *views)


class Spread:
    def __init__(self, links, base, share, full, local):
        self.links, self.share, self.full = links, share, full
        self.send_base = base * (4 * links.depth + 2)
        self.recv_base = base * (4 * links.depth + 2)
        k = links
        self.local = pltpu.make_async_copy(share, full.at[k.far, k.near, k.core], local)

    def index(self, far, near, core):
        return self.recv_base + (far * 2 + near) * 2 + core

    def copy(self, src, slot, send, peer):
        return self.links.copy_two(src, self.full.at[slot], self.send_base + send, self.index(*slot), peer)

    def source(self, k):
        return self.links.ring[k]

    def far_copy(self, k):
        links = self.links
        return self.copy(self.share, (links.far, links.near, links.core), k - 1, links.peer(far=links.ring[k]))

    def near_copy(self, k):
        links = self.links
        slot = (self.source(k), links.near, links.core)
        return self.copy(self.share if k == 0 else self.full.at[slot], slot, links.depth - 1 + k, links.to_near())

    def core_copy(self, k, across):
        links = self.links
        slot = (self.source(k), 1 - links.near if across else links.near, links.core)
        src = self.share if k == 0 and not across else self.full.at[slot]
        return self.copy(src, slot, 2 * links.depth - 1 + 2 * k + across, links.to_core())

    def arrive(self, far, near, core):
        self.copy(self.share, (far, near, core), 0, self.links.to_core()).wait_recv()

    def begin(self):
        self.local.start()
        for k in range(1, self.links.depth):
            self.far_copy(k).start()
        self.near_copy(0).start()
        self.core_copy(0, 0).start()

    def pass_far(self):
        links = self.links
        for k in range(1, links.depth):
            self.arrive(self.source(k), links.near, links.core)
            self.near_copy(k).start()
            self.core_copy(k, 0).start()

    def pass_near(self):
        links = self.links
        for k in range(links.depth):
            self.arrive(self.source(k), 1 - links.near, links.core)
            self.core_copy(k, 1).start()

    def complete(self):
        links = self.links
        for k in range(links.depth):
            for near in range(2):
                self.arrive(self.source(k), near, 1 - links.core)
        self.local.wait()

    def finish(self):
        for k in range(self.links.depth):
            if k:
                self.far_copy(k).wait_send()
            self.near_copy(k).wait_send()
            self.core_copy(k, 0).wait_send()
            self.core_copy(k, 1).wait_send()


class SpreadHalf(Spread):
    def __init__(self, links, base, share, full, local):
        high = share.shape[0] // 2
        mine, others = pl.ds(links.seq * high, high), pl.ds((1 - links.seq) * high, high)
        super().__init__(links, base, share.at[mine], full.at[:, :, :, mine], local)
        self.mine = full.at[:, :, links.core, mine]
        self.others = full.at[:, :, links.core, others]
        self.across = full.at[:, :, 1 - links.core, others]

    def seq_copy(self):
        n = self.recv_base + 4 * self.links.depth
        return self.links.copy_two(self.mine, self.mine, n, n, self.links.to_seq())

    def seq_arrive(self):
        n = self.recv_base + 4 * self.links.depth
        self.links.copy_two(self.others, self.others, n, n, self.links.to_seq()).wait_recv()

    def other_copy(self):
        n = self.recv_base + 4 * self.links.depth + 1
        return self.links.copy_two(self.others, self.others, n, n, self.links.to_core())

    def pass_near(self):
        super().pass_near()
        self.local.wait()
        self.seq_copy().start()

    def pass_seq(self):
        self.seq_arrive()
        self.other_copy().start()

    def complete(self):
        links = self.links
        for k in range(links.depth):
            for near in range(2):
                self.arrive(self.source(k), near, 1 - links.core)
        n = self.recv_base + 4 * links.depth + 1
        links.copy_two(self.across, self.across, n, n, links.to_core()).wait_recv()

    def finish(self):
        super().finish()
        self.seq_copy().wait_send()
        self.other_copy().wait_send()


ROWS = (0, 2, 3, 7, 8, 9, 10, 11)


def forward_kernel(depth, pairs, later, chunk, *refs):
    x_ref, aug_ref, qkv_share = refs[:3]
    vec_refs = refs[3 : 3 + len(ROWS)]
    refs = refs[3 + len(ROWS) :]
    n_src = 1 + max(piece[0] for piece in later)
    shares = refs[:n_src]
    refs = refs[n_src:]
    q_ref, qt_ref, k_ref, kt_ref, v_ref, o_ref, lse_ref, xt_ref, sums_ref, qkv_out = refs[:10]
    fulls = refs[10 : 10 + n_src]
    w_own, w_all, v_all, v_own, other, vt, bias, qt_all, held, stats, send_sem, recv_sem, local_sem = refs[10 + n_src :]
    step = pl.program_id(0)
    g = step % pairs
    rows, width = x_ref.shape
    links = Links(depth, send_sem, recv_sem)
    groups = [Spread(links, n, w_own.at[n], w_all.at[n], local_sem.at[n]) for n in range(GROUPS)]
    vectors = Spread(links, GROUPS, v_own, v_all, local_sem.at[GROUPS])
    base = GROUPS + 1
    pieces = []
    for n, (source, start, wide, halved) in enumerate(later):
        part = pl.ds(start, wide)
        kind = SpreadHalf if halved else Spread
        pieces.append(kind(links, base + n, shares[source].at[:, part], fulls[source].at[:, :, :, :, part], local_sem.at[base + n]))
    spare = (base + len(later)) * (4 * depth + 2)
    tokens_copy = links.copy_two(x_ref, other, spare, spare, links.to_seq())
    span = width // GROUPS
    in_copies, out_copies = [], []
    for n in range(GROUPS):
        for third in range(3):
            mine, theirs = pl.ds(third * span, span), pl.ds(third * width + n * span, span)
            index = base + len(later) + 3 * n + third
            in_copies.append(pltpu.make_async_copy(qkv_share.at[:, theirs], w_own.at[n, :, mine], local_sem.at[index]))
            out_copies.append(
                pltpu.make_async_copy(w_all.at[n, :, :, :, :, mine], qkv_out.at[:, :, :, :, theirs], local_sem.at[index])
            )

    @pl.when(step == 0)
    def _():
        for copy in in_copies:
            copy.start()
        v_own[...] = jnp.zeros_like(v_own)
        for n, ref in enumerate(vec_refs):
            v_own[n : n + 1, 0 : ref.shape[1]] = ref[...]
        links.barrier()
        for copy in in_copies[:3]:
            copy.wait()
        groups[0].begin()
        tokens_copy.start()
        vectors.begin()
        for copy in in_copies[3:]:
            copy.wait()
        for n in range(1, GROUPS):
            groups[n].begin()
        xt_ref[:, 0:rows] = x_ref[...].T
        groups[0].pass_far()
        vectors.pass_far()
        groups[0].pass_near()
        vectors.pass_near()
        groups[1].pass_far()
        vectors.complete()
        target = lax.broadcasted_iota(jnp.int32, (16, width), 0)
        total = jnp.zeros((16, width), F32)
        blank = jnp.zeros((8, width - v_own.shape[1]), F32)
        for place in range(4 * depth):
            values = v_all[place // 4, place // 2 % 2, place % 2].astype(F32)
            values = jnp.concatenate([values, blank], axis=1)
            fitted = {}
            for size in VECTOR_UNITS:
                shift = place % (4 * depth // size) * (width * size // (4 * depth))
                fitted[size] = pltpu.roll(values, shift, 1) if shift else values
            for n, (first, size) in enumerate(zip(ROWS, VECTOR_SIZES)):
                row = first + place // (4 * depth // size)
                total = total + jnp.where(target == row, fitted[size][n : n + 1, :], 0.0)
        sums_ref[...] = total
        for n in range(pairs):
            bias[n, 0:2, :] = total[0:2, n * 128 : n * 128 + 128]
        groups[0].complete()

    def at(when, *actions):
        @pl.when(step == when)
        def _():
            for action in actions:
                action()

    group, place = g * GROUPS // pairs, g % (pairs // GROUPS)

    def weight(third):
        column = pl.ds(pl.multiple_of(third * span + place * 128, 128), 128)
        return w_all[group, :, :, :, :, column].reshape(width, 128)

    def project(tokens):
        kv = dot_nn(tokens[...], jnp.concatenate([weight(1), weight(2)], axis=1))
        k = kv[:, 0:128]
        v = kv[:, 128:256] + bias[g, 1:2, :]
        k_ref[...] = k.astype(BF)
        kt_ref[...] = k.T.astype(BF)
        v_ref[...] = v.astype(BF)
        vt[...] = v.T.astype(BF)

    here = pl.ds(pl.multiple_of(g * 128, 128), 128)

    @pl.when(step < pairs)
    def _():
        q = dot_nn(x_ref[...], weight(0)) + bias[g, 0:1, :]
        q_ref[...] = q.astype(BF)
        turned = q.T.astype(BF)
        qt_ref[...] = turned
        qt_all[here, :] = turned
        project(x_ref)
        held[g] = jnp.zeros(held.shape[1:], F32)
        stats[g, 0:2, :] = jnp.full((2, rows), -jnp.inf, F32)
        stats[g, 2:4, :] = jnp.zeros((2, rows), F32)

    @pl.when(step >= pairs)
    def _():
        @pl.when(step == pairs)
        def _():
            tokens_copy.wait_recv()
            xt_ref[:, rows : 2 * rows] = other[...].T

        project(other)

    row = lax.broadcasted_iota(jnp.int32, (16, rows), 0)
    tail = jnp.where(row == 0, 1.0, 0.0).astype(BF)
    none = jnp.zeros((HD, rows), BF)
    rest = jnp.zeros((112, rows), BF)
    qt = qt_all[here, :]
    queries = [
        jnp.concatenate([qt[0:HD, :], none, tail, rest], axis=0),
        jnp.concatenate([none, qt[HD : 2 * HD, :], tail, rest], axis=0),
    ]
    largest = [stats[g, h : h + 1, :] for h in range(2)]
    total = [stats[g, 2 + h : 3 + h, :] for h in range(2)]
    context = [held[g, HD * h : HD * h + HD, :] for h in range(2)]

    def score(c, h):
        part = slice(c * chunk, (c + 1) * chunk)
        return dot_nn(jnp.concatenate([k_ref[part, :], aug_ref[part, :]], axis=1), queries[h])

    ahead = [score(0, h) for h in range(2)]
    chunks = rows // chunk
    for c in range(chunks):
        part = slice(c * chunk, (c + 1) * chunk)
        for h in range(2):
            scores = ahead[h]
            if c + 1 < chunks:
                ahead[h] = score(c + 1, h)
            top = jnp.maximum(largest[h], jnp.max(scores, axis=0, keepdims=True))
            fade = jnp.exp2((largest[h] - top) * EXP2_SCALE)
            weights = jnp.exp2((scores - top) * EXP2_SCALE)
            largest[h] = top
            total[h] = total[h] * fade + total_rows(weights)
            context[h] = context[h] * fade + dot_nn(vt[HD * h : HD * h + HD, part], weights.astype(BF))

    @pl.when(step < pairs)
    def _():
        for h in range(2):
            stats[g, h : h + 1, :] = largest[h]
            stats[g, 2 + h : 3 + h, :] = total[h]
            held[g, HD * h : HD * h + HD, :] = context[h]

    @pl.when(step >= pairs)
    def _():
        for h in range(2):
            o_ref[HD * h : HD * h + HD, :] = (context[h] / total[h]).astype(BF)
            lse_ref[h : h + 1, :] = largest[h] * SCALE + jnp.log(total[h])

    at(0, groups[2].pass_far, *[piece.begin for piece in pieces])
    at(1, groups[1].pass_near, groups[1].complete)
    at(3, groups[2].pass_near, groups[2].complete, pieces[0].pass_far)
    at(4, pieces[1].pass_far, *[copy.start for copy in out_copies])
    at(5, pieces[2].pass_far)
    at(6, pieces[0].pass_near)
    at(7, pieces[1].pass_near, pieces[3].pass_far)
    at(8, pieces[2].pass_near)
    at(9, pieces[4].pass_far)
    at(10, pieces[3].pass_near, pieces[5].pass_far)

    @pl.when(step == 2 * pairs - 1)
    def _():
        pieces[4].pass_near()
        pieces[5].pass_near()
        for piece in pieces:
            if isinstance(piece, SpreadHalf):
                piece.pass_seq()
        for piece in pieces:
            piece.complete()
        for piece in groups + [vectors] + pieces:
            piece.finish()
        tokens_copy.wait_send()
        for copy in out_copies:
            copy.wait()


GROUPS = 3
VECTOR_SIZES = (2, 1, 4, 1, 1, 1, 1, 1)
VECTOR_UNITS = (1, 2, 4)
LATER = ((2, 0, 2, 1), (2, 1, 2, 1), (0, 0, 1, 0), (1, 0, 3, 0), (1, 1, 3, 0), (1, 2, 3, 0))


def forward(x, aug, vectors, w_qkv, w_out, w_up, w_down, depth):
    rows, width = x.shape
    pairs = width // 128
    keys = 2 * rows
    chunk = min(512, rows)
    shares = (w_out, w_up, w_down)
    later = [(n, part * (shares[n].shape[1] // of), shares[n].shape[1] // of, halved) for n, part, of, halved in LATER]
    whole = pl.BlockSpec(memory_space=pltpu.VMEM)
    there = pl.BlockSpec(memory_space=pl.ANY)
    half_rows = pl.BlockSpec((rows, 128), lambda i: (i // pairs, i % pairs))
    fulls = [(depth, 2, 2) + s.shape for s in (w_qkv,) + shares]
    low = lambda *shape: jax.ShapeDtypeStruct(shape, BF)
    copies = (1 + GROUPS + len(later)) * (4 * depth + 2) + 1
    return pl.pallas_call(
        functools.partial(forward_kernel, depth, pairs, later, chunk),
        grid=(2 * pairs,),
        in_specs=[whole, pl.BlockSpec((rows, 128), lambda i: (i // pairs, 0)), there] + [whole] * len(vectors) + [there] * 3,
        out_specs=[
            pl.BlockSpec((rows, 128), lambda i: (0, jnp.minimum(i, pairs - 1))),
            pl.BlockSpec((128, rows), lambda i: (jnp.minimum(i, pairs - 1), 0)),
            half_rows,
            pl.BlockSpec((128, rows), lambda i: (i % pairs, i // pairs)),
            half_rows,
            pl.BlockSpec((128, rows), lambda i: (jnp.maximum(i - pairs, 0), 0)),
            pl.BlockSpec((None, 2, rows), lambda i: (jnp.maximum(i - pairs, 0), 0, 0)),
            whole,
            whole,
            there,
            there,
            there,
            there,
        ],
        out_shape=[
            low(rows, width),
            low(width, rows),
            low(keys, width),
            low(width, keys),
            low(keys, width),
            low(width, rows),
            jax.ShapeDtypeStruct((pairs, 2, rows), F32),
            low(width, keys),
            jax.ShapeDtypeStruct((16, width), F32),
        ]
        + [low(*f) for f in fulls],
        scratch_shapes=[
            pltpu.VMEM((GROUPS, w_qkv.shape[0], 3 * width // GROUPS), BF),
            pltpu.VMEM((GROUPS, depth, 2, 2, w_qkv.shape[0], 3 * width // GROUPS), BF),
            pltpu.VMEM((depth, 2, 2, 8, 256), BF),
            pltpu.VMEM((8, 256), BF),
            pltpu.VMEM((rows, width), BF),
            pltpu.VMEM((128, rows), BF),
            pltpu.VMEM((pairs, 8, 128), F32),
            pltpu.VMEM((width, rows), BF),
            pltpu.VMEM((pairs, 128, rows), F32),
            pltpu.VMEM((pairs, 8, rows), F32),
            pltpu.SemaphoreType.DMA((copies,)),
            pltpu.SemaphoreType.DMA((copies,)),
            pltpu.SemaphoreType.DMA((1 + 4 * GROUPS + len(later),)),
        ],
        compiler_params=pltpu.CompilerParams(vmem_limit_bytes=58 << 20, collective_id=2, has_side_effects=True),
        cost_estimate=pl.CostEstimate(
            flops=16 * rows * keys * width, transcendentals=rows * keys * 2 * pairs, bytes_accessed=2 * width * 10 * keys
        ),
        name="forward",
    )(x, aug, w_qkv, *[v.reshape(1, -1) for v in vectors], *shares)


def back_plain(k, kt, v, qt, q, grad_context, aug, lse, delta, full_qkv, both, grad_one, grads, sources, sizes):
    width = k.shape[1]
    rows = q.shape[0]

    def scatter(value):
        return lax.psum_scatter(value.astype(BF), "dp", scatter_dimension=0, tiled=True)

    def over_seq(value):
        value = value.astype(BF)
        return value.astype(F32) + lax.ppermute(value, "seq", [(0, 1), (1, 0)]).astype(F32)

    share_wout, share_wup, share_wdown = [scatter(s) for s in sources]
    dqt, dk, dv = attend_back(k, kt, v, qt, q, grad_context.T, grad_context, aug, lse, delta)
    dq = dqt.T
    partial = dot_nt(jnp.concatenate([dk[rows:], dv[rows:]], axis=1), full_qkv[:, width:])
    partial = lax.ppermute(partial.astype(BF), "seq", [(0, 1), (1, 0)])
    own = jnp.concatenate([dq, dk[:rows], dv[:rows]], axis=1)
    grad_wq, grad_wk, grad_wv = dot_tn(both[:rows], dq), dot_tn(both, dk), dot_tn(both, dv)
    grad_inputs = grad_one + dot_nt(own, full_qkv) + partial.astype(F32)
    grads = (jnp.concatenate([column_sum(dq), column_sum(dv)]),) + tuple(grads)
    extra = sum(g.shape[0] for g in grads) // width
    packed = jnp.concatenate([g.reshape(-1, size) for g, size in zip(grads, sizes)], axis=1).reshape(width, extra)
    packed = jnp.pad(packed, ((0, 0), (0, 128 - extra)))
    share_qkv = over_seq(scatter(jnp.concatenate([grad_wq, grad_wk, grad_wv, packed], axis=1)))
    packed = share_qkv[:, 3 * width : 3 * width + extra].reshape(-1)
    out_vectors, start = [], 0
    for size in sizes:
        out_vectors.append(packed[start : start + size])
        start += size
    return share_qkv[:, : 3 * width], over_seq(share_wout), over_seq(share_wup), over_seq(share_wdown), out_vectors, grad_inputs


def normalize(values):
    center = jnp.mean(values, axis=-1, keepdims=True)
    shifted = values - center
    spread = jnp.mean(shifted * shifted, axis=-1, keepdims=True)
    scale = lax.rsqrt(spread + EPS)
    return shifted * scale, scale


def normalize_back(grad, normal, scale):
    mean = jnp.mean(grad, axis=-1, keepdims=True)
    along = jnp.mean(grad * normal, axis=-1, keepdims=True)
    return (grad - mean - normal * along) * scale


def middle_kernel(*refs):
    x_ref, ot_ref, vec_ref, cot_hbm, wout_hbm, wup_hbm, wdown_hbm = refs[:7]
    result_hbm, one_hbm, g_hbm, gt_hbm, delta_ref, sums_ref, gdown_hbm, gup_hbm, gout_hbm = refs[7:16]
    wout, wup, wdown, cot_buf, acts, pres, hiddens, branches, projs, normals, grads, result, turned_buf, stage, sem = refs[16:]
    rows, width = x_ref.shape
    ff = wup.shape[1]
    wide = ff // FF_PARTS
    copies = [
        pltpu.make_async_copy(src, dst, sem.at[n])
        for n, (src, dst) in enumerate(((wout_hbm, wout), (wup_hbm, wup), (wdown_hbm, wdown), (cot_hbm, cot_buf)))
    ]
    for copy in copies:
        copy.start()

    def vector(n):
        return vec_ref[n : n + 1, :]

    ot = ot_ref[...]
    context = ot.T
    copies[0].wait()
    attn = dot_nn(context, wout[...]) + vector(2)
    normal_one, scale_one = normalize(x_ref[...].astype(F32) + attn)
    normals[...] = normal_one
    low = (normal_one * vector(8) + vector(9)).astype(BF)
    hiddens[...] = low
    copies[1].wait()
    copies[2].wait()
    grads[...] = normals[...] * vector(8) + (vector(9) + vector(7))
    for c in range(FF_PARTS):
        part = slice(c * wide, (c + 1) * wide)
        row, start = divmod(c * wide, width)
        pre = dot_nn(hiddens[...], wup[:, part]) + vec_ref[3 + row : 4 + row, start : start + wide]
        bell = 0.5 * (1.0 + lax.erf(pre * 0.7071067811865476))
        act = (pre * bell).astype(BF)
        pres[:, part] = (bell + pre * (jnp.exp(-0.5 * pre * pre) * 0.3989422804014327)).astype(BF)
        acts[:, part] = act
        grads[...] += dot_nn(act, wdown[part, :])
    normal_two, scale_two = normalize(grads[...])
    result[...] = (normal_two * vector(10) + vector(11)).astype(BF)
    out_result = pltpu.make_async_copy(result, result_hbm, sem.at[4])
    out_result.start()
    copies[3].wait()
    cot = cot_buf[...].astype(F32)
    sums_ref[...] = jnp.zeros_like(sums_ref)
    sums_ref[10:11, :] = total_rows(cot * normal_two)
    sums_ref[11:12, :] = total_rows(cot)
    grad_two = normalize_back(cot * vector(10), normal_two, scale_two)
    grads[...] = grad_two
    branch = grad_two.astype(BF)
    branches[...] = branch
    sums_ref[7:8, :] = total_rows(branch.astype(F32))
    for c in range(FF_PARTS):
        part = slice(c * wide, (c + 1) * wide)
        row, start = divmod(c * wide, width)
        grad_pre = (dot_nt(branches[...], wdown[part, :]) * pres[:, part].astype(F32)).astype(BF)
        pres[:, part] = grad_pre
        sums_ref[3 + row : 4 + row, start : start + wide] = total_rows(grad_pre.astype(F32))
        grads[...] += dot_nt(grad_pre, wup[:, part])
    grad_hidden = grads[...]
    normal_one = normals[...]
    sums_ref[8:9, :] = total_rows(grad_hidden * normal_one)
    sums_ref[9:10, :] = total_rows(grad_hidden)
    grad_one = normalize_back(grad_hidden * vector(8), normal_one, scale_one)
    grads[...] = grad_one
    out_one = pltpu.make_async_copy(grads, one_hbm, sem.at[5])
    out_one.start()
    proj = grad_one.astype(BF)
    projs[...] = proj
    sums_ref[2:3, :] = total_rows(proj.astype(F32))
    grad_context = dot_nt(projs[...], wout[...])
    out_result.wait()
    result[...] = grad_context.astype(BF)
    out_g = pltpu.make_async_copy(result, g_hbm, sem.at[4])
    out_g.start()
    turned = grad_context.T.astype(BF)
    turned_buf[...] = turned
    out_gt = pltpu.make_async_copy(turned_buf, gt_hbm, sem.at[6])
    out_gt.start()
    each = (turned.astype(F32) * ot.astype(F32)).reshape(width // HD, HD, rows)
    delta_ref[...] = jnp.sum(each, axis=1).reshape(delta_ref.shape)

    outs = []

    def put(value, target):
        n = len(outs)
        if n >= 2:
            outs[n - 2].wait()
        stage[n % 2] = value.astype(BF)
        outs.append(pltpu.make_async_copy(stage.at[n % 2], target, sem.at[7 + n % 2]))
        outs[n].start()

    for c in range(ff // width):
        part = slice(c * width, (c + 1) * width)
        put(dot_nn(acts[:, part].T, branches[...]), gdown_hbm.at[pl.ds(c * width, width)])
    turned = hiddens[...].T
    for c in range(ff // width):
        part = slice(c * width, (c + 1) * width)
        put(dot_nn(turned, pres[:, part]), gup_hbm.at[:, pl.ds(c * width, width)])
    put(dot_nn(ot_ref[...], projs[...]), gout_hbm)
    for copy in outs[-2:] + [out_one, out_g, out_gt]:
        copy.wait()


FF_PARTS = 4


def middle(x, cotangent, context_t, vectors, w_out, w_up, w_down):
    rows, width = x.shape
    ff = w_up.shape[1]
    pairs = width // 128
    whole = pl.BlockSpec(memory_space=pltpu.VMEM)
    there = pl.BlockSpec(memory_space=pl.ANY)
    shape = jax.ShapeDtypeStruct
    return pl.pallas_call(
        middle_kernel,
        in_specs=[whole, whole, whole, there, there, there, there],
        out_specs=[there, there, there, there, whole, whole, there, there, there],
        out_shape=[
            shape((rows, width), BF),
            shape((rows, width), F32),
            shape((rows, width), BF),
            shape((width, rows), BF),
            shape((pairs, 2, rows), F32),
            shape((16, width), F32),
            shape((ff, width), BF),
            shape((width, ff), BF),
            shape((width, width), BF),
        ],
        scratch_shapes=[
            pltpu.VMEM((width, width), BF),
            pltpu.VMEM((width, ff), BF),
            pltpu.VMEM((ff, width), BF),
            pltpu.VMEM((rows, width), BF),
            pltpu.VMEM((rows, ff), BF),
            pltpu.VMEM((rows, ff), BF),
            pltpu.VMEM((rows, width), BF),
            pltpu.VMEM((rows, width), BF),
            pltpu.VMEM((rows, width), BF),
            pltpu.VMEM((rows, width), F32),
            pltpu.VMEM((rows, width), F32),
            pltpu.VMEM((rows, width), BF),
            pltpu.VMEM((width, rows), BF),
            pltpu.VMEM((2, width, width), BF),
            pltpu.SemaphoreType.DMA((9,)),
        ],
        compiler_params=pltpu.CompilerParams(vmem_limit_bytes=58 << 20),
        cost_estimate=pl.CostEstimate(
            flops=6 * rows * width * (width + 2 * ff), transcendentals=2 * rows * ff, bytes_accessed=8 * width * (width + 2 * ff)
        ),
        name="middle",
    )(x, context_t, vectors, cotangent, w_out, w_up, w_down)


def finish_kernel(parts, *refs):
    count = (len(refs) - 2 - len(ROWS)) // 3
    sums_ref, sources = refs[0], refs[1 : 1 + count]
    targets, small = refs[1 + count : 1 + 2 * count], refs[1 + 2 * count : 1 + 2 * count + len(ROWS)]
    held, sem = refs[-1 - count : -1], refs[-1]
    rows = sources[0].shape[0] // 4
    cuts = [(0, pl.ds(n * rows, rows)) for n in range(4)] + [(n, slice(None)) for n in range(1, count)]
    loads, stores = [], []
    for index, (n, part) in enumerate(cuts):
        loads.append(pltpu.make_async_copy(sources[n].at[part], held[n].at[part], sem.at[index]))
        stores.append(pltpu.make_async_copy(held[n].at[part], targets[n].at[part], sem.at[len(cuts) + index]))
    for copy in loads:
        copy.start()
    width = sums_ref.shape[1]
    place = lax.axis_index("dp")
    picked = []
    for base, size in zip(ROWS, VECTOR_SIZES):
        picked.append(sums_ref[pl.ds(base + place // (parts // size), 1), :])
    picked = jnp.concatenate(picked, axis=0)
    for size in VECTOR_UNITS:
        shift = (place % (parts // size)) * (width * size // parts)
        turned = pltpu.roll(picked, (width - shift) % width, 1)
        for n in range(len(ROWS)):
            if VECTOR_SIZES[n] == size:
                small[n][...] = turned[n : n + 1, 0 : small[n].shape[1]]
    for load, store in zip(loads, stores):
        load.wait()
        store.start()
    for store in stores:
        store.wait()


def finish(sums, tokens, shares, parts):
    whole = pl.BlockSpec(memory_space=pltpu.VMEM)
    there = pl.BlockSpec(memory_space=pl.ANY)
    width = sums.shape[1]
    large = (tokens,) + shares
    small = [jax.ShapeDtypeStruct((1, width * size // parts), F32) for size in VECTOR_SIZES]
    out = pl.pallas_call(
        functools.partial(finish_kernel, parts),
        in_specs=[whole] + [there] * len(large),
        out_specs=[there] * len(large) + [whole] * len(small),
        out_shape=[jax.ShapeDtypeStruct(x.shape, x.dtype) for x in large] + small,
        scratch_shapes=[pltpu.VMEM(x.shape, x.dtype) for x in large] + [pltpu.SemaphoreType.DMA((2 * (len(shares) + 4),))],
        compiler_params=pltpu.CompilerParams(vmem_limit_bytes=58 << 20),
        name="finish",
    )(sums, *large)
    return out[: len(large)], [v.reshape(-1) for v in out[len(large) :]]


def forward_plain(x, aug, vectors, w_qkv):
    width = x.shape[1]
    other = lax.ppermute(x, "seq", [(0, 1), (1, 0)])
    sizes = [v.shape[0] for v in vectors]
    share = w_qkv.shape[0]
    extra = sum(sizes) // share
    beside = jnp.concatenate(vectors).reshape(share, extra)
    beside = jnp.concatenate([w_qkv, jnp.pad(beside, ((0, 0), (0, 128 - extra)))], axis=1)
    full_qkv = lax.all_gather(beside, "dp", axis=0, tiled=True)
    full_vectors = full_qkv[:, 3 * width : 3 * width + extra].reshape(-1, sum(sizes)).astype(F32)
    full_qkv = full_qkv[:, : 3 * width]
    full, start = [], 0
    for size in sizes:
        full.append(full_vectors[:, start : start + size].reshape(-1))
        start += size
    both = jnp.concatenate([x, other], axis=0)
    q = (dot_nn(x, full_qkv[:, :width]) + full[0][:width]).astype(BF)
    k = dot_nn(both, full_qkv[:, width : 2 * width]).astype(BF)
    v = (dot_nn(both, full_qkv[:, 2 * width :]) + full[0][width:]).astype(BF)
    qt, kt, vt = q.T, k.T, v.T
    context_t, lse = attend(k, qt, vt, aug)
    return q, qt, k, kt, v, both, context_t, lse, full_qkv, full[1:]


def plain(x, aug, vectors, w_qkv, w_out, w_up, w_down, upstream):
    rows, width = x.shape
    sizes = [v.shape[0] for v in vectors]
    q, qt, k, kt, v, both, context_t, lse, full_qkv, full = forward_plain(x, aug, vectors, w_qkv)
    full_bout, full_bup, full_bdown, gain_one, shift_one, gain_two, shift_two = full
    full_wout, full_wup, full_wdown = [lax.all_gather(w, "dp", axis=0, tiled=True) for w in (w_out, w_up, w_down)]
    context = context_t.T
    attn_branch = dot_nn(context, full_wout) + full_bout
    resid_one = x.astype(F32) + attn_branch
    hidden_one, first_pull = jax.vjp(layer_norm, resid_one, gain_one, shift_one)
    hidden_low = hidden_one.astype(BF)
    pre_act = dot_nn(hidden_low, full_wup) + full_bup
    activated, gelu_pull = jax.vjp(gelu_exact, pre_act)
    act_low = activated.astype(BF)
    ffn_branch = dot_nn(act_low, full_wdown) + full_bdown
    resid_two = hidden_one + ffn_branch
    output, second_pull = jax.vjp(layer_norm, resid_two, gain_two, shift_two)
    grad_two, grad_gain_two, grad_shift_two = second_pull(upstream.astype(F32))
    grad_branch = grad_two.astype(BF)
    grad_wdown = dot_tn(act_low, grad_branch)
    grad_bdown = column_sum(grad_branch)
    (grad_pre,) = gelu_pull(dot_nt(grad_branch, full_wdown))
    grad_pre_low = grad_pre.astype(BF)
    grad_wup = dot_tn(hidden_low, grad_pre_low)
    grad_bup = column_sum(grad_pre_low)
    grad_hidden = grad_two + dot_nt(grad_pre_low, full_wup)
    grad_one, grad_gain_one, grad_shift_one = first_pull(grad_hidden)
    grad_proj = grad_one.astype(BF)
    grad_wout = dot_tn(context, grad_proj)
    grad_bout = column_sum(grad_proj)
    grad_context = dot_nt(grad_proj, full_wout).astype(BF)
    delta = jnp.sum((grad_context.astype(F32) * context.astype(F32)).reshape(rows, HEADS, HD), axis=-1)
    delta = delta.T.reshape(HEADS // 2, 2, rows)

    grads = (grad_bout, grad_bup, grad_bdown, grad_gain_one, grad_shift_one, grad_gain_two, grad_shift_two)
    share_qkv, share_out, share_up, share_down, out_vectors, grad_inputs = back_plain(
        k, kt, v, qt, q, grad_context, aug, lse, delta, full_qkv, both, grad_one, grads, (grad_wout, grad_wup, grad_wdown), sizes
    )
    return output.astype(BF), grad_inputs, share_qkv, share_out, share_up, share_down, out_vectors


def local(
    tokens,
    lengths,
    w_qkv,
    bias_qv,
    w_out,
    bias_out,
    w_up,
    bias_up,
    w_down,
    bias_down,
    gain_attn,
    shift_attn,
    gain_ffn,
    shift_ffn,
    cotangent,
):
    x = tokens[0]
    rows, width = x.shape
    ff = w_up.shape[1]
    me = lax.axis_index("seq")
    parts = lax.axis_size("dp")
    aligned = parts % 4 == 0 and width % (16 * parts) == 0 and ff % (16 * parts) == 0
    vectors = (bias_qv, bias_out, bias_up, bias_down, gain_attn, shift_attn, gain_ffn, shift_ffn)
    sizes = [v.shape[0] for v in vectors]
    aligned = aligned and tuple(s * parts for s in sizes) == tuple(n * width for n in VECTOR_SIZES) and parts == 16

    slot = jnp.arange(2 * rows)
    slot = jnp.where(slot < rows, me * rows + slot, (1 - me) * rows + slot - rows)
    lane = jnp.arange(128)
    masked = jnp.where(slot < lengths[0], 0.0, MASK)
    aug = jnp.where(lane[None] == 0, masked[:, None], jnp.where(lane[None] < 4, -1.0, 0.0)).astype(BF)

    if aligned:
        q, qt, k, kt, v, context_t, lse, xt, summed, full_qkv, full_wout, full_wup, full_wdown = forward(
            x, aug, vectors, w_qkv, w_out, w_up, w_down, parts // 4
        )
        full_qkv = full_qkv.reshape(width, 3 * width)
        output, grad_one, grad_context, grad_context_t, delta, sums, grad_wdown, grad_wup, grad_wout = middle(
            x, cotangent[0], context_t, summed, full_wout.reshape(width, width), full_wup.reshape(width, ff), full_wdown.reshape(ff, width)
        )
        sources = (grad_wdown, grad_wup, grad_wout)
        share_qkv, share_down, share_up, share_out, sums, grad_inputs = back_reduce(
            k, kt, v, qt, q, grad_context_t, grad_context, aug, lse, delta, full_qkv, xt, grad_one, sums, sources, parts // 4
        )
        large, out_vectors = finish(sums, grad_inputs, (share_qkv, share_out, share_up, share_down), parts)
        grad_inputs, share_qkv, share_out, share_up, share_down = large
    else:
        output, grad_inputs, share_qkv, share_out, share_up, share_down, out_vectors = plain(
            x, aug, vectors, w_qkv, w_out, w_up, w_down, cotangent[0]
        )
    s_bqv, s_bout, s_bup, s_bdown, s_gain_one, s_shift_one, s_gain_two, s_shift_two = out_vectors
    return (
        output[None],
        grad_inputs[None],
        share_qkv,
        s_bqv,
        share_out,
        s_bout,
        share_up,
        s_bup,
        share_down,
        s_bdown,
        s_gain_one,
        s_shift_one,
        s_gain_two,
        s_shift_two,
    )


def solution(mesh):
    act, mat, vec = P("dp", "seq", None), P("dp", None), P("dp")
    in_specs = (act, vec, mat, vec, mat, vec, mat, vec, mat, vec, vec, vec, vec, vec, act)
    out_specs = (act, act, mat, vec, mat, vec, mat, vec, mat, vec, vec, vec, vec, vec)
    return jax.shard_map(local, mesh=mesh, in_specs=in_specs, out_specs=out_specs, check_vma=False)
```
